256 devices in a mesh: member: 16 (over z_lo, x), grid: 16 (over z_hi, y, core).
Axes of the slice: x: 4, y: 4, z: 8 (z_hi: 2, z_lo: 4; z = z_hi * 4 + z_lo), core: 2. Of those that a mesh axis runs over, the one named last changes fastest.
Arguments:
- slabs: bfloat16 [16, 4096, 256], P('member', 'grid'), may hold values from -6 to 6
- loader: int32 [1], replicated, may hold values from 0 to 15
- hidden_jitter: bfloat16 [16, 2048, 16], P('member', 'grid'), may hold values from -3 to 3
- w_noise: bfloat16 [16, 1024], replicated, may hold values from -1.5 to 1.5
- w_enc: bfloat16 [128, 1024], replicated, may hold values from -0.10986328 to 0.10986328
- enc_offset: int32 [2048, 8], P('grid'), may hold values from -128 to 128
- enc_weight: float32 [2048, 8], P('grid'), may hold values from -1 to 1
- w_qkv: bfloat16 [1024, 1536], replicated, may hold values from -0.1875 to 0.1875
- window_offset: int32 [2048], P('grid'), may hold values from -64 to 0
- w_out: bfloat16 [512, 1024], replicated, may hold values from -0.25 to 0.25
- unpacker_linear_map: bfloat16 [1024, 128], replicated, may hold values from -0.1875 to 0.1875
- dec_offset: int32 [4096, 3], P('grid'), may hold values from -64 to 64
- unpacker_arc_scales: float32 [4096, 3], P('grid'), may hold values from 0.2 to 1
Outputs:
- grad_noise: float32 [16, 1024], P(None, ('member', 'grid'))
- grad_enc: float32 [128, 1024], P(None, ('member', 'grid'))
- grad_qkv: float32 [1024, 1536], P(('member', 'grid'))
- grad_out: float32 [512, 1024], P(None, ('member', 'grid'))
- unpacker_map_sensitivity: float32 [1024, 128], P(('member', 'grid'))
The draws below stay inside these ranges and needn't reach their ends.
All inputs are finite; a program needn't handle non-finite values.
Results may differ from the reference program's by a relative error of at most 0.0075.
Values may be sent and summed in bfloat16 or wider, within the bound.
No kernel may reach another device: no remote copies, remote signals or barrier semaphores. Data moves between devices by JAX's collectives and lax.ppermute only.
A program may use at most 128 MiB of HBM per device.

```python
import jax
import jax.numpy as jnp
from jax import lax

D = 1024
HEADS = 8
HEAD_DIM = 64
C = 128
NOISE = 16
K_ENC = 8
K_DEC = 3
RIM_G = 128
RIM_H = 64
WIN = 64
H_DEV = 128
G_DEV = 256
MEMBERS = 16
HID = 2048
NPTS = 4096


def place_ends(entries, rng, smallest, largest):
    place = [jax.random.randint(jax.random.fold_in(rng, axis), (), 0, length) for axis, length in enumerate(entries.shape)]
    widest = entries.shape.index(max(entries.shape))
    beside = place[:widest] + [(place[widest] + 1) % entries.shape[widest]] + place[widest + 1:]
    return entries.at[tuple(place)].set(smallest).at[tuple(beside)].set(largest)


def levels(own_key, extent, split, smallest, largest):
    level = 1.0
    for position, shards_of in split:
        heights = jax.random.uniform(jax.random.fold_in(jax.random.fold_in(own_key, 6), position), (shards_of,), jnp.float32, smallest / len(split), largest / len(split))
        level = level * jnp.repeat(jnp.exp(heights), extent[position] // shards_of).reshape((-1,) + (1,) * (len(extent) - 1 - position))
    return level


def gaussian(key, shape, spread, bound, cuts=(), kind=jnp.bfloat16):
    entries = jax.random.normal(key, shape, jnp.float32) * spread
    if len(cuts) > 0:
        entries = levels(key, shape, cuts, -0.22, 0.18) * entries
    return jnp.clip(entries, min=-bound, max=bound).astype(kind)


def setup_inputs(seed: int = 0) -> dict:
    key_list = jax.random.split(jax.random.key(seed), 14)
    slabs = jnp.clip(jax.random.uniform(key_list[0], (MEMBERS, NPTS, 2 * C), jnp.float32, -6.0, 6.0) * levels(key_list[0], (MEMBERS, NPTS, 2 * C), ((0, 16), (1, 16)), -0.4, 0.0), -6.0, 6.0).astype(jnp.bfloat16)
    loader = jax.random.randint(key_list[1], (1,), 0, MEMBERS).astype(jnp.int32)
    hidden_jitter = gaussian(key_list[2], (MEMBERS, HID, NOISE), 0.5, 3.0, ((0, 16), (1, 16)))
    w_noise = gaussian(key_list[3], (NOISE, D), NOISE ** -0.5, 1.5)
    w_enc = jnp.clip(jax.random.uniform(key_list[4], (C, D), jnp.float32, -0.10986328, 0.10986328), -0.10986328, 0.10986328).astype(jnp.bfloat16)
    enc_offset = place_ends(jax.random.randint(key_list[5], (HID, K_ENC), 0 - RIM_G, RIM_G + 1), jax.random.fold_in(key_list[5], 1), 0 - RIM_G, RIM_G).astype(jnp.int32)
    enc_weight = jnp.clip(jax.random.uniform(key_list[6], (HID, K_ENC), jnp.float32, -1.0, 1.0) * levels(key_list[6], (HID, K_ENC), ((0, 16),), -0.4, 0.0), -1.0, 1.0)
    w_qkv = gaussian(key_list[7], (D, 3 * HEADS * HEAD_DIM), D ** -0.5, 0.1875)
    window_offset = place_ends(jax.random.randint(key_list[8], (HID,), 0 - WIN, 1), jax.random.fold_in(key_list[8], 1), 0 - WIN, 0).astype(jnp.int32)
    w_out = gaussian(key_list[9], (HEADS * HEAD_DIM, D), (HEADS * HEAD_DIM) ** -0.5, 0.25)
    unpacker_linear_map = gaussian(key_list[10], (D, C), D ** -0.5, 0.1875)
    dec_offset = place_ends(jax.random.randint(key_list[11], (NPTS, K_DEC), 0 - RIM_H, RIM_H + 1), jax.random.fold_in(key_list[11], 1), 0 - RIM_H, RIM_H).astype(jnp.int32)
    unpacker_arc_scales = jnp.clip(0.2 + 0.8 * jax.random.uniform(key_list[12], (NPTS, K_DEC), jnp.float32) ** levels(key_list[12], (NPTS, K_DEC), ((0, 16),), -0.2, 0.2), 0.2, 1.0)
    return {"slabs": slabs, "loader": loader, "hidden_jitter": hidden_jitter, "w_noise": w_noise, "w_enc": w_enc, "enc_offset": enc_offset, "enc_weight": enc_weight, "w_qkv": w_qkv, "window_offset": window_offset, "w_out": w_out, "unpacker_linear_map": unpacker_linear_map, "dec_offset": dec_offset, "unpacker_arc_scales": unpacker_arc_scales}


EPS = 1e-06
DELTA_SQ = 0.01

def rms_factor(values):
    return lax.rsqrt(lax.optimization_barrier(jnp.mean(values * values, axis=-1, keepdims=True)) + EPS)

def rms_back(values, factor, gradient):
    inner = lax.optimization_barrier(jnp.mean(gradient * values, axis=-1, keepdims=True))
    return factor * gradient - values * (factor * factor * factor) * inner

def silu_slope(pre):
    sigma = jax.nn.sigmoid(pre)
    return sigma * (1.0 + pre * (1.0 - sigma))

def eased_sensitivity(diff):
    return diff * lax.rsqrt(diff * diff + DELTA_SQ)

def widen(values):
    return lax.optimization_barrier(values).astype(jnp.float32)

def exact_dot(left, right):
    return jnp.dot(left, right, precision=lax.Precision.HIGHEST)

def window_attention(query_norm, key_norm, value_rows, attender_tags):
    blocks = HID // H_DEV
    inv_root = HEAD_DIM ** (-0.5)

    def one_block(compacted_amounts):
        query_block, ids = compacted_amounts
        key_window = widen(key_norm[ids])
        value_window = widen(value_rows[ids])
        scores = jnp.einsum('rhd,rwhd->rhw', widen(query_block), key_window) * inv_root
        weights_exp = jnp.exp(scores)
        prob_rows = (weights_exp / lax.optimization_barrier(jnp.sum(weights_exp, axis=-1, keepdims=True))).astype(jnp.bfloat16)
        out_rows = jnp.einsum('rhw,rwhd->rhd', widen(prob_rows), value_window).astype(jnp.bfloat16)
        return (out_rows, prob_rows)
    out_rows, prob_rows = lax.map(one_block, (query_norm.reshape(blocks, H_DEV, HEADS, HEAD_DIM), attender_tags.reshape(blocks, H_DEV, WIN)))
    return (out_rows.reshape(HID, HEADS * HEAD_DIM), prob_rows)

def window_back(query_norm, key_norm, value_rows, attender_tags, prob_rows, grad_attended):
    blocks = HID // H_DEV
    inv_root = HEAD_DIM ** (-0.5)

    def one_block(carry, compacted_amounts):
        grad_keys, grad_values = carry
        query_block, ids, prob_block, grad_block = compacted_amounts
        key_window = widen(key_norm[ids])
        value_window = widen(value_rows[ids])
        prob32 = widen(prob_block)
        grad32 = widen(grad_block)
        grad_probs = jnp.einsum('rhd,rwhd->rhw', grad32, value_window)
        grad_scores = widen((prob32 * (grad_probs - lax.optimization_barrier(jnp.sum(prob32 * grad_probs, axis=-1, keepdims=True)))).astype(jnp.bfloat16))
        grad_query = jnp.einsum('rhw,rwhd->rhd', grad_scores, key_window) * inv_root
        grad_keys = grad_keys.at[ids].add(jnp.einsum('rhw,rhd->rwhd', grad_scores, widen(query_block)) * inv_root)
        grad_values = grad_values.at[ids].add(jnp.einsum('rhw,rhd->rwhd', prob32, grad32))
        return ((grad_keys, grad_values), grad_query)
    empty = jnp.zeros((HID, HEADS, HEAD_DIM), jnp.float32)
    packs = (query_norm.reshape(blocks, H_DEV, HEADS, HEAD_DIM), attender_tags.reshape(blocks, H_DEV, WIN), prob_rows, grad_attended.reshape(blocks, H_DEV, HEADS, HEAD_DIM))
    (grad_keys, grad_values), grad_query = lax.scan(one_block, (empty, empty), packs)
    return (grad_query.reshape(HID, HEADS, HEAD_DIM), grad_keys, grad_values)

def realization_evaluate_run(averaged_cells, jitter_cell_amounts, scales_array, attender_tags, unpacker_start_cell, unpacker_arc_scales, unadorned_state):
    w_noise, w_qkv, w_out, unpacker_linear_map = scales_array
    factor0 = rms_factor(averaged_cells)
    state0 = averaged_cells * factor0 + jnp.dot(jitter_cell_amounts, w_noise, preferred_element_type=jnp.float32)
    factor1 = rms_factor(state0)
    normed = (state0 * factor1).astype(jnp.bfloat16)
    mixed_rows = jnp.dot(normed, w_qkv, preferred_element_type=jnp.float32).reshape(HID, 3, HEADS, HEAD_DIM)
    queries = mixed_rows[:, 0]
    key_raw = mixed_rows[:, 1]
    query_factor = rms_factor(queries)
    key_factor = rms_factor(key_raw)
    query_norm = (queries * query_factor).astype(jnp.bfloat16)
    key_norm = (key_raw * key_factor).astype(jnp.bfloat16)
    value_rows = mixed_rows[:, 2].astype(jnp.bfloat16)
    attended, prob_rows = window_attention(query_norm, key_norm, value_rows, attender_tags)
    state1 = state0 + jnp.dot(attended, w_out, preferred_element_type=jnp.float32)
    factor2 = rms_factor(state1)
    dnorm = (state1 * factor2).astype(jnp.bfloat16)
    projected = jnp.dot(dnorm, unpacker_linear_map, preferred_element_type=jnp.float32)
    restored_cells = jnp.zeros((NPTS, C), jnp.float32)
    for arc_location in range(K_DEC):
        restored_cells = restored_cells + unpacker_arc_scales[:, arc_location:arc_location + 1] * projected[unpacker_start_cell[:, arc_location]]
    prognosis_cells = unadorned_state.astype(jnp.float32) + restored_cells
    kept_amounts = (factor0, state0, factor1, normed, queries, key_raw, query_factor, key_factor, query_norm, key_norm, value_rows, attended, prob_rows, state1, factor2, dnorm)
    return (prognosis_cells, kept_amounts)

def realization_adjoint_run(averaged_cells, jitter_cell_amounts, scales_array, kept_amounts, prognosis_sensitivity, attender_tags, unpacker_start_cell, unpacker_arc_scales):
    w_noise, w_qkv, w_out, unpacker_linear_map = scales_array
    factor0, state0, factor1, normed, queries, key_raw, query_factor, key_factor, query_norm, key_norm, value_rows, attended, prob_rows, state1, factor2, dnorm = kept_amounts
    mapped_sensitivity_result = jnp.zeros((HID, C), jnp.float32)
    for arc_location in range(K_DEC):
        mapped_sensitivity_result = mapped_sensitivity_result.at[unpacker_start_cell[:, arc_location]].add(unpacker_arc_scales[:, arc_location:arc_location + 1] * prognosis_sensitivity)
    unpacker_map_sensitivity = exact_dot(widen(dnorm).T, mapped_sensitivity_result)
    grad_dnorm = exact_dot(mapped_sensitivity_result, unpacker_linear_map.astype(jnp.float32).T)
    grad_state1 = rms_back(state1, factor2, grad_dnorm)
    grad_state1_b = grad_state1.astype(jnp.bfloat16)
    grad_out = jnp.dot(attended.T, grad_state1_b, preferred_element_type=jnp.float32)
    grad_attended = jnp.dot(grad_state1_b, w_out.T, preferred_element_type=jnp.float32).astype(jnp.bfloat16)
    grad_qnorm, grad_knorm, grad_values = window_back(query_norm, key_norm, value_rows, attender_tags, prob_rows, grad_attended)
    grad_queries = rms_back(queries, query_factor, grad_qnorm)
    grad_keys = rms_back(key_raw, key_factor, grad_knorm)
    grad_mixed = jnp.stack([grad_queries, grad_keys, grad_values], axis=1).reshape(HID, 3 * HEADS * HEAD_DIM).astype(jnp.bfloat16)
    grad_qkv = jnp.dot(normed.T, grad_mixed, preferred_element_type=jnp.float32)
    grad_normed = jnp.dot(grad_mixed, w_qkv.T, preferred_element_type=jnp.float32)
    grad_state0 = grad_state1 + rms_back(state0, factor1, grad_normed)
    grad_noise = jnp.dot(jitter_cell_amounts.T, grad_state0.astype(jnp.bfloat16), preferred_element_type=jnp.float32)
    grad_pooled = rms_back(averaged_cells, factor0, grad_state0)
    return (grad_noise, grad_pooled, grad_qkv, grad_out, unpacker_map_sensitivity)

def prognosis_sensitivity_array(prognosis_array, verifying_cell_amounts):
    verifying_state_f32 = verifying_cell_amounts.astype(jnp.float32)
    loss_scale = float(MEMBERS * NPTS * C) ** (-0.5)
    verifying_sensitivity = eased_sensitivity(prognosis_array - verifying_state_f32[None])

    def duo_spread_move(summed_score, partner_realization):
        return (summed_score + eased_sensitivity(prognosis_array - partner_realization[None]), None)
    duo_spread_sum, ignored_result = lax.scan(duo_spread_move, jnp.zeros_like(prognosis_array), prognosis_array)
    return (verifying_sensitivity / MEMBERS - duo_spread_sum / (MEMBERS * (MEMBERS - 1))) * loss_scale

def reference(slabs, loader, hidden_jitter, w_noise, w_enc, enc_offset, enc_weight, w_qkv, window_offset, w_out, unpacker_linear_map, dec_offset, unpacker_arc_scales):
    analysis = lax.dynamic_index_in_dim(slabs, loader[0], 0, keepdims=False)
    unadorned_state = analysis[:, :C]
    verifying_cell_amounts = analysis[:, C:]
    pre_enc = jnp.dot(unadorned_state, w_enc, preferred_element_type=jnp.float32)
    messages = jax.nn.silu(pre_enc).astype(jnp.bfloat16)
    home_rows = jnp.arange(HID, dtype=jnp.int32) * G_DEV // H_DEV
    enc_source = ((home_rows[:, None] + enc_offset) % NPTS).astype(jnp.int32)
    averaged_cells = jnp.zeros((HID, D), jnp.float32)
    for arc_location in range(K_ENC):
        averaged_cells = averaged_cells + enc_weight[:, arc_location:arc_location + 1] * widen(messages[enc_source[:, arc_location]])
    node_ids = jnp.arange(HID, dtype=jnp.int32)
    attender_tags = ((node_ids[:, None] + window_offset[:, None] + jnp.arange(WIN, dtype=jnp.int32)[None, :]) % HID).astype(jnp.int32)
    home_nodes = jnp.arange(NPTS, dtype=jnp.int32) * H_DEV // G_DEV
    unpacker_start_cell = ((home_nodes[:, None] + dec_offset) % HID).astype(jnp.int32)
    scales_array = (w_noise, w_qkv, w_out, unpacker_linear_map)

    def compute_prognosis(jitter_cell_amounts):
        return realization_evaluate_run(averaged_cells, jitter_cell_amounts, scales_array, attender_tags, unpacker_start_cell, unpacker_arc_scales, unadorned_state)[0]
    prognosis_array = lax.map(compute_prognosis, hidden_jitter)
    sensitivity_array = prognosis_sensitivity_array(prognosis_array, verifying_cell_amounts)

    def accumulate(totals, compacted_amounts):
        jitter_cell_amounts, prognosis_sensitivity = compacted_amounts
        prognosis_cells, kept_amounts = realization_evaluate_run(averaged_cells, jitter_cell_amounts, scales_array, attender_tags, unpacker_start_cell, unpacker_arc_scales, unadorned_state)
        shard_array = realization_adjoint_run(averaged_cells, jitter_cell_amounts, scales_array, kept_amounts, prognosis_sensitivity, attender_tags, unpacker_start_cell, unpacker_arc_scales)
        return (tuple((summed_score + part for summed_score, part in zip(totals, shard_array))), None)
    init = (jnp.zeros((NOISE, D), jnp.float32), jnp.zeros((HID, D), jnp.float32), jnp.zeros((D, 3 * HEADS * HEAD_DIM), jnp.float32), jnp.zeros((HEADS * HEAD_DIM, D), jnp.float32), jnp.zeros((D, C), jnp.float32))
    totals, ignored_result = lax.scan(accumulate, init, (hidden_jitter, sensitivity_array))
    grad_noise, grad_pooled, grad_qkv, grad_out, unpacker_map_sensitivity = totals
    grad_messages = jnp.zeros((NPTS, D), jnp.float32)
    for arc_location in range(K_ENC):
        grad_messages = grad_messages.at[enc_source[:, arc_location]].add(enc_weight[:, arc_location:arc_location + 1] * grad_pooled)
    grad_enc = exact_dot(unadorned_state.astype(jnp.float32).T, grad_messages * silu_slope(pre_enc))
    return (grad_noise, grad_enc, grad_qkv, grad_out, unpacker_map_sensitivity)
```

```python
import jax
import jax.numpy as jnp
from jax import lax
from jax.sharding import Mesh
from jax.sharding import PartitionSpec as P

HEAD_DIM = 64
RIM_G = 128
RIM_H = 64
WIN = 64

EPS = 1e-06
DELTA_SQ = 0.01

MEMBER = ("zl", "x")
GRID = ("zh", "y", "core")
F32 = jnp.float32
BF16 = jnp.bfloat16
HIGHEST = lax.Precision.HIGHEST


def rms_factor(values):
    return lax.rsqrt(jnp.mean(values * values, axis=-1, keepdims=True) + EPS)


def rms_back(values, factor, gradient):
    inner = jnp.mean(gradient * values, axis=-1, keepdims=True)
    return factor * gradient - values * (factor * factor * factor) * inner


def silu_slope(pre):
    sigma = jax.nn.sigmoid(pre)
    return sigma * (1.0 + pre * (1.0 - sigma))


def eased_sensitivity(diff):
    return diff * lax.rsqrt(diff * diff + DELTA_SQ)


def dot(left, right, dims, **options):
    return lax.dot_general(left, right, (dims, ((), ())), preferred_element_type=F32, **options)


NN = ((1,), (0,))
TN = ((0,), (0,))
NT = ((1,), (1,))


def two_terms(values):
    high = lax.reduce_precision(values, 8, 7)
    return high.astype(BF16), (values - high).astype(BF16)


def swap(values, axes):
    return lax.all_to_all(values, axes, split_axis=0, concat_axis=0, tiled=True)


def shifted(values, step):
    count = lax.axis_size(GRID)
    return lax.ppermute(values, GRID, [(i, (i + step) % count) for i in range(count)])


def per_device(
    slabs,
    loader,
    hidden_jitter,
    w_noise,
    w_enc,
    enc_offset,
    enc_weight,
    w_qkv,
    window_offset,
    w_out,
    unpacker_linear_map,
    dec_offset,
    unpacker_arc_scales,
):
    members = lax.axis_size(MEMBER)
    shards = lax.axis_size(GRID)
    channels, width = w_enc.shape
    attn = w_out.shape[0]
    heads = attn // HEAD_DIM
    points = slabs.shape[1]
    nodes = enc_offset.shape[0]
    per_node = points // nodes
    sub = points // members
    noise = w_noise.shape[0]
    k_enc = enc_offset.shape[1]
    k_dec = dec_offset.shape[1]
    inv_root = HEAD_DIM ** (-0.5)

    pieces = swap(slabs[0].reshape(members, sub, 2 * channels), MEMBER)
    piece = lax.dynamic_index_in_dim(pieces, loader[0], 0, keepdims=False)
    truth = piece[:, channels:].astype(F32)
    x_own = swap(jnp.broadcast_to(piece[None, :, :channels], (members, sub, channels)), MEMBER)
    x_own = x_own.reshape(points, channels)

    packed = jnp.concatenate(
        [
            enc_offset.astype(F32),
            enc_weight,
            window_offset[:, None].astype(F32),
            hidden_jitter[0].astype(F32),
            dec_offset.astype(F32).reshape(nodes, per_node * k_dec),
            unpacker_arc_scales.reshape(nodes, per_node * k_dec),
        ],
        axis=1,
    )
    packed = jnp.pad(packed, ((0, 0), (0, 128 - packed.shape[1])))
    x_own, packed = lax.optimization_barrier((x_own, packed))
    x_all = jnp.concatenate(
        [
            shifted(x_own[points - RIM_G :], 2),
            shifted(x_own, 1),
            x_own,
            shifted(x_own, -1),
            shifted(x_own[:RIM_G], -2),
        ],
        axis=0,
    )
    packed = jnp.concatenate([shifted(packed, 1), packed, shifted(packed, -1)], axis=0)
    enc_offset_all = packed[:, :k_enc].astype(jnp.int32)
    enc_weight_all = packed[:, k_enc : 2 * k_enc]
    at = 2 * k_enc
    window_all = packed[:, at : at + 1].astype(jnp.int32)
    at += 1
    jitter_all = packed[:, at : at + noise].astype(BF16)
    at += noise
    dec_offset_all = packed[:, at : at + per_node * k_dec].astype(jnp.int32)
    dec_offset_all = dec_offset_all.reshape(3 * points, k_dec)
    at += per_node * k_dec
    dec_scale_all = packed[:, at : at + per_node * k_dec].reshape(3 * points, k_dec)

    reach = points + 2 * RIM_G
    pre_enc = dot(x_all, w_enc, NN)
    messages = jax.nn.silu(pre_enc).astype(BF16)
    home = (jnp.arange(3 * nodes, dtype=jnp.int32) % nodes) * per_node
    source = home[:, None] + enc_offset_all + RIM_G
    span = lax.broadcasted_iota(jnp.int32, (3 * nodes, reach), 1)
    spread = jnp.zeros((3 * nodes, reach), F32)
    for k in range(k_enc):
        spread = spread + jnp.where(
            source[:, k : k + 1] == span, enc_weight_all[:, k : k + 1], 0.0
        )
    spread_high, spread_low = two_terms(spread)
    pooled = []
    for s in range(3):
        rows = slice(s * nodes, (s + 1) * nodes)
        near = messages[s * points : s * points + reach]
        pooled.append(dot(spread_high[rows], near, NN) + dot(spread_low[rows], near, NN))
    pooled = jnp.concatenate(pooled, axis=0)
    factor0 = rms_factor(pooled)
    state0 = pooled * factor0 + dot(jitter_all, w_noise, NN)
    factor1 = rms_factor(state0)
    normed = (state0 * factor1).astype(BF16)
    mixed = dot(normed, w_qkv, NN).reshape(3 * nodes, 3, heads, HEAD_DIM)

    own = slice(nodes, 2 * nodes)
    asked = slice(nodes - WIN, 2 * nodes + WIN)
    n_asked = nodes + 2 * WIN
    own_asked = slice(WIN, WIN + nodes)
    queries = mixed[asked, 0]
    key_raw = mixed[:, 1]
    query_factor = rms_factor(queries)
    key_factor = rms_factor(key_raw)
    query_norm = (queries * query_factor).astype(BF16)
    key_norm = (key_raw * key_factor).astype(BF16)
    value_rows = mixed[:, 2].astype(BF16)
    relative = (
        jnp.arange(3 * nodes, dtype=jnp.int32)[None, :]
        - WIN
        - jnp.arange(n_asked, dtype=jnp.int32)[:, None]
    )
    offsets = window_all[asked]
    allowed = ((relative >= offsets) & (relative < offsets + WIN)).astype(F32)
    scores = (
        jnp.einsum("qhd,khd->hqk", query_norm, key_norm, preferred_element_type=F32) * inv_root
    )
    weights_exp = jnp.exp(scores) * allowed[None]
    prob = (weights_exp / jnp.sum(weights_exp, axis=-1, keepdims=True)).astype(BF16)
    attended = jnp.einsum("hqk,khd->qhd", prob, value_rows, preferred_element_type=F32)
    attended = attended.astype(BF16).reshape(n_asked, attn)
    state1 = state0[asked] + dot(attended, w_out, NN)
    factor2 = rms_factor(state1)
    dnorm = (state1 * factor2).astype(BF16)

    projected = dot(dnorm, unpacker_linear_map, NN)
    homeh = jnp.arange(3 * points, dtype=jnp.int32) // per_node - nodes + RIM_H
    dec_source = homeh[:, None] + dec_offset_all
    dec_span = lax.broadcasted_iota(jnp.int32, (3 * points, n_asked), 1)
    arcs = jnp.zeros((3 * points, n_asked), F32)
    for k in range(k_dec):
        arcs = arcs + jnp.where(
            dec_source[:, k : k + 1] == dec_span, dec_scale_all[:, k : k + 1], 0.0
        )
    restored = dot(arcs[points : 2 * points], projected, NN, precision=HIGHEST)
    forecast = x_own.astype(F32) + restored

    cells = swap(forecast.reshape(members, sub, channels), MEMBER)
    loss_scale = float(members * points * shards * channels) ** (-0.5)
    fair = jnp.sum(eased_sensitivity(cells[:, None] - cells[None, :]), axis=1)
    sensitivity = (
        eased_sensitivity(cells - truth[None]) / members - fair / (members * (members - 1))
    ) * loss_scale
    grad_forecast = swap(sensitivity, MEMBER).reshape(points, channels)
    grad_forecast = jnp.concatenate(
        [shifted(grad_forecast, 1), grad_forecast, shifted(grad_forecast, -1)], axis=0
    )

    zl, x = (lax.axis_size(a) for a in MEMBER)
    zh, y, core = (lax.axis_size(a) for a in GRID)
    rows = width // (members * shards)
    order = jnp.arange(width, dtype=jnp.int32).reshape(core, x, y, zl, zh, rows)
    c_i, x_i, y_i, zl_i, zh_i, r_i = (
        lax.broadcasted_iota(jnp.int32, order.shape, d) for d in range(6)
    )
    target = ((((zl_i * x + x_i) * zh + zh_i) * y + y_i) * core + c_i) * rows + r_i
    target = target.reshape(1, width)
    reorder = (lax.broadcasted_iota(jnp.int32, (width, width), 0) == target).astype(BF16)

    def reordered(values):
        return dot(values, reorder, NN).astype(BF16)

    grad_projected = dot(arcs, grad_forecast, TN, precision=HIGHEST)
    gp_high, gp_low = two_terms(grad_projected)
    dnorm_r = reordered(dnorm[own_asked])
    dec_term = dot(dnorm_r, gp_high[own_asked], TN) + dot(dnorm_r, gp_low[own_asked], TN)
    grad_dnorm = dot(gp_high, unpacker_linear_map, NT) + dot(gp_low, unpacker_linear_map, NT)
    grad_state1 = rms_back(state1, factor2, grad_dnorm)
    grad_state1_b = grad_state1.astype(BF16)
    out_term = dot(reordered(grad_state1_b[own_asked]), attended[own_asked], TN)
    grad_attended = dot(grad_state1_b, w_out, NT).astype(BF16).reshape(n_asked, heads, HEAD_DIM)
    grad_probs = jnp.einsum("qhd,khd->hqk", grad_attended, value_rows, preferred_element_type=F32)
    prob_wide = prob.astype(F32)
    grad_scores = (
        prob_wide * (grad_probs - jnp.sum(prob_wide * grad_probs, axis=-1, keepdims=True))
    ).astype(BF16)
    grad_qnorm = (
        jnp.einsum(
            "hqk,khd->qhd", grad_scores[:, own_asked], key_norm, preferred_element_type=F32
        )
        * inv_root
    )
    grad_knorm = (
        jnp.einsum("hqk,qhd->khd", grad_scores[:, :, own], query_norm, preferred_element_type=F32)
        * inv_root
    )
    grad_values = jnp.einsum(
        "hqk,qhd->khd", prob[:, :, own], grad_attended, preferred_element_type=F32
    )
    grad_queries = rms_back(queries[own_asked], query_factor[own_asked], grad_qnorm)
    grad_keys = rms_back(key_raw[own], key_factor[own], grad_knorm)
    grad_mixed = (
        jnp.stack([grad_queries, grad_keys, grad_values], axis=1)
        .reshape(nodes, 3 * attn)
        .astype(BF16)
    )
    qkv_term = dot(reordered(normed[own]), grad_mixed, TN)
    grad_normed = dot(grad_mixed, w_qkv, NT)
    grad_state0 = grad_state1[own_asked] + rms_back(state0[own], factor1[own], grad_normed)
    grad_state0_r = reordered(grad_state0.astype(BF16))
    jitter_own = jnp.pad(hidden_jitter[0], ((0, 0), (0, 128 - noise)))
    noise_term = dot(grad_state0_r, jitter_own, TN)
    grad_pooled = rms_back(pooled[own], factor0[own], grad_state0)
    grad_messages = dot(spread[own], grad_pooled, TN, precision=HIGHEST)
    near = slice(points, points + reach)
    grad_pre = grad_messages * silu_slope(pre_enc[near])
    enc_term = dot(x_all[near].astype(F32), grad_pre, TN, precision=HIGHEST)
    enc_term = dot(reorder, enc_term.astype(BF16), ((0,), (1,)))

    parts = (qkv_term, out_term, enc_term, dec_term, noise_term)
    total = jnp.concatenate([part.astype(BF16) for part in parts], axis=1)
    lanes = total.shape[1]
    total = total.reshape(core, width // core, lanes)
    side = lax.axis_index("core")
    kept = lax.dynamic_index_in_dim(total, side, 0, keepdims=False)
    sent = lax.dynamic_index_in_dim(total, 1 - side, 0, keepdims=False)
    total = kept.astype(F32) + lax.ppermute(sent, "core", [(0, 1), (1, 0)]).astype(F32)
    total = swap(total.astype(BF16).reshape(x * y, -1, lanes), ("x", "y"))
    total = jnp.sum(total.astype(F32), axis=0)
    total = swap(total.astype(BF16).reshape(zl * zh, rows, lanes), ("zl", "zh"))
    total = jnp.sum(total.astype(F32), axis=0)
    cuts = []
    at = 0
    for part in parts:
        cuts.append(total[:, at : at + part.shape[1]])
        at += part.shape[1]
    grad_qkv, grad_out, grad_enc, grad_map, grad_noise = cuts
    return (grad_noise[:, :noise].T, grad_enc.T, grad_qkv, grad_out.T, grad_map)


def solution(mesh):
    member, grid = mesh.shape["member"], mesh.shape["grid"]
    inner = 4 if member == 16 else 2
    fine = Mesh(
        mesh.devices.reshape(member // inner, inner, 2, grid // 4, 2), MEMBER + GRID
    )
    in_specs = (
        P(MEMBER, GRID, None),
        P(),
        P(MEMBER, GRID, None),
        P(),
        P(),
        P(GRID, None),
        P(GRID, None),
        P(),
        P(GRID),
        P(),
        P(),
        P(GRID, None),
        P(GRID, None),
    )
    both = MEMBER + GRID
    out_specs = (P(None, both), P(None, both), P(both, None), P(None, both), P(both, None))
    return jax.shard_map(
        per_device, mesh=fine, in_specs=in_specs, out_specs=out_specs, check_vma=False
    )
```

```python
import jax
import jax.numpy as jnp
from jax import lax
from jax.sharding import Mesh
from jax.sharding import PartitionSpec as P

HEAD_DIM = 64
RIM_G = 128
RIM_H = 64
WIN = 64

EPS = 1e-06
DELTA_SQ = 0.01

MEMBER = ("zl", "x")
GRID = ("zh", "y", "core")
F32 = jnp.float32
BF16 = jnp.bfloat16
HIGHEST = lax.Precision.HIGHEST


def rms_factor(values):
    return lax.rsqrt(jnp.mean(values * values, axis=-1, keepdims=True) + EPS)


def rms_back(values, factor, gradient):
    inner = jnp.mean(gradient * values, axis=-1, keepdims=True)
    return factor * gradient - values * (factor * factor * factor) * inner


def silu_slope(pre):
    sigma = jax.nn.sigmoid(pre)
    return sigma * (1.0 + pre * (1.0 - sigma))


def eased_sensitivity(diff):
    return diff * lax.rsqrt(diff * diff + DELTA_SQ)


def dot(left, right, dims, **options):
    return lax.dot_general(left, right, (dims, ((), ())), preferred_element_type=F32, **options)


NN = ((1,), (0,))
TN = ((0,), (0,))
NT = ((1,), (1,))


def two_terms(values):
    high = lax.reduce_precision(values, 8, 7)
    return high.astype(BF16), (values - high).astype(BF16)


def three_terms(values):
    high = lax.reduce_precision(values, 8, 7)
    middle = lax.reduce_precision(values - high, 8, 7)
    return [high.astype(BF16), middle.astype(BF16), (values - high - middle).astype(BF16)]


def swap(values, axes):
    return lax.all_to_all(values, axes, split_axis=0, concat_axis=0, tiled=True)


def shifted(values, step):
    count = lax.axis_size(GRID)
    return lax.ppermute(values, GRID, [(i, (i + step) % count) for i in range(count)])


def per_device(
    slabs,
    loader,
    hidden_jitter,
    w_noise,
    w_enc,
    enc_offset,
    enc_weight,
    w_qkv,
    window_offset,
    w_out,
    unpacker_linear_map,
    dec_offset,
    unpacker_arc_scales,
):
    members = lax.axis_size(MEMBER)
    shards = lax.axis_size(GRID)
    channels, width = w_enc.shape
    attn = w_out.shape[0]
    heads = attn // HEAD_DIM
    points = slabs.shape[1]
    nodes = enc_offset.shape[0]
    per_node = points // nodes
    sub = points // members
    noise = w_noise.shape[0]
    k_enc = enc_offset.shape[1]
    k_dec = dec_offset.shape[1]
    inv_root = HEAD_DIM ** (-0.5)

    pieces = swap(slabs[0].reshape(members, sub, 2 * channels), MEMBER)
    piece = lax.dynamic_index_in_dim(pieces, loader[0], 0, keepdims=False)
    truth = piece[:, channels:].astype(F32)

    packed = jnp.concatenate(
        [enc_offset.astype(BF16)]
        + three_terms(enc_weight)
        + [window_offset[:, None].astype(BF16)]
        + [dec_offset.reshape(nodes, per_node * k_dec).astype(BF16)]
        + three_terms(unpacker_arc_scales.reshape(nodes, per_node * k_dec)),
        axis=1,
    )
    packed = jnp.pad(packed, ((0, 0), (0, channels - packed.shape[1])))
    share = nodes // members
    member = lax.axis_index(MEMBER)
    shard = lax.axis_index(GRID)
    jitter_rows = nodes * noise // channels
    chunk = jnp.concatenate(
        [
            piece[:, :channels],
            hidden_jitter[0].reshape(jitter_rows, channels),
            lax.dynamic_slice_in_dim(packed, member * share, share, 0),
        ],
        axis=0,
    )
    got = swap(jnp.broadcast_to(chunk[None], (shards,) + chunk.shape), GRID)
    far2, low, mid, high, far1 = (
        lax.dynamic_index_in_dim(got, (shard + o) % shards, 0, keepdims=False)
        for o in (-2, -1, 0, 1, 2)
    )
    at = sub + jitter_rows
    far = jnp.where(member >= members // 2, far2[:sub], far1[:sub])
    payload = jnp.concatenate(
        [low[:sub], mid[:sub], high[:sub], far, low[at:], mid[at:], high[at:]], axis=0
    )
    got = swap(jnp.broadcast_to(payload[None], (members,) + payload.shape), MEMBER)
    x_parts = [
        got[:, i * sub : (i + 1) * sub].reshape(points, channels) for i in range(3)
    ]
    x_own = x_parts[1]
    far = got[:, 3 * sub : 4 * sub]
    x_all = jnp.concatenate(
        [far[members // 2 :].reshape(-1, channels)]
        + x_parts
        + [far[: members // 2].reshape(-1, channels)],
        axis=0,
    )
    packed = got[:, 4 * sub :].reshape(members, 3, share, channels)
    packed = packed.transpose(1, 0, 2, 3).reshape(3 * nodes, channels)
    jitter_all = jnp.concatenate([low[sub:at], mid[sub:at], high[sub:at]], axis=0)
    jitter_all = jitter_all.reshape(3 * nodes, noise)
    packed = packed.astype(F32)

    def column(start, count):
        return packed[:, start : start + count]

    def summed(start, count):
        return sum(column(start + i * count, count) for i in range(1, 3)) + column(start, count)

    enc_offset_all = column(0, k_enc).astype(jnp.int32)
    enc_weight_all = summed(k_enc, k_enc)
    at = 4 * k_enc
    window_all = column(at, 1).astype(jnp.int32)
    at += 1
    each = per_node * k_dec
    dec_offset_all = column(at, each).astype(jnp.int32).reshape(3 * points, k_dec)
    dec_scale_all = summed(at + each, each).reshape(3 * points, k_dec)

    reach = points + 2 * RIM_G
    pre_enc = dot(x_all, w_enc, NN)
    messages = jax.nn.silu(pre_enc).astype(BF16)
    home = (jnp.arange(3 * nodes, dtype=jnp.int32) % nodes) * per_node
    source = home[:, None] + enc_offset_all + RIM_G
    span = lax.broadcasted_iota(jnp.int32, (3 * nodes, reach), 1)
    spread = jnp.zeros((3 * nodes, reach), F32)
    for k in range(k_enc):
        spread = spread + jnp.where(
            source[:, k : k + 1] == span, enc_weight_all[:, k : k + 1], 0.0
        )
    spread_high, spread_low = two_terms(spread)
    pooled = []
    for s in range(3):
        rows = slice(s * nodes, (s + 1) * nodes)
        near = messages[s * points : s * points + reach]
        pooled.append(dot(spread_high[rows], near, NN) + dot(spread_low[rows], near, NN))
    pooled = jnp.concatenate(pooled, axis=0)
    factor0 = rms_factor(pooled)
    state0 = pooled * factor0 + dot(jitter_all, w_noise, NN)
    factor1 = rms_factor(state0)
    normed = (state0 * factor1).astype(BF16)
    mixed = dot(normed, w_qkv, NN).reshape(3 * nodes, 3, heads, HEAD_DIM)

    own = slice(nodes, 2 * nodes)
    asked = slice(nodes - WIN, 2 * nodes + WIN)
    n_asked = nodes + 2 * WIN
    own_asked = slice(WIN, WIN + nodes)
    queries = mixed[asked, 0]
    key_raw = mixed[:, 1]
    query_factor = rms_factor(queries)
    key_factor = rms_factor(key_raw)
    query_norm = (queries * query_factor).astype(BF16)
    key_norm = (key_raw * key_factor).astype(BF16)
    value_rows = mixed[:, 2].astype(BF16)
    relative = (
        jnp.arange(3 * nodes, dtype=jnp.int32)[None, :]
        - WIN
        - jnp.arange(n_asked, dtype=jnp.int32)[:, None]
    )
    offsets = window_all[asked]
    allowed = ((relative >= offsets) & (relative < offsets + WIN)).astype(F32)
    scores = (
        jnp.einsum("qhd,khd->hqk", query_norm, key_norm, preferred_element_type=F32) * inv_root
    )
    weights_exp = jnp.exp(scores) * allowed[None]
    prob = (weights_exp / jnp.sum(weights_exp, axis=-1, keepdims=True)).astype(BF16)
    attended = jnp.einsum("hqk,khd->qhd", prob, value_rows, preferred_element_type=F32)
    attended = attended.astype(BF16).reshape(n_asked, attn)
    state1 = state0[asked] + dot(attended, w_out, NN)
    factor2 = rms_factor(state1)
    dnorm = (state1 * factor2).astype(BF16)

    projected = dot(dnorm, unpacker_linear_map, NN)
    homeh = jnp.arange(3 * points, dtype=jnp.int32) // per_node - nodes + RIM_H
    dec_source = homeh[:, None] + dec_offset_all
    dec_span = lax.broadcasted_iota(jnp.int32, (3 * points, n_asked), 1)
    arcs = jnp.zeros((3 * points, n_asked), F32)
    for k in range(k_dec):
        arcs = arcs + jnp.where(
            dec_source[:, k : k + 1] == dec_span, dec_scale_all[:, k : k + 1], 0.0
        )
    restored = dot(arcs[points : 2 * points], projected, NN, precision=HIGHEST)
    forecast = x_own.astype(F32) + restored

    cells = swap(forecast.reshape(members, sub, channels), MEMBER)
    loss_scale = float(members * points * shards * channels) ** (-0.5)
    fair = jnp.sum(eased_sensitivity(cells[:, None] - cells[None, :]), axis=1)
    sensitivity = (
        eased_sensitivity(cells - truth[None]) / members - fair / (members * (members - 1))
    ) * loss_scale
    grad_forecast = swap(sensitivity.astype(BF16), MEMBER).reshape(points, channels)
    grad_forecast = jnp.concatenate(
        [shifted(grad_forecast, 1), grad_forecast, shifted(grad_forecast, -1)], axis=0
    ).astype(F32)

    zl, x = (lax.axis_size(a) for a in MEMBER)
    zh, y, core = (lax.axis_size(a) for a in GRID)
    rows = width // (members * shards)
    order = jnp.arange(width, dtype=jnp.int32).reshape(core, x, y, zl, zh, rows)
    c_i, x_i, y_i, zl_i, zh_i, r_i = (
        lax.broadcasted_iota(jnp.int32, order.shape, d) for d in range(6)
    )
    target = ((((zl_i * x + x_i) * zh + zh_i) * y + y_i) * core + c_i) * rows + r_i
    target = target.reshape(1, width)
    reorder = (lax.broadcasted_iota(jnp.int32, (width, width), 0) == target).astype(BF16)

    def reordered(values):
        return dot(values, reorder, NN).astype(BF16)

    grad_projected = dot(arcs, grad_forecast, TN, precision=HIGHEST)
    gp_high, gp_low = two_terms(grad_projected)
    dnorm_r = reordered(dnorm[own_asked])
    dec_term = dot(dnorm_r, gp_high[own_asked], TN) + dot(dnorm_r, gp_low[own_asked], TN)
    grad_dnorm = dot(gp_high, unpacker_linear_map, NT) + dot(gp_low, unpacker_linear_map, NT)
    grad_state1 = rms_back(state1, factor2, grad_dnorm)
    grad_state1_b = grad_state1.astype(BF16)
    out_term = dot(reordered(grad_state1_b[own_asked]), attended[own_asked], TN)
    grad_attended = dot(grad_state1_b, w_out, NT).astype(BF16).reshape(n_asked, heads, HEAD_DIM)
    grad_probs = jnp.einsum("qhd,khd->hqk", grad_attended, value_rows, preferred_element_type=F32)
    prob_wide = prob.astype(F32)
    grad_scores = (
        prob_wide * (grad_probs - jnp.sum(prob_wide * grad_probs, axis=-1, keepdims=True))
    ).astype(BF16)
    grad_qnorm = (
        jnp.einsum(
            "hqk,khd->qhd", grad_scores[:, own_asked], key_norm, preferred_element_type=F32
        )
        * inv_root
    )
    grad_knorm = (
        jnp.einsum("hqk,qhd->khd", grad_scores[:, :, own], query_norm, preferred_element_type=F32)
        * inv_root
    )
    grad_values = jnp.einsum(
        "hqk,qhd->khd", prob[:, :, own], grad_attended, preferred_element_type=F32
    )
    grad_queries = rms_back(queries[own_asked], query_factor[own_asked], grad_qnorm)
    grad_keys = rms_back(key_raw[own], key_factor[own], grad_knorm)
    grad_mixed = (
        jnp.stack([grad_queries, grad_keys, grad_values], axis=1)
        .reshape(nodes, 3 * attn)
        .astype(BF16)
    )
    qkv_term = dot(reordered(normed[own]), grad_mixed, TN)
    grad_normed = dot(grad_mixed, w_qkv, NT)
    grad_state0 = grad_state1[own_asked] + rms_back(state0[own], factor1[own], grad_normed)
    grad_state0_r = reordered(grad_state0.astype(BF16))
    jitter_own = jnp.pad(hidden_jitter[0], ((0, 0), (0, 128 - noise)))
    noise_term = dot(grad_state0_r, jitter_own, TN)
    grad_pooled = rms_back(pooled[own], factor0[own], grad_state0)
    grad_messages = dot(spread[own], grad_pooled, TN, precision=HIGHEST)
    near = slice(points, points + reach)
    grad_pre = grad_messages * silu_slope(pre_enc[near])
    enc_term = dot(x_all[near].astype(F32), grad_pre, TN, precision=HIGHEST)
    enc_term = dot(reorder, enc_term.astype(BF16), ((0,), (1,)))

    parts = (qkv_term, out_term, enc_term, dec_term, noise_term)
    total = jnp.concatenate([part.astype(BF16) for part in parts], axis=1)
    lanes = total.shape[1]
    total = total.reshape(core, width // core, lanes)
    side = lax.axis_index("core")
    kept = lax.dynamic_index_in_dim(total, side, 0, keepdims=False)
    sent = lax.dynamic_index_in_dim(total, 1 - side, 0, keepdims=False)
    total = kept.astype(F32) + lax.ppermute(sent, "core", [(0, 1), (1, 0)]).astype(F32)
    total = swap(total.astype(BF16).reshape(x * y, -1, lanes), ("x", "y"))
    total = jnp.sum(total.astype(F32), axis=0)
    total = swap(total.astype(BF16).reshape(zl * zh, rows, lanes), ("zl", "zh"))
    total = jnp.sum(total.astype(F32), axis=0)
    cuts = []
    at = 0
    for part in parts:
        cuts.append(total[:, at : at + part.shape[1]])
        at += part.shape[1]
    grad_qkv, grad_out, grad_enc, grad_map, grad_noise = cuts
    return (grad_noise[:, :noise].T, grad_enc.T, grad_qkv, grad_out.T, grad_map)


def solution(mesh):
    member, grid = mesh.shape["member"], mesh.shape["grid"]
    inner = 4 if member == 16 else 2
    fine = Mesh(
        mesh.devices.reshape(member // inner, inner, 2, grid // 4, 2), MEMBER + GRID
    )
    in_specs = (
        P(MEMBER, GRID, None),
        P(),
        P(MEMBER, GRID, None),
        P(),
        P(),
        P(GRID, None),
        P(GRID, None),
        P(),
        P(GRID),
        P(),
        P(),
        P(GRID, None),
        P(GRID, None),
    )
    both = MEMBER + GRID
    out_specs = (P(None, both), P(None, both), P(both, None), P(None, both), P(both, None))
    return jax.shard_map(
        per_device, mesh=fine, in_specs=in_specs, out_specs=out_specs, check_vma=False
    )
```

```python
import functools

import jax
import jax.numpy as jnp
from jax import lax
from jax.experimental import pallas as pl
from jax.experimental.pallas import tpu as pltpu
from jax.sharding import Mesh
from jax.sharding import PartitionSpec as P

HEAD_DIM = 64
RIM_G = 128
RIM_H = 64
WIN = 64

EPS = 1e-06
DELTA_SQ = 0.01

MEMBER = ("zl", "x")
GRID = ("zh", "y", "core")
F32 = jnp.float32
BF16 = jnp.bfloat16
INTERPRET = False
NODES = 128
POINTS = 256
ASKED = NODES + 2 * WIN


def rms_factor(values):
    return lax.rsqrt(jnp.mean(values * values, axis=-1, keepdims=True) + EPS)


def rms_back(values, factor, gradient):
    inner = jnp.mean(gradient * values, axis=-1, keepdims=True)
    return factor * gradient - values * (factor * factor * factor) * inner


def silu_slope(pre):
    sigma = jax.nn.sigmoid(pre)
    return sigma * (1.0 + pre * (1.0 - sigma))


def eased_sensitivity(diff):
    return diff * lax.rsqrt(diff * diff + DELTA_SQ)


def dot(left, right, dims, **options):
    return lax.dot_general(left, right, (dims, ((), ())), preferred_element_type=F32, **options)


NN = ((1,), (0,))
TN = ((0,), (0,))
NT = ((1,), (1,))


def two_terms(values):
    high = lax.reduce_precision(values, 8, 7)
    return high.astype(BF16), (values - high).astype(BF16)


def three_terms(values):
    high = lax.reduce_precision(values, 8, 7)
    middle = lax.reduce_precision(values - high, 8, 7)
    return [high.astype(BF16), middle.astype(BF16), (values - high - middle).astype(BF16)]


def swap(values, axes):
    return lax.all_to_all(values, axes, split_axis=0, concat_axis=0, tiled=True)


def shifted(values, step):
    count = lax.axis_size(GRID)
    return lax.ppermute(values, GRID, [(i, (i + step) % count) for i in range(count)])


def split2(values):
    high = values.astype(BF16)
    return high, (values - high.astype(F32)).astype(BF16)


def same_head(attn):
    row = lax.broadcasted_iota(jnp.int32, (attn, attn), 0) // HEAD_DIM
    column = lax.broadcasted_iota(jnp.int32, (attn, attn), 1) // HEAD_DIM
    return jnp.where(row == column, 1.0, 0.0).astype(BF16)


def head_mean(values, heads):
    high, low = split2(values)
    return (dot(high, heads, NN) + dot(low, heads, NN)) * (1.0 / HEAD_DIM)


def head_masks():
    lane = lax.broadcasted_iota(jnp.int32, (1, 2 * HEAD_DIM), 1)
    return (lane < HEAD_DIM, lane >= HEAD_DIM)


def masked(mask, values):
    return jnp.where(mask, values, jnp.zeros_like(values))


def spread_matrix(facts, k_enc, reach):
    span = lax.broadcasted_iota(jnp.int32, (NODES, reach), 1)
    home = lax.broadcasted_iota(jnp.int32, (NODES, 1), 0) * (POINTS // NODES) + RIM_G
    spread = jnp.zeros((NODES, reach), F32)
    for k in range(k_enc):
        source = facts[:, k : k + 1].astype(jnp.int32) + home
        spread = spread + jnp.where(source == span, facts[:, k_enc + k : k_enc + k + 1], 0.0)
    return split2(spread)


def interleave(parity, shape, point_dim):
    point = lax.broadcasted_iota(jnp.int32, shape, point_dim)
    node = lax.broadcasted_iota(jnp.int32, shape, 1 - point_dim)
    return jnp.where(point == 2 * node + parity, 1.0, 0.0).astype(BF16)


def forward_kernel(k_enc, k_dec, *refs):
    x_ref, facts_ref, jitter_ref, wn_ref, we_ref, wq_ref, wo_ref, u_ref = refs[:8]
    (forecast_ref, pooled_ref, state0_ref, normed_ref, raw_ref, qn_ref, kn_ref, v_ref) = refs[8:16]
    prob_ref, att_ref, state1_ref, dnorm_ref, msg_ref, all0_ref, proj_ref = refs[16:]
    attn = wo_ref.shape[0]
    reach = POINTS + 2 * RIM_G
    inv_root = HEAD_DIM ** (-0.5)

    def message_rows(i, carry):
        rows = pl.ds(pl.multiple_of(i * 128, 128), 128)
        pre = dot(x_ref[rows, :], we_ref[...], NN)
        msg_ref[rows, :] = (pre * jax.nn.sigmoid(pre)).astype(BF16)
        return carry

    lax.fori_loop(0, x_ref.shape[0] // 128, message_rows, 0)
    heads = same_head(attn)
    for s in range(3):
        rows = slice(s * NODES, (s + 1) * NODES)
        high, low = spread_matrix(facts_ref[rows, :], k_enc, reach)
        near = msg_ref[s * POINTS : s * POINTS + reach, :]
        pooled = dot(high, near, NN) + dot(low, near, NN)
        state0 = pooled * rms_factor(pooled) + dot(jitter_ref[rows, :], wn_ref[...], NN)
        all0_ref[rows, :] = state0
        normed = (state0 * rms_factor(state0)).astype(BF16)
        mixed = dot(normed, wq_ref[...], NN)
        queries, keys = mixed[:, :attn], mixed[:, attn : 2 * attn]
        qn_ref[rows, :] = (
            queries * lax.rsqrt(head_mean(queries * queries, heads) + EPS)
        ).astype(BF16)
        kn_ref[rows, :] = (keys * lax.rsqrt(head_mean(keys * keys, heads) + EPS)).astype(BF16)
        v_ref[rows, :] = mixed[:, 2 * attn :].astype(BF16)
        if s == 1:
            pooled_ref[...] = pooled
            state0_ref[...] = state0
            normed_ref[...] = normed
            raw_ref[...] = mixed[:, : 2 * attn]

    masks = head_masks()
    span = 2 * NODES
    relative = (
        lax.broadcasted_iota(jnp.int32, (NODES, span), 1)
        - lax.broadcasted_iota(jnp.int32, (NODES, span), 0)
        - WIN
    )
    for b in range(2):
        asked = slice(WIN + b * NODES, WIN + (b + 1) * NODES)
        known = slice(b * NODES, b * NODES + span)
        rows = slice(b * NODES, (b + 1) * NODES)
        offsets = facts_ref[asked, 2 * k_enc : 2 * k_enc + 1].astype(jnp.int32)
        allowed = (relative >= offsets) & (relative < offsets + WIN)
        for pair in range(attn // 128):
            lanes = slice(pair * 128, (pair + 1) * 128)
            query, key, value = qn_ref[asked, lanes], kn_ref[known, lanes], v_ref[known, lanes]
            out = jnp.zeros((NODES, 128), F32)
            for h in range(2):
                scores = dot(masked(masks[h], query), key, NT) * inv_root
                weights = jnp.where(allowed, jnp.exp(scores), 0.0)
                prob = (weights / jnp.sum(weights, axis=-1, keepdims=True)).astype(BF16)
                prob_ref[(b * attn // 128 + pair) * 2 + h] = prob
                out = out + dot(prob, masked(masks[h], value), NN)
            att_ref[rows, lanes] = out.astype(BF16)
        state1 = all0_ref[asked, :] + dot(att_ref[rows, :], wo_ref[...], NN)
        state1_ref[rows, :] = state1
        dnorm = (state1 * rms_factor(state1)).astype(BF16)
        dnorm_ref[rows, :] = dnorm
        proj_ref[rows, :] = dot(dnorm, u_ref[...], NN)

    proj_high, proj_low = split2(proj_ref[...])
    facts = facts_ref[NODES : 2 * NODES, :]
    span = lax.broadcasted_iota(jnp.int32, (NODES, ASKED), 1)
    home = lax.broadcasted_iota(jnp.int32, (NODES, 1), 0) + RIM_H
    forecast = x_ref[POINTS + RIM_G : 2 * POINTS + RIM_G, :].astype(F32)
    for parity in range(2):
        arcs = jnp.zeros((NODES, ASKED), F32)
        for k in range(k_dec):
            at = 2 * k_enc + 1 + parity * k_dec + k
            source = facts[:, at : at + 1].astype(jnp.int32) + home
            scale = facts[:, at + 2 * k_dec : at + 2 * k_dec + 1]
            arcs = arcs + jnp.where(source == span, scale, 0.0)
        high, low = split2(arcs)
        rest = dot(high, proj_high, NN) + dot(high, proj_low, NN) + dot(low, proj_high, NN)
        place = interleave(parity, (POINTS, NODES), 0)
        high, low = split2(rest)
        forecast = forecast + dot(place, high, NN) + dot(place, low, NN)
    forecast_ref[...] = forecast


def backward_kernel(k_enc, k_dec, *refs):
    (low_ref, mid_ref, high_ref, facts_ref, turned_ref, x_ref, jitter_ref, wet_ref) = refs[:8]
    (wq_ref, wo_ref, u_ref, order_ref, pooled_ref, state0_ref, normed_ref, raw_ref) = refs[8:16]
    (qn_ref, kn_ref, v_ref, prob_ref, att_ref, state1_ref, dnorm_ref) = refs[16:23]
    kept_ref, sent_ref, grad1_ref, g1b_ref, ga_ref, gq_ref, gk_ref, gv_ref, mixed_ref = refs[23:]
    attn, width = wo_ref.shape
    reach = POINTS + 2 * RIM_G
    inv_root = HEAD_DIM ** (-0.5)
    own = slice(NODES, 2 * NODES)
    own_asked = slice(WIN, WIN + NODES)
    quarter = width // 4

    def store(r, start, values):
        ref = kept_ref if r < 2 else sent_ref
        at = (r % 2) * quarter
        ref[at : at + quarter, start : start + values.shape[1]] = values.astype(BF16)

    def turned(r, values):
        return dot(order_ref[r * quarter : (r + 1) * quarter, :], values, NT).astype(BF16)

    grad_proj = jnp.zeros((ASKED, low_ref.shape[1]), F32)
    span = lax.broadcasted_iota(jnp.int32, (ASKED, NODES), 0)
    node = lax.broadcasted_iota(jnp.int32, (1, NODES), 1)
    for s, ref in enumerate((low_ref, mid_ref, high_ref)):
        lanes = slice(s * NODES, (s + 1) * NODES)
        for parity in range(2):
            arcs = jnp.zeros((ASKED, NODES), F32)
            for k in range(k_dec):
                at = 2 * k_enc + 1 + parity * k_dec + k
                source = turned_ref[at : at + 1, lanes].astype(jnp.int32) + node
                source = source + (s * NODES - NODES + RIM_H)
                scale = turned_ref[at + 2 * k_dec : at + 2 * k_dec + 1, lanes]
                arcs = arcs + jnp.where(source == span, scale, 0.0)
            grad = dot(interleave(parity, (NODES, POINTS), 1), ref[...], NN).astype(BF16)
            high, low = split2(arcs)
            grad_proj = grad_proj + dot(high, grad, NN) + dot(low, grad, NN)
    proj_high, proj_low = split2(grad_proj)
    for b in range(2):
        rows = slice(b * NODES, (b + 1) * NODES)
        state1 = state1_ref[rows, :]
        grad = dot(proj_high[rows], u_ref[...], NT) + dot(proj_low[rows], u_ref[...], NT)
        grad = rms_back(state1, rms_factor(state1), grad)
        grad1_ref[rows, :] = grad
        g1b_ref[rows, :] = grad.astype(BF16)
        ga_ref[rows, :] = dot(g1b_ref[rows, :], wo_ref[...], NT).astype(BF16)
    for r in range(4):
        dnorm = turned(r, dnorm_ref[own_asked, :])
        store(
            r,
            4 * attn + 128,
            dot(dnorm, proj_high[own_asked], NN) + dot(dnorm, proj_low[own_asked], NN),
        )
        store(r, 3 * attn, dot(turned(r, g1b_ref[own_asked, :]), att_ref[own_asked, :], NN))

    masks = head_masks()
    for pair in range(attn // 128):
        lanes = slice(pair * 128, (pair + 1) * 128)
        grad_key = jnp.zeros((NODES, 128), F32)
        grad_value = jnp.zeros((NODES, 128), F32)
        for b in range(2):
            asked = slice(WIN + b * NODES, WIN + (b + 1) * NODES)
            known = slice(b * NODES, b * NODES + 2 * NODES)
            mine = slice(NODES, 2 * NODES) if b == 0 else slice(0, NODES)
            half = slice(WIN, NODES) if b == 0 else slice(0, WIN)
            query, key, value = qn_ref[asked, lanes], kn_ref[known, lanes], v_ref[known, lanes]
            grad_out = ga_ref[b * NODES : (b + 1) * NODES, lanes]
            grad_query = jnp.zeros((WIN, 128), F32)
            for h in range(2):
                grad_head = masked(masks[h], grad_out)
                grad_prob = dot(grad_head, value, NT)
                prob = prob_ref[(b * attn // 128 + pair) * 2 + h]
                wide = prob.astype(F32)
                inner = jnp.sum(wide * grad_prob, axis=-1, keepdims=True)
                grad_scores = (wide * (grad_prob - inner)).astype(BF16)
                grad_query = grad_query + dot(grad_scores[half, :], masked(masks[h], key), NN)
                grad_key = grad_key + dot(grad_scores[:, mine], masked(masks[h], query), TN)
                grad_value = grad_value + dot(prob[:, mine], grad_head, TN)
            gq_ref[b * WIN : (b + 1) * WIN, lanes] = grad_query * inv_root
        gk_ref[:, lanes] = grad_key * inv_root
        gv_ref[:, lanes] = grad_value
    heads = same_head(attn)
    for i, ref in enumerate((gq_ref, gk_ref)):
        values = raw_ref[:, i * attn : (i + 1) * attn]
        grad = ref[...]
        factor = lax.rsqrt(head_mean(values * values, heads) + EPS)
        inner = head_mean(grad * values, heads)
        grad = factor * grad - values * (factor * factor * factor) * inner
        mixed_ref[:, i * attn : (i + 1) * attn] = grad.astype(BF16)
    mixed_ref[:, 2 * attn :] = gv_ref[...].astype(BF16)

    grad_normed = dot(mixed_ref[...], wq_ref[...], NT)
    state0 = state0_ref[...]
    grad0 = grad1_ref[own_asked, :] + rms_back(state0, rms_factor(state0), grad_normed)
    grad0_b = grad0.astype(BF16)
    pooled = pooled_ref[...]
    pool_high, pool_low = split2(rms_back(pooled, rms_factor(pooled), grad0))
    high, low = spread_matrix(facts_ref[own, :], k_enc, reach)
    for r in range(4):
        store(r, 0, dot(turned(r, normed_ref[...]), mixed_ref[...], NN))
        store(r, 4 * attn + 256, dot(turned(r, grad0_b), jitter_ref[...], NN))
        first = turned(r, pool_high)
        grad = dot(first, high, NN) + dot(first, low, NN) + dot(turned(r, pool_low), high, NN)
        pre = dot(wet_ref[r * quarter : (r + 1) * quarter, :], x_ref[...], NT)
        grad_high, grad_low = split2(grad * silu_slope(pre))
        store(r, 4 * attn, dot(grad_high, x_ref[...], NN) + dot(grad_low, x_ref[...], NN))


def call(kernel, args, outs, scratch, name):
    return pl.pallas_call(
        kernel,
        out_shape=[jax.ShapeDtypeStruct(*out) for out in outs],
        scratch_shapes=[pltpu.VMEM(*one) for one in scratch],
        compiler_params=pltpu.CompilerParams(vmem_limit_bytes=48 << 20),
        interpret=INTERPRET,
        name=name,
    )(*args)


def per_device(
    slabs,
    loader,
    hidden_jitter,
    w_noise,
    w_enc,
    enc_offset,
    enc_weight,
    w_qkv,
    window_offset,
    w_out,
    unpacker_linear_map,
    dec_offset,
    unpacker_arc_scales,
):
    members = lax.axis_size(MEMBER)
    shards = lax.axis_size(GRID)
    channels, width = w_enc.shape
    attn = w_out.shape[0]
    heads = attn // HEAD_DIM
    points = slabs.shape[1]
    nodes = enc_offset.shape[0]
    per_node = points // nodes
    sub = points // members
    noise = w_noise.shape[0]
    k_enc = enc_offset.shape[1]
    k_dec = dec_offset.shape[1]
    inv_root = HEAD_DIM ** (-0.5)

    pieces = swap(slabs[0].reshape(members, sub, 2 * channels), MEMBER)
    piece = lax.dynamic_index_in_dim(pieces, loader[0], 0, keepdims=False)
    truth = piece[:, channels:].astype(F32)

    packed = jnp.concatenate(
        [enc_offset.astype(BF16)]
        + three_terms(enc_weight)
        + [window_offset[:, None].astype(BF16)]
        + [dec_offset.reshape(nodes, per_node * k_dec).astype(BF16)]
        + three_terms(unpacker_arc_scales.reshape(nodes, per_node * k_dec)),
        axis=1,
    )
    packed = jnp.pad(packed, ((0, 0), (0, channels - packed.shape[1])))
    share = nodes // members
    member = lax.axis_index(MEMBER)
    shard = lax.axis_index(GRID)
    jitter_rows = nodes * noise // channels
    chunk = jnp.concatenate(
        [
            piece[:, :channels],
            hidden_jitter[0].reshape(jitter_rows, channels),
            lax.dynamic_slice_in_dim(packed, member * share, share, 0),
        ],
        axis=0,
    )
    got = swap(jnp.broadcast_to(chunk[None], (shards,) + chunk.shape), GRID)
    far2, low, mid, high, far1 = (
        lax.dynamic_index_in_dim(got, (shard + o) % shards, 0, keepdims=False)
        for o in (-2, -1, 0, 1, 2)
    )
    at = sub + jitter_rows
    far = jnp.where(member >= members // 2, far2[:sub], far1[:sub])
    payload = jnp.concatenate(
        [low[:sub], mid[:sub], high[:sub], far, low[at:], mid[at:], high[at:]], axis=0
    )
    got = swap(jnp.broadcast_to(payload[None], (members,) + payload.shape), MEMBER)
    x_parts = [
        got[:, i * sub : (i + 1) * sub].reshape(points, channels) for i in range(3)
    ]
    x_own = x_parts[1]
    far = got[:, 3 * sub : 4 * sub]
    x_all = jnp.concatenate(
        [far[members // 2 :].reshape(-1, channels)]
        + x_parts
        + [far[: members // 2].reshape(-1, channels)],
        axis=0,
    )
    packed = got[:, 4 * sub :].reshape(members, 3, share, channels)
    packed = packed.transpose(1, 0, 2, 3).reshape(3 * nodes, channels)
    jitter_all = jnp.concatenate([low[sub:at], mid[sub:at], high[sub:at]], axis=0)
    jitter_all = jnp.pad(jitter_all.reshape(3 * nodes, noise), ((0, 0), (0, channels - noise)))
    packed = packed.astype(F32)

    def column(start, count):
        return packed[:, start : start + count]

    def summed(start, count):
        return sum(column(start + i * count, count) for i in range(1, 3)) + column(start, count)

    each = per_node * k_dec
    at = 4 * k_enc
    facts = jnp.concatenate(
        [
            column(0, k_enc),
            summed(k_enc, k_enc),
            column(at, 1),
            column(at + 1, each),
            summed(at + 1 + each, each),
        ],
        axis=1,
    )
    facts = jnp.pad(facts, ((0, 0), (0, channels - facts.shape[1])))
    w_noise = jnp.pad(w_noise, ((0, channels - noise), (0, 0)))
    residuals = [
        ((nodes, width), F32),
        ((nodes, width), F32),
        ((nodes, width), BF16),
        ((nodes, 2 * attn), F32),
        ((3 * nodes, attn), BF16),
        ((3 * nodes, attn), BF16),
        ((3 * nodes, attn), BF16),
        ((2 * attn // HEAD_DIM, nodes, 2 * nodes), BF16),
        ((ASKED, attn), BF16),
        ((ASKED, width), F32),
        ((ASKED, width), BF16),
    ]
    forecast, *saved = call(
        functools.partial(forward_kernel, k_enc, k_dec),
        (x_all, facts, jitter_all, w_noise, w_enc, w_qkv, w_out, unpacker_linear_map),
        [((points, channels), F32)] + residuals,
        [
            ((4 * points, width), BF16),
            ((3 * nodes, width), F32),
            ((ASKED, channels), F32),
        ],
        "forward",
    )

    cells = swap(forecast.reshape(members, sub, channels), MEMBER)
    loss_scale = float(members * points * shards * channels) ** (-0.5)
    fair = jnp.sum(eased_sensitivity(cells[:, None] - cells[None, :]), axis=1)
    sensitivity = (
        eased_sensitivity(cells - truth[None]) / members - fair / (members * (members - 1))
    ) * loss_scale
    grad_forecast = swap(sensitivity.astype(BF16), MEMBER).reshape(points, channels)
    grad_low, grad_high = shifted(grad_forecast, 1), shifted(grad_forecast, -1)

    zl, x = (lax.axis_size(a) for a in MEMBER)
    zh, y, core = (lax.axis_size(a) for a in GRID)
    rows = width // (members * shards)
    order = jnp.arange(width, dtype=jnp.int32).reshape(core, x, y, zl, zh, rows)
    c_i, x_i, y_i, zl_i, zh_i, r_i = (
        lax.broadcasted_iota(jnp.int32, order.shape, d) for d in range(6)
    )
    c_i = c_i ^ lax.axis_index("core")
    target = ((((zl_i * x + x_i) * zh + zh_i) * y + y_i) * core + c_i) * rows + r_i
    target = target.reshape(width, 1)
    reorder = (lax.broadcasted_iota(jnp.int32, (width, width), 1) == target).astype(BF16)
    w_enc_turned = dot(reorder, w_enc, NT).astype(BF16)
    lanes = 4 * attn + 3 * channels
    kept, sent = call(
        functools.partial(backward_kernel, k_enc, k_dec),
        (
            grad_low,
            grad_forecast,
            grad_high,
            facts,
            facts.T,
            x_all[points : 3 * points],
            jitter_all[nodes : 2 * nodes],
            w_enc_turned,
            w_qkv,
            w_out,
            unpacker_linear_map,
            reorder,
            *saved,
        ),
        [((width // core, lanes), BF16)] * 2,
        [
            ((ASKED, width), F32),
            ((ASKED, width), BF16),
            ((ASKED, attn), BF16),
            ((nodes, attn), F32),
            ((nodes, attn), F32),
            ((nodes, attn), F32),
            ((nodes, 3 * attn), BF16),
        ],
        "backward",
    )

    total = kept.astype(F32) + lax.ppermute(sent, "core", [(0, 1), (1, 0)]).astype(F32)
    total = swap(total.astype(BF16).reshape(x * y, -1, lanes), ("x", "y"))
    total = jnp.sum(total.astype(F32), axis=0)
    total = swap(total.astype(BF16).reshape(zl * zh, rows, lanes), ("zl", "zh"))
    total = jnp.sum(total.astype(F32), axis=0)
    grad_qkv, grad_out, grad_enc, grad_map, grad_noise = (
        total[:, start:stop]
        for start, stop in (
            (0, 3 * attn),
            (3 * attn, 4 * attn),
            (4 * attn, 4 * attn + channels),
            (4 * attn + channels, 4 * attn + 2 * channels),
            (4 * attn + 2 * channels, 4 * attn + 2 * channels + noise),
        )
    )
    return (grad_noise.T, grad_enc.T, grad_qkv, grad_out.T, grad_map)


def solution(mesh):
    member, grid = mesh.shape["member"], mesh.shape["grid"]
    inner = 4 if member == 16 else 2
    fine = Mesh(
        mesh.devices.reshape(member // inner, inner, 2, grid // 4, 2), MEMBER + GRID
    )
    in_specs = (
        P(MEMBER, GRID, None),
        P(),
        P(MEMBER, GRID, None),
        P(),
        P(),
        P(GRID, None),
        P(GRID, None),
        P(),
        P(GRID),
        P(),
        P(),
        P(GRID, None),
        P(GRID, None),
    )
    both = MEMBER + GRID
    out_specs = (P(None, both), P(None, both), P(both, None), P(None, both), P(both, None))
    return jax.shard_map(
        per_device, mesh=fine, in_specs=in_specs, out_specs=out_specs, check_vma=False
    )
```

```python
import functools

import jax
import jax.numpy as jnp
from jax import lax
from jax.experimental import pallas as pl
from jax.experimental.pallas import tpu as pltpu
from jax.sharding import Mesh
from jax.sharding import PartitionSpec as P

HEAD_DIM = 64
RIM_G = 128
RIM_H = 64
WIN = 64

EPS = 1e-06
DELTA_SQ = 0.01

MEMBER = ("zl", "x")
GRID = ("zh", "y", "core")
F32 = jnp.float32
BF16 = jnp.bfloat16
INTERPRET = False
NODES = 128
POINTS = 256
ASKED = NODES + 2 * WIN


def rms_factor(values):
    return lax.rsqrt(jnp.mean(values * values, axis=-1, keepdims=True) + EPS)


def rms_back(values, factor, gradient):
    inner = jnp.mean(gradient * values, axis=-1, keepdims=True)
    return factor * gradient - values * (factor * factor * factor) * inner


def silu_slope(pre):
    sigma = jax.nn.sigmoid(pre)
    return sigma * (1.0 + pre * (1.0 - sigma))


def eased_sensitivity(diff):
    return diff * lax.rsqrt(diff * diff + DELTA_SQ)


def dot(left, right, dims, **options):
    return lax.dot_general(left, right, (dims, ((), ())), preferred_element_type=F32, **options)


NN = ((1,), (0,))
TN = ((0,), (0,))
NT = ((1,), (1,))


def two_terms(values):
    high = lax.reduce_precision(values, 8, 7)
    return high.astype(BF16), (values - high).astype(BF16)


def three_terms(values):
    high = lax.reduce_precision(values, 8, 7)
    middle = lax.reduce_precision(values - high, 8, 7)
    return [high.astype(BF16), middle.astype(BF16), (values - high - middle).astype(BF16)]


def swap(values, axes):
    return lax.all_to_all(values, axes, split_axis=0, concat_axis=0, tiled=True)


def shifted(values, step):
    count = lax.axis_size(GRID)
    return lax.ppermute(values, GRID, [(i, (i + step) % count) for i in range(count)])


def split2(values):
    high = values.astype(BF16)
    return high, (values - high.astype(F32)).astype(BF16)


def same_head(attn):
    row = lax.broadcasted_iota(jnp.int32, (attn, attn), 0) // HEAD_DIM
    column = lax.broadcasted_iota(jnp.int32, (attn, attn), 1) // HEAD_DIM
    return jnp.where(row == column, 1.0, 0.0).astype(BF16)


def head_mean(values, heads):
    high, low = split2(values)
    return (dot(high, heads, NN) + dot(low, heads, NN)) * (1.0 / HEAD_DIM)


def head_masks():
    lane = lax.broadcasted_iota(jnp.int32, (1, 2 * HEAD_DIM), 1)
    return (lane < HEAD_DIM, lane >= HEAD_DIM)


def masked(mask, values):
    return jnp.where(mask, values, jnp.zeros_like(values))


def spread_matrix(facts, k_enc, reach):
    span = lax.broadcasted_iota(jnp.int32, (NODES, reach), 1)
    home = lax.broadcasted_iota(jnp.int32, (NODES, 1), 0) * (POINTS // NODES) + RIM_G
    spread = jnp.zeros((NODES, reach), F32)
    for k in range(k_enc):
        source = facts[:, k : k + 1].astype(jnp.int32) + home
        spread = spread + jnp.where(source == span, facts[:, k_enc + k : k_enc + k + 1], 0.0)
    return split2(spread)


def interleave(parity, shape, point_dim):
    point = lax.broadcasted_iota(jnp.int32, shape, point_dim)
    node = lax.broadcasted_iota(jnp.int32, shape, 1 - point_dim)
    return jnp.where(point == 2 * node + parity, 1.0, 0.0).astype(BF16)


def forward_kernel(k_enc, k_dec, need, push, *refs):
    x_ref, facts_ref, jitter_ref, wn_ref, we_ref, wq_ref, wo_ref, u_ref = refs[:8]
    (forecast_ref, pooled_ref, state0_ref, normed_ref, raw_ref, qn_ref, kn_ref, v_ref) = refs[8:16]
    prob_ref, att_ref, state1_ref, dnorm_ref, msg_ref, all0_ref, proj_ref = refs[16:]
    attn = wo_ref.shape[0]
    reach = POINTS + 2 * RIM_G
    inv_root = HEAD_DIM ** (-0.5)

    def message_rows(i, carry):
        rows = pl.ds(pl.multiple_of(i * 128, 128), 128)
        pre = dot(x_ref[rows, :], we_ref[...], NN)
        msg_ref[rows, :] = (pre * jax.nn.sigmoid(pre)).astype(BF16)
        return carry

    lax.fori_loop(0, x_ref.shape[0] // 128, message_rows, 0)
    heads = same_head(attn)
    for s in range(3):
        rows = slice(s * NODES, (s + 1) * NODES)
        high, low = spread_matrix(facts_ref[rows, :], k_enc, reach)
        near = msg_ref[s * POINTS : s * POINTS + reach, :]
        pooled = dot(high, near, NN) + dot(low, near, NN)
        state0 = pooled * rms_factor(pooled) + dot(jitter_ref[rows, :], wn_ref[...], NN)
        all0_ref[rows, :] = state0
        normed = (state0 * rms_factor(state0)).astype(BF16)
        if s == 0:
            need(5)
        mixed = dot(normed, wq_ref[...], NN)
        queries, keys = mixed[:, :attn], mixed[:, attn : 2 * attn]
        qn_ref[rows, :] = (
            queries * lax.rsqrt(head_mean(queries * queries, heads) + EPS)
        ).astype(BF16)
        kn_ref[rows, :] = (keys * lax.rsqrt(head_mean(keys * keys, heads) + EPS)).astype(BF16)
        v_ref[rows, :] = mixed[:, 2 * attn :].astype(BF16)
        if s == 1:
            pooled_ref[...] = pooled
            state0_ref[...] = state0
            normed_ref[...] = normed
            raw_ref[...] = mixed[:, : 2 * attn]
            push(1, 2, 3, 4)
    push(5, 6, 7)
    need(6, 7)

    masks = head_masks()
    span = 2 * NODES
    relative = (
        lax.broadcasted_iota(jnp.int32, (NODES, span), 1)
        - lax.broadcasted_iota(jnp.int32, (NODES, span), 0)
        - WIN
    )
    for b in range(2):
        asked = slice(WIN + b * NODES, WIN + (b + 1) * NODES)
        known = slice(b * NODES, b * NODES + span)
        rows = slice(b * NODES, (b + 1) * NODES)
        offsets = facts_ref[asked, 2 * k_enc : 2 * k_enc + 1].astype(jnp.int32)
        allowed = (relative >= offsets) & (relative < offsets + WIN)
        for pair in range(attn // 128):
            lanes = slice(pair * 128, (pair + 1) * 128)
            query, key, value = qn_ref[asked, lanes], kn_ref[known, lanes], v_ref[known, lanes]
            out = jnp.zeros((NODES, 128), F32)
            for h in range(2):
                scores = dot(masked(masks[h], query), key, NT) * inv_root
                weights = jnp.where(allowed, jnp.exp(scores), 0.0)
                prob = (weights / jnp.sum(weights, axis=-1, keepdims=True)).astype(BF16)
                prob_ref[(b * attn // 128 + pair) * 2 + h] = prob
                out = out + dot(prob, masked(masks[h], value), NN)
            att_ref[rows, lanes] = out.astype(BF16)
        state1 = all0_ref[asked, :] + dot(att_ref[rows, :], wo_ref[...], NN)
        state1_ref[rows, :] = state1
        dnorm = (state1 * rms_factor(state1)).astype(BF16)
        dnorm_ref[rows, :] = dnorm
        proj_ref[rows, :] = dot(dnorm, u_ref[...], NN)
    push(8, 9, 10, 11)

    proj_high, proj_low = split2(proj_ref[...])
    facts = facts_ref[NODES : 2 * NODES, :]
    span = lax.broadcasted_iota(jnp.int32, (NODES, ASKED), 1)
    home = lax.broadcasted_iota(jnp.int32, (NODES, 1), 0) + RIM_H
    forecast = x_ref[POINTS + RIM_G : 2 * POINTS + RIM_G, :].astype(F32)
    for parity in range(2):
        arcs = jnp.zeros((NODES, ASKED), F32)
        for k in range(k_dec):
            at = 2 * k_enc + 1 + parity * k_dec + k
            source = facts[:, at : at + 1].astype(jnp.int32) + home
            scale = facts[:, at + 2 * k_dec : at + 2 * k_dec + 1]
            arcs = arcs + jnp.where(source == span, scale, 0.0)
        high, low = split2(arcs)
        rest = dot(high, proj_high, NN) + dot(high, proj_low, NN) + dot(low, proj_high, NN)
        place = interleave(parity, (POINTS, NODES), 0)
        high, low = split2(rest)
        forecast = forecast + dot(place, high, NN) + dot(place, low, NN)
    forecast_ref[...] = forecast


def backward_kernel(k_enc, k_dec, need, push, *refs):
    (low_ref, mid_ref, high_ref, facts_ref, turned_ref, x_ref, jitter_ref, wet_ref) = refs[:8]
    (wq_ref, wo_ref, u_ref, order_ref, pooled_ref, state0_ref, normed_ref, raw_ref) = refs[8:16]
    (qn_ref, kn_ref, v_ref, prob_ref, att_ref, state1_ref, dnorm_ref) = refs[16:23]
    kept_ref, sent_ref, grad1_ref, g1b_ref, ga_ref, gq_ref, gk_ref, gv_ref, mixed_ref = refs[23:]
    attn, width = wo_ref.shape
    reach = POINTS + 2 * RIM_G
    inv_root = HEAD_DIM ** (-0.5)
    own = slice(NODES, 2 * NODES)
    own_asked = slice(WIN, WIN + NODES)
    quarter = width // 4

    def store(r, start, values):
        ref = kept_ref if r < 2 else sent_ref
        at = (r % 2) * quarter
        ref[at : at + quarter, start : start + values.shape[1]] = values.astype(BF16)

    def turned(r, values):
        return dot(order_ref[r * quarter : (r + 1) * quarter, :], values, NT).astype(BF16)

    grad_proj = jnp.zeros((ASKED, low_ref.shape[1]), F32)
    span = lax.broadcasted_iota(jnp.int32, (ASKED, NODES), 0)
    node = lax.broadcasted_iota(jnp.int32, (1, NODES), 1)
    for s, ref in enumerate((low_ref, mid_ref, high_ref)):
        lanes = slice(s * NODES, (s + 1) * NODES)
        for parity in range(2):
            arcs = jnp.zeros((ASKED, NODES), F32)
            for k in range(k_dec):
                at = 2 * k_enc + 1 + parity * k_dec + k
                source = turned_ref[at : at + 1, lanes].astype(jnp.int32) + node
                source = source + (s * NODES - NODES + RIM_H)
                scale = turned_ref[at + 2 * k_dec : at + 2 * k_dec + 1, lanes]
                arcs = arcs + jnp.where(source == span, scale, 0.0)
            grad = dot(interleave(parity, (NODES, POINTS), 1), ref[...], NN).astype(BF16)
            high, low = split2(arcs)
            grad_proj = grad_proj + dot(high, grad, NN) + dot(low, grad, NN)
    proj_high, proj_low = split2(grad_proj)
    need(21, 10, 9)
    for b in range(2):
        rows = slice(b * NODES, (b + 1) * NODES)
        state1 = state1_ref[rows, :]
        grad = dot(proj_high[rows], u_ref[...], NT) + dot(proj_low[rows], u_ref[...], NT)
        grad = rms_back(state1, rms_factor(state1), grad)
        grad1_ref[rows, :] = grad
        g1b_ref[rows, :] = grad.astype(BF16)
        ga_ref[rows, :] = dot(g1b_ref[rows, :], wo_ref[...], NT).astype(BF16)
    need(22, 11, 20)
    for r in range(4):
        dnorm = turned(r, dnorm_ref[own_asked, :])
        store(
            r,
            4 * attn + 128,
            dot(dnorm, proj_high[own_asked], NN) + dot(dnorm, proj_low[own_asked], NN),
        )
        store(r, 3 * attn, dot(turned(r, g1b_ref[own_asked, :]), att_ref[own_asked, :], NN))

    need(16, 17, 18, 19)
    masks = head_masks()
    for pair in range(attn // 128):
        lanes = slice(pair * 128, (pair + 1) * 128)
        grad_key = jnp.zeros((NODES, 128), F32)
        grad_value = jnp.zeros((NODES, 128), F32)
        for b in range(2):
            asked = slice(WIN + b * NODES, WIN + (b + 1) * NODES)
            known = slice(b * NODES, b * NODES + 2 * NODES)
            mine = slice(NODES, 2 * NODES) if b == 0 else slice(0, NODES)
            half = slice(WIN, NODES) if b == 0 else slice(0, WIN)
            query, key, value = qn_ref[asked, lanes], kn_ref[known, lanes], v_ref[known, lanes]
            grad_out = ga_ref[b * NODES : (b + 1) * NODES, lanes]
            grad_query = jnp.zeros((WIN, 128), F32)
            for h in range(2):
                grad_head = masked(masks[h], grad_out)
                grad_prob = dot(grad_head, value, NT)
                prob = prob_ref[(b * attn // 128 + pair) * 2 + h]
                wide = prob.astype(F32)
                inner = jnp.sum(wide * grad_prob, axis=-1, keepdims=True)
                grad_scores = (wide * (grad_prob - inner)).astype(BF16)
                grad_query = grad_query + dot(grad_scores[half, :], masked(masks[h], key), NN)
                grad_key = grad_key + dot(grad_scores[:, mine], masked(masks[h], query), TN)
                grad_value = grad_value + dot(prob[:, mine], grad_head, TN)
            gq_ref[b * WIN : (b + 1) * WIN, lanes] = grad_query * inv_root
        gk_ref[:, lanes] = grad_key * inv_root
        gv_ref[:, lanes] = grad_value
    heads = same_head(attn)
    need(15)
    for i, ref in enumerate((gq_ref, gk_ref)):
        values = raw_ref[:, i * attn : (i + 1) * attn]
        grad = ref[...]
        factor = lax.rsqrt(head_mean(values * values, heads) + EPS)
        inner = head_mean(grad * values, heads)
        grad = factor * grad - values * (factor * factor * factor) * inner
        mixed_ref[:, i * attn : (i + 1) * attn] = grad.astype(BF16)
    mixed_ref[:, 2 * attn :] = gv_ref[...].astype(BF16)

    need(8, 13, 12, 14, 7)
    grad_normed = dot(mixed_ref[...], wq_ref[...], NT)
    state0 = state0_ref[...]
    grad0 = grad1_ref[own_asked, :] + rms_back(state0, rms_factor(state0), grad_normed)
    grad0_b = grad0.astype(BF16)
    pooled = pooled_ref[...]
    pool_high, pool_low = split2(rms_back(pooled, rms_factor(pooled), grad0))
    high, low = spread_matrix(facts_ref[own, :], k_enc, reach)
    for r in range(4):
        store(r, 0, dot(turned(r, normed_ref[...]), mixed_ref[...], NN))
        store(r, 4 * attn + 256, dot(turned(r, grad0_b), jitter_ref[...], NN))
        first = turned(r, pool_high)
        grad = dot(first, high, NN) + dot(first, low, NN) + dot(turned(r, pool_low), high, NN)
        pre = dot(wet_ref[r * quarter : (r + 1) * quarter, :], x_ref[...], NT)
        grad_high, grad_low = split2(grad * silu_slope(pre))
        store(r, 4 * attn, dot(grad_high, x_ref[...], NN) + dot(grad_low, x_ref[...], NN))


def call(kernel, args, late, outs, pushed, scratch, name):
    n_in, n_out = len(args), len(outs)
    sems = len(late) + len(pushed)

    def body(*refs):
        ins, out_refs = list(refs[:n_in]), list(refs[n_in : n_in + n_out])
        rest = refs[n_in + n_out :]
        sem, rest = rest[0], rest[1:]
        incoming, outgoing = {}, {}
        for j, i in enumerate(late):
            incoming[i] = pltpu.make_async_copy(ins[i], rest[j], sem.at[j])
            incoming[i].start()
            ins[i] = rest[j]
        for j, o in enumerate(pushed):
            buffer = rest[len(late) + j]
            outgoing[o] = pltpu.make_async_copy(buffer, out_refs[o], sem.at[len(late) + j])
            out_refs[o] = buffer

        def need(*which):
            for i in which:
                incoming[i].wait()

        def push(*which):
            for o in which:
                outgoing[o].start()

        kernel(need, push, *ins, *out_refs, *rest[sems:])
        for o in pushed:
            outgoing[o].wait()

    vmem = pl.BlockSpec(memory_space=pltpu.VMEM)
    hbm = pl.BlockSpec(memory_space=pltpu.HBM)
    buffers = [pltpu.VMEM(args[i].shape, args[i].dtype) for i in late]
    buffers += [pltpu.VMEM(*outs[o]) for o in pushed]
    if not INTERPRET:
        args = [
            pltpu.with_memory_space_constraint(arg, pltpu.HBM) if i in late else arg
            for i, arg in enumerate(args)
        ]
    return pl.pallas_call(
        body,
        out_shape=[
            (pltpu.HBM if o in pushed and not INTERPRET else jax.ShapeDtypeStruct)(*out)
            for o, out in enumerate(outs)
        ],
        in_specs=[hbm if i in late else vmem for i in range(n_in)],
        out_specs=[hbm if o in pushed else vmem for o in range(n_out)],
        scratch_shapes=[pltpu.SemaphoreType.DMA((sems,))]
        + buffers
        + [pltpu.VMEM(*one) for one in scratch],
        compiler_params=pltpu.CompilerParams(vmem_limit_bytes=48 << 20),
        interpret=INTERPRET,
        name=name,
    )(*args)


def per_device(
    slabs,
    loader,
    hidden_jitter,
    w_noise,
    w_enc,
    enc_offset,
    enc_weight,
    w_qkv,
    window_offset,
    w_out,
    unpacker_linear_map,
    dec_offset,
    unpacker_arc_scales,
):
    members = lax.axis_size(MEMBER)
    shards = lax.axis_size(GRID)
    channels, width = w_enc.shape
    attn = w_out.shape[0]
    heads = attn // HEAD_DIM
    points = slabs.shape[1]
    nodes = enc_offset.shape[0]
    per_node = points // nodes
    sub = points // members
    noise = w_noise.shape[0]
    k_enc = enc_offset.shape[1]
    k_dec = dec_offset.shape[1]
    inv_root = HEAD_DIM ** (-0.5)

    pieces = swap(slabs[0].reshape(members, sub, 2 * channels), MEMBER)
    piece = lax.dynamic_index_in_dim(pieces, loader[0], 0, keepdims=False)
    truth = piece[:, channels:].astype(F32)

    packed = jnp.concatenate(
        [enc_offset.astype(BF16)]
        + three_terms(enc_weight)
        + [window_offset[:, None].astype(BF16)]
        + [dec_offset.reshape(nodes, per_node * k_dec).astype(BF16)]
        + three_terms(unpacker_arc_scales.reshape(nodes, per_node * k_dec)),
        axis=1,
    )
    packed = jnp.pad(packed, ((0, 0), (0, channels - packed.shape[1])))
    share = nodes // members
    member = lax.axis_index(MEMBER)
    jitter_rows = nodes * noise // channels
    chunk = jnp.concatenate(
        [
            piece[:, :channels],
            hidden_jitter[0].reshape(jitter_rows, channels),
            lax.dynamic_slice_in_dim(packed, member * share, share, 0),
        ],
        axis=0,
    )
    low, mid, high = shifted(chunk, 1), chunk, shifted(chunk, -1)
    at = sub + jitter_rows
    pairs = []
    for m in range(members):
        step = 2 if m >= members // 2 else -2
        for i in range(shards):
            pairs.append((m * shards + i, m * shards + (i + step) % shards))
    far = lax.ppermute(piece[:, :channels], MEMBER + GRID, pairs)
    payload = jnp.concatenate(
        [low[:sub], mid[:sub], high[:sub], far, low[at:], mid[at:], high[at:]], axis=0
    )
    got = swap(jnp.broadcast_to(payload[None], (members,) + payload.shape), MEMBER)
    x_parts = [
        got[:, i * sub : (i + 1) * sub].reshape(points, channels) for i in range(3)
    ]
    x_own = x_parts[1]
    far = got[:, 3 * sub : 4 * sub]
    x_all = jnp.concatenate(
        [far[members // 2 :].reshape(-1, channels)]
        + x_parts
        + [far[: members // 2].reshape(-1, channels)],
        axis=0,
    )
    packed = got[:, 4 * sub :].reshape(members, 3, share, channels)
    packed = packed.transpose(1, 0, 2, 3).reshape(3 * nodes, channels)
    jitter_all = jnp.concatenate([low[sub:at], mid[sub:at], high[sub:at]], axis=0)
    jitter_all = jnp.pad(jitter_all.reshape(3 * nodes, noise), ((0, 0), (0, channels - noise)))
    packed = packed.astype(F32)

    def column(start, count):
        return packed[:, start : start + count]

    def summed(start, count):
        return sum(column(start + i * count, count) for i in range(1, 3)) + column(start, count)

    each = per_node * k_dec
    at = 4 * k_enc
    facts = jnp.concatenate(
        [
            column(0, k_enc),
            summed(k_enc, k_enc),
            column(at, 1),
            column(at + 1, each),
            summed(at + 1 + each, each),
        ],
        axis=1,
    )
    facts = jnp.pad(facts, ((0, 0), (0, channels - facts.shape[1])))
    w_noise = jnp.pad(w_noise, ((0, channels - noise), (0, 0)))
    residuals = [
        ((nodes, width), F32),
        ((nodes, width), F32),
        ((nodes, width), BF16),
        ((nodes, 2 * attn), F32),
        ((3 * nodes, attn), BF16),
        ((3 * nodes, attn), BF16),
        ((3 * nodes, attn), BF16),
        ((2 * attn // HEAD_DIM, nodes, 2 * nodes), BF16),
        ((ASKED, attn), BF16),
        ((ASKED, width), F32),
        ((ASKED, width), BF16),
    ]
    forecast, *saved = call(
        functools.partial(forward_kernel, k_enc, k_dec),
        (x_all, facts, jitter_all, w_noise, w_enc, w_qkv, w_out, unpacker_linear_map),
        (5, 6, 7),
        [((points, channels), F32)] + residuals,
        tuple(range(1, 1 + len(residuals))),
        [
            ((4 * points, width), BF16),
            ((3 * nodes, width), F32),
            ((ASKED, channels), F32),
        ],
        "forward",
    )

    cells = swap(forecast.reshape(members, sub, channels), MEMBER)
    loss_scale = float(members * points * shards * channels) ** (-0.5)
    fair = jnp.sum(eased_sensitivity(cells[:, None] - cells[None, :]), axis=1)
    sensitivity = (
        eased_sensitivity(cells - truth[None]) / members - fair / (members * (members - 1))
    ) * loss_scale
    grad_forecast = swap(sensitivity.astype(BF16), MEMBER).reshape(points, channels)
    grad_low, grad_high = shifted(grad_forecast, 1), shifted(grad_forecast, -1)

    zl, x = (lax.axis_size(a) for a in MEMBER)
    zh, y, core = (lax.axis_size(a) for a in GRID)
    rows = width // (members * shards)
    order = jnp.arange(width, dtype=jnp.int32).reshape(core, x, y, zl, zh, rows)
    c_i, x_i, y_i, zl_i, zh_i, r_i = (
        lax.broadcasted_iota(jnp.int32, order.shape, d) for d in range(6)
    )
    c_i = c_i ^ lax.axis_index("core")
    target = ((((zl_i * x + x_i) * zh + zh_i) * y + y_i) * core + c_i) * rows + r_i
    target = target.reshape(width, 1)
    reorder = (lax.broadcasted_iota(jnp.int32, (width, width), 1) == target).astype(BF16)
    w_enc_turned = dot(reorder, w_enc, NT).astype(BF16)
    lanes = 4 * attn + 3 * channels
    kept, sent = call(
        functools.partial(backward_kernel, k_enc, k_dec),
        (
            grad_low,
            grad_forecast,
            grad_high,
            facts,
            facts.T,
            x_all[points : 3 * points],
            jitter_all[nodes : 2 * nodes],
            w_enc_turned,
            w_qkv,
            w_out,
            unpacker_linear_map,
            reorder,
            *saved,
        ),
        (21, 10, 9, 22, 11, 20, 16, 17, 18, 19, 15, 8, 13, 12, 14, 7),
        [((width // core, lanes), BF16)] * 2,
        (),
        [
            ((ASKED, width), F32),
            ((ASKED, width), BF16),
            ((ASKED, attn), BF16),
            ((nodes, attn), F32),
            ((nodes, attn), F32),
            ((nodes, attn), F32),
            ((nodes, 3 * attn), BF16),
        ],
        "backward",
    )

    total = kept.astype(F32) + lax.ppermute(sent, "core", [(0, 1), (1, 0)]).astype(F32)
    total = swap(total.astype(BF16).reshape(x * y, -1, lanes), ("x", "y"))
    total = jnp.sum(total.astype(F32), axis=0)
    total = swap(total.astype(BF16).reshape(zl * zh, rows, lanes), ("zl", "zh"))
    total = jnp.sum(total.astype(F32), axis=0)
    grad_qkv, grad_out, grad_enc, grad_map, grad_noise = (
        total[:, start:stop]
        for start, stop in (
            (0, 3 * attn),
            (3 * attn, 4 * attn),
            (4 * attn, 4 * attn + channels),
            (4 * attn + channels, 4 * attn + 2 * channels),
            (4 * attn + 2 * channels, 4 * attn + 2 * channels + noise),
        )
    )
    return (grad_noise.T, grad_enc.T, grad_qkv, grad_out.T, grad_map)


def solution(mesh):
    member, grid = mesh.shape["member"], mesh.shape["grid"]
    inner = 4 if member == 16 else 2
    fine = Mesh(
        mesh.devices.reshape(member // inner, inner, 2, grid // 4, 2), MEMBER + GRID
    )
    in_specs = (
        P(MEMBER, GRID, None),
        P(),
        P(MEMBER, GRID, None),
        P(),
        P(),
        P(GRID, None),
        P(GRID, None),
        P(),
        P(GRID),
        P(),
        P(),
        P(GRID, None),
        P(GRID, None),
    )
    both = MEMBER + GRID
    out_specs = (P(None, both), P(None, both), P(both, None), P(None, both), P(both, None))
    return jax.shard_map(
        per_device, mesh=fine, in_specs=in_specs, out_specs=out_specs, check_vma=False
    )
```

```python
import functools

import jax
import jax.numpy as jnp
from jax import lax
from jax.experimental import pallas as pl
from jax.experimental.pallas import tpu as pltpu
from jax.sharding import Mesh
from jax.sharding import PartitionSpec as P

HEAD_DIM = 64
RIM_G = 128
RIM_H = 64
WIN = 64

EPS = 1e-06
DELTA_SQ = 0.01

MEMBER = ("zl", "x")
GRID = ("zh", "y", "core")
F32 = jnp.float32
BF16 = jnp.bfloat16
INTERPRET = False
NODES = 128
POINTS = 256
ASKED = NODES + 2 * WIN


def rms_factor(values):
    return lax.rsqrt(jnp.mean(values * values, axis=-1, keepdims=True) + EPS)


def rms_back(values, factor, gradient):
    inner = jnp.mean(gradient * values, axis=-1, keepdims=True)
    return factor * gradient - values * (factor * factor * factor) * inner


def sigmoid(values):
    return 0.5 + 0.5 * jnp.tanh(0.5 * values)


def silu_slope(pre):
    sigma = sigmoid(pre)
    return sigma * (1.0 + pre * (1.0 - sigma))


def eased_sensitivity(diff):
    return diff * lax.rsqrt(diff * diff + DELTA_SQ)


def dot(left, right, dims, **options):
    return lax.dot_general(left, right, (dims, ((), ())), preferred_element_type=F32, **options)


NN = ((1,), (0,))
TN = ((0,), (0,))
NT = ((1,), (1,))


def two_terms(values):
    high = lax.reduce_precision(values, 8, 7)
    return high.astype(BF16), (values - high).astype(BF16)


def three_terms(values):
    high = lax.reduce_precision(values, 8, 7)
    middle = lax.reduce_precision(values - high, 8, 7)
    return [high.astype(BF16), middle.astype(BF16), (values - high - middle).astype(BF16)]


def swap(values, axes):
    return lax.all_to_all(values, axes, split_axis=0, concat_axis=0, tiled=True)


def shifted(values, step):
    count = lax.axis_size(GRID)
    return lax.ppermute(values, GRID, [(i, (i + step) % count) for i in range(count)])


def split2(values):
    high = values.astype(BF16)
    return high, (values - high.astype(F32)).astype(BF16)


def same_head(attn):
    row = lax.broadcasted_iota(jnp.int32, (attn, attn), 0) // HEAD_DIM
    column = lax.broadcasted_iota(jnp.int32, (attn, attn), 1) // HEAD_DIM
    return jnp.where(row == column, 1.0, 0.0).astype(BF16)


def head_mean(values, heads):
    high, low = split2(values)
    return (dot(high, heads, NN) + dot(low, heads, NN)) * (1.0 / HEAD_DIM)


def head_masks():
    lane = lax.broadcasted_iota(jnp.int32, (1, 2 * HEAD_DIM), 1)
    return (lane < HEAD_DIM, lane >= HEAD_DIM)


def masked(mask, values):
    return jnp.where(mask, values, jnp.zeros_like(values))


def spread_matrix(facts, k_enc, reach):
    span = lax.broadcasted_iota(jnp.int32, (NODES, reach), 1)
    home = lax.broadcasted_iota(jnp.int32, (NODES, 1), 0) * (POINTS // NODES) + RIM_G
    spread = jnp.zeros((NODES, reach), F32)
    for k in range(k_enc):
        source = facts[:, k : k + 1].astype(jnp.int32) + home
        spread = spread + jnp.where(source == span, facts[:, k_enc + k : k_enc + k + 1], 0.0)
    return split2(spread)


def interleave(parity, shape, point_dim):
    point = lax.broadcasted_iota(jnp.int32, shape, point_dim)
    node = lax.broadcasted_iota(jnp.int32, shape, 1 - point_dim)
    return jnp.where(point == 2 * node + parity, 1.0, 0.0).astype(BF16)


def forward_kernel(k_enc, k_dec, need, push, *refs):
    got_ref, jitter_ref, wn_ref, we_ref, wq_ref, wo_ref, u_ref = refs[:7]
    (forecast_ref, pooled_ref, state0_ref, normed_ref, raw_ref, qn_ref, kn_ref, v_ref) = refs[7:15]
    prob_ref, att_ref, state1_ref, dnorm_ref, facts_ref, near_ref = refs[15:21]
    x_ref, msg_ref, all0_ref, proj_ref = refs[21:]
    attn = wo_ref.shape[0]
    reach = POINTS + 2 * RIM_G
    inv_root = HEAD_DIM ** (-0.5)
    members = got_ref.shape[0]
    sub, share = POINTS // members, NODES // members

    for m in range(members):
        for i in range(3):
            start = RIM_G + i * POINTS + m * sub
            x_ref[start : start + sub, :] = got_ref[m, i * sub : (i + 1) * sub, :]
        start = m * sub - RIM_G if m >= members // 2 else RIM_G + 3 * POINTS + m * sub
        x_ref[start : start + sub, :] = got_ref[m, 3 * sub : 4 * sub, :]
    near_ref[...] = x_ref[POINTS : POINTS + reach, :]
    each = 2 * k_dec
    at = 4 * k_enc + 1
    for m in range(members):
        for i in range(3):
            start = 4 * sub + i * share
            facts_ref[i * NODES + m * share : i * NODES + (m + 1) * share, :] = got_ref[
                m, start : start + share, :
            ].astype(F32)
    facts = facts_ref[...]
    weight = sum(facts[:, k_enc * i : k_enc * (i + 1)] for i in (3, 2, 1))
    scale = sum(facts[:, at + each * i : at + each * (i + 1)] for i in (3, 2, 1))
    facts_ref[:, k_enc : 2 * k_enc] = weight
    facts_ref[:, 2 * k_enc : 2 * k_enc + 1] = facts[:, at - 1 : at]
    facts_ref[:, 2 * k_enc + 1 : 2 * k_enc + 1 + each] = facts[:, at : at + each]
    facts_ref[:, 2 * k_enc + 1 + each : 2 * k_enc + 1 + 2 * each] = scale
    push(12, 13)

    def message_rows(i, carry):
        rows = pl.ds(pl.multiple_of(i * 128, 128), 128)
        pre = dot(x_ref[rows, :], we_ref[...], NN)
        msg_ref[rows, :] = (pre * sigmoid(pre)).astype(BF16)
        return carry

    lax.fori_loop(0, x_ref.shape[0] // 128, message_rows, 0)
    heads = same_head(attn)
    for s in range(3):
        rows = slice(s * NODES, (s + 1) * NODES)
        high, low = spread_matrix(facts_ref[rows, :], k_enc, reach)
        near = msg_ref[s * POINTS : s * POINTS + reach, :]
        pooled = dot(high, near, NN) + dot(low, near, NN)
        state0 = pooled * rms_factor(pooled) + dot(jitter_ref[rows, :], wn_ref[...], NN)
        all0_ref[rows, :] = state0
        normed = (state0 * rms_factor(state0)).astype(BF16)
        if s == 0:
            need(4)
        mixed = dot(normed, wq_ref[...], NN)
        queries, keys = mixed[:, :attn], mixed[:, attn : 2 * attn]
        qn_ref[rows, :] = (
            queries * lax.rsqrt(head_mean(queries * queries, heads) + EPS)
        ).astype(BF16)
        kn_ref[rows, :] = (keys * lax.rsqrt(head_mean(keys * keys, heads) + EPS)).astype(BF16)
        v_ref[rows, :] = mixed[:, 2 * attn :].astype(BF16)
        if s == 1:
            pooled_ref[...] = pooled
            state0_ref[...] = state0
            normed_ref[...] = normed
            raw_ref[...] = mixed[:, : 2 * attn]
            push(1, 2, 3, 4)
    push(5, 6, 7)
    need(5, 6)

    masks = head_masks()
    span = 2 * NODES
    relative = (
        lax.broadcasted_iota(jnp.int32, (NODES, span), 1)
        - lax.broadcasted_iota(jnp.int32, (NODES, span), 0)
        - WIN
    )
    for b in range(2):
        asked = slice(WIN + b * NODES, WIN + (b + 1) * NODES)
        known = slice(b * NODES, b * NODES + span)
        rows = slice(b * NODES, (b + 1) * NODES)
        offsets = facts_ref[asked, 2 * k_enc : 2 * k_enc + 1].astype(jnp.int32)
        allowed = (relative >= offsets) & (relative < offsets + WIN)
        for pair in range(attn // 128):
            lanes = slice(pair * 128, (pair + 1) * 128)
            query, key, value = qn_ref[asked, lanes], kn_ref[known, lanes], v_ref[known, lanes]
            out = jnp.zeros((NODES, 128), F32)
            for h in range(2):
                scores = dot(masked(masks[h], query), key, NT) * inv_root
                weights = jnp.where(allowed, jnp.exp(scores), 0.0)
                prob = (weights * (1.0 / jnp.sum(weights, axis=-1, keepdims=True))).astype(BF16)
                prob_ref[(b * attn // 128 + pair) * 2 + h] = prob
                out = out + dot(prob, masked(masks[h], value), NN)
            att_ref[rows, lanes] = out.astype(BF16)
        state1 = all0_ref[asked, :] + dot(att_ref[rows, :], wo_ref[...], NN)
        state1_ref[rows, :] = state1
        dnorm = (state1 * rms_factor(state1)).astype(BF16)
        dnorm_ref[rows, :] = dnorm
        proj_ref[rows, :] = dot(dnorm, u_ref[...], NN)
    push(8, 9, 10, 11)

    proj_high, proj_low = split2(proj_ref[...])
    facts = facts_ref[NODES : 2 * NODES, :]
    span = lax.broadcasted_iota(jnp.int32, (NODES, ASKED), 1)
    home = lax.broadcasted_iota(jnp.int32, (NODES, 1), 0) + RIM_H
    forecast = x_ref[POINTS + RIM_G : 2 * POINTS + RIM_G, :].astype(F32)
    for parity in range(2):
        arcs = jnp.zeros((NODES, ASKED), F32)
        for k in range(k_dec):
            at = 2 * k_enc + 1 + parity * k_dec + k
            source = facts[:, at : at + 1].astype(jnp.int32) + home
            scale = facts[:, at + 2 * k_dec : at + 2 * k_dec + 1]
            arcs = arcs + jnp.where(source == span, scale, 0.0)
        high, low = split2(arcs)
        rest = dot(high, proj_high, NN) + dot(high, proj_low, NN) + dot(low, proj_high, NN)
        place = interleave(parity, (POINTS, NODES), 0)
        high, low = split2(rest)
        forecast = forecast + dot(place, high, NN) + dot(place, low, NN)
    forecast_ref[...] = forecast


def prepare_kernel(k_enc, k_dec, need, push, *refs):
    facts_ref, turned_ref, x_ref, wet_ref, order_ref, normed_ref, dnorm_ref = refs[:7]
    slope_ref, nt_ref, dt_ref, sh_ref, sl_ref, ah_ref, al_ref = refs[7:]
    quarter = order_ref.shape[0] // 4
    for r in range(4):
        rows = slice(r * quarter, (r + 1) * quarter)
        slope_ref[rows, :] = silu_slope(dot(wet_ref[rows, :], x_ref[...], NT))
    push(0)
    for r in range(4):
        rows = slice(r * quarter, (r + 1) * quarter)
        nt_ref[rows, :] = dot(order_ref[rows, :], normed_ref[...], NT).astype(BF16)
        dt_ref[rows, :] = dot(order_ref[rows, :], dnorm_ref[WIN : WIN + NODES, :], NT).astype(BF16)
    push(1, 2)
    facts = facts_ref[NODES : 2 * NODES, :]
    sh_ref[...], sl_ref[...] = spread_matrix(facts, k_enc, POINTS + 2 * RIM_G)
    push(3, 4)
    span = lax.broadcasted_iota(jnp.int32, (ASKED, NODES), 0)
    node = lax.broadcasted_iota(jnp.int32, (1, NODES), 1)
    for s in range(3):
        lanes = slice(s * NODES, (s + 1) * NODES)
        for parity in range(2):
            arcs = jnp.zeros((ASKED, NODES), F32)
            for k in range(k_dec):
                at = 2 * k_enc + 1 + parity * k_dec + k
                source = turned_ref[at : at + 1, lanes].astype(jnp.int32) + node
                source = source + (s * NODES - NODES + RIM_H)
                scale = turned_ref[at + 2 * k_dec : at + 2 * k_dec + 1, lanes]
                arcs = arcs + jnp.where(source == span, scale, 0.0)
            ah_ref[2 * s + parity], al_ref[2 * s + parity] = split2(arcs)
    push(5, 6)


def backward_kernel(need, push, *refs):
    (low_ref, mid_ref, high_ref, x_ref, jitter_ref, wq_ref, wo_ref, u_ref, order_ref) = refs[:9]
    (pooled_ref, state0_ref, raw_ref, qn_ref, kn_ref, v_ref, prob_ref, att_ref) = refs[9:17]
    (state1_ref, slope_ref, nt_ref, dt_ref, sh_ref, sl_ref, ah_ref, al_ref) = refs[17:25]
    kept_ref, sent_ref, grad1_ref, g1b_ref, ga_ref, gq_ref, gk_ref, gv_ref, mixed_ref = refs[25:]
    attn, width = wo_ref.shape
    inv_root = HEAD_DIM ** (-0.5)
    own_asked = slice(WIN, WIN + NODES)
    quarter = width // 4

    def store(r, start, values):
        ref = kept_ref if r < 2 else sent_ref
        at = (r % 2) * quarter
        ref[at : at + quarter, start : start + values.shape[1]] = values.astype(BF16)

    def turned(r, values):
        return dot(order_ref[r * quarter : (r + 1) * quarter, :], values, NT).astype(BF16)

    need(23, 24)
    grad_proj = jnp.zeros((ASKED, low_ref.shape[1]), F32)
    for s, ref in enumerate((low_ref, mid_ref, high_ref)):
        for parity in range(2):
            grad = dot(interleave(parity, (NODES, POINTS), 1), ref[...], NN).astype(BF16)
            grad_proj = grad_proj + dot(ah_ref[2 * s + parity], grad, NN)
            grad_proj = grad_proj + dot(al_ref[2 * s + parity], grad, NN)
    proj_high, proj_low = split2(grad_proj)
    need(17, 7, 6)
    for b in range(2):
        rows = slice(b * NODES, (b + 1) * NODES)
        state1 = state1_ref[rows, :]
        grad = dot(proj_high[rows], u_ref[...], NT) + dot(proj_low[rows], u_ref[...], NT)
        grad = rms_back(state1, rms_factor(state1), grad)
        grad1_ref[rows, :] = grad
        g1b_ref[rows, :] = grad.astype(BF16)
        ga_ref[rows, :] = dot(g1b_ref[rows, :], wo_ref[...], NT).astype(BF16)
    need(20, 8, 16)
    for r in range(4):
        dnorm = dt_ref[r * quarter : (r + 1) * quarter, :]
        store(
            r,
            4 * attn + 128,
            dot(dnorm, proj_high[own_asked], NN) + dot(dnorm, proj_low[own_asked], NN),
        )
        store(r, 3 * attn, dot(turned(r, g1b_ref[own_asked, :]), att_ref[own_asked, :], NN))

    need(12, 13, 14, 15)
    masks = head_masks()
    for pair in range(attn // 128):
        lanes = slice(pair * 128, (pair + 1) * 128)
        grad_key = jnp.zeros((NODES, 128), F32)
        grad_value = jnp.zeros((NODES, 128), F32)
        for b in range(2):
            asked = slice(WIN + b * NODES, WIN + (b + 1) * NODES)
            known = slice(b * NODES, b * NODES + 2 * NODES)
            mine = slice(NODES, 2 * NODES) if b == 0 else slice(0, NODES)
            half = slice(WIN, NODES) if b == 0 else slice(0, WIN)
            query, key, value = qn_ref[asked, lanes], kn_ref[known, lanes], v_ref[known, lanes]
            grad_out = ga_ref[b * NODES : (b + 1) * NODES, lanes]
            grad_query = jnp.zeros((WIN, 128), F32)
            for h in range(2):
                grad_head = masked(masks[h], grad_out)
                grad_prob = dot(grad_head, value, NT)
                prob = prob_ref[(b * attn // 128 + pair) * 2 + h]
                wide = prob.astype(F32)
                inner = jnp.sum(wide * grad_prob, axis=-1, keepdims=True)
                grad_scores = (wide * (grad_prob - inner)).astype(BF16)
                grad_query = grad_query + dot(grad_scores[half, :], masked(masks[h], key), NN)
                grad_key = grad_key + dot(grad_scores[:, mine], masked(masks[h], query), TN)
                grad_value = grad_value + dot(prob[:, mine], grad_head, TN)
            gq_ref[b * WIN : (b + 1) * WIN, lanes] = grad_query * inv_root
        gk_ref[:, lanes] = grad_key * inv_root
        gv_ref[:, lanes] = grad_value
    heads = same_head(attn)
    need(11)
    for i, ref in enumerate((gq_ref, gk_ref)):
        values = raw_ref[:, i * attn : (i + 1) * attn]
        grad = ref[...]
        factor = lax.rsqrt(head_mean(values * values, heads) + EPS)
        inner = head_mean(grad * values, heads)
        grad = factor * grad - values * (factor * factor * factor) * inner
        mixed_ref[:, i * attn : (i + 1) * attn] = grad.astype(BF16)
    mixed_ref[:, 2 * attn :] = gv_ref[...].astype(BF16)

    need(5, 10, 9, 19, 18, 21, 22)
    grad_normed = dot(mixed_ref[...], wq_ref[...], NT)
    state0 = state0_ref[...]
    grad0 = grad1_ref[own_asked, :] + rms_back(state0, rms_factor(state0), grad_normed)
    grad0_b = grad0.astype(BF16)
    pooled = pooled_ref[...]
    pool_high, pool_low = split2(rms_back(pooled, rms_factor(pooled), grad0))
    high, low = sh_ref[...], sl_ref[...]
    for r in range(4):
        rows = slice(r * quarter, (r + 1) * quarter)
        store(r, 0, dot(nt_ref[rows, :], mixed_ref[...], NN))
        store(r, 4 * attn + 256, dot(turned(r, grad0_b), jitter_ref[...], NN))
        first = turned(r, pool_high)
        grad = dot(first, high, NN) + dot(first, low, NN) + dot(turned(r, pool_low), high, NN)
        grad_high, grad_low = split2(grad * slope_ref[rows, :])
        store(r, 4 * attn, dot(grad_high, x_ref[...], NN) + dot(grad_low, x_ref[...], NN))


def call(kernel, args, late, outs, pushed, scratch, name):
    n_in, n_out = len(args), len(outs)
    sems = len(late) + len(pushed)

    def body(*refs):
        ins, out_refs = list(refs[:n_in]), list(refs[n_in : n_in + n_out])
        rest = refs[n_in + n_out :]
        sem, rest = rest[0], rest[1:]
        incoming, outgoing = {}, {}
        for j, i in enumerate(late):
            incoming[i] = pltpu.make_async_copy(ins[i], rest[j], sem.at[j])
            incoming[i].start()
            ins[i] = rest[j]
        for j, o in enumerate(pushed):
            buffer = rest[len(late) + j]
            outgoing[o] = pltpu.make_async_copy(buffer, out_refs[o], sem.at[len(late) + j])
            out_refs[o] = buffer

        def need(*which):
            for i in which:
                incoming[i].wait()

        def push(*which):
            for o in which:
                outgoing[o].start()

        kernel(need, push, *ins, *out_refs, *rest[sems:])
        for o in pushed:
            outgoing[o].wait()

    vmem = pl.BlockSpec(memory_space=pltpu.VMEM)
    hbm = pl.BlockSpec(memory_space=pltpu.HBM)
    buffers = [pltpu.VMEM(args[i].shape, args[i].dtype) for i in late]
    buffers += [pltpu.VMEM(*outs[o]) for o in pushed]
    if not INTERPRET:
        args = [
            pltpu.with_memory_space_constraint(arg, pltpu.HBM) if i in late else arg
            for i, arg in enumerate(args)
        ]
    return pl.pallas_call(
        body,
        out_shape=[
            (pltpu.HBM if o in pushed and not INTERPRET else jax.ShapeDtypeStruct)(*out)
            for o, out in enumerate(outs)
        ],
        in_specs=[hbm if i in late else vmem for i in range(n_in)],
        out_specs=[hbm if o in pushed else vmem for o in range(n_out)],
        scratch_shapes=[pltpu.SemaphoreType.DMA((sems,))]
        + buffers
        + [pltpu.VMEM(*one) for one in scratch],
        compiler_params=pltpu.CompilerParams(vmem_limit_bytes=48 << 20),
        interpret=INTERPRET,
        name=name,
    )(*args)


def per_device(
    slabs,
    loader,
    hidden_jitter,
    w_noise,
    w_enc,
    enc_offset,
    enc_weight,
    w_qkv,
    window_offset,
    w_out,
    unpacker_linear_map,
    dec_offset,
    unpacker_arc_scales,
):
    members = lax.axis_size(MEMBER)
    shards = lax.axis_size(GRID)
    channels, width = w_enc.shape
    attn = w_out.shape[0]
    heads = attn // HEAD_DIM
    points = slabs.shape[1]
    nodes = enc_offset.shape[0]
    per_node = points // nodes
    sub = points // members
    noise = w_noise.shape[0]
    k_enc = enc_offset.shape[1]
    k_dec = dec_offset.shape[1]
    inv_root = HEAD_DIM ** (-0.5)

    pieces = swap(slabs[0].reshape(members, sub, 2 * channels), MEMBER)
    piece = lax.dynamic_index_in_dim(pieces, loader[0], 0, keepdims=False)
    truth = piece[:, channels:].astype(F32)

    packed = jnp.concatenate(
        [enc_offset.astype(BF16)]
        + three_terms(enc_weight)
        + [window_offset[:, None].astype(BF16)]
        + [dec_offset.reshape(nodes, per_node * k_dec).astype(BF16)]
        + three_terms(unpacker_arc_scales.reshape(nodes, per_node * k_dec)),
        axis=1,
    )
    packed = jnp.pad(packed, ((0, 0), (0, channels - packed.shape[1])))
    share = nodes // members
    member = lax.axis_index(MEMBER)
    jitter_rows = nodes * noise // channels
    chunk = jnp.concatenate(
        [
            piece[:, :channels],
            hidden_jitter[0].reshape(jitter_rows, channels),
            lax.dynamic_slice_in_dim(packed, member * share, share, 0),
        ],
        axis=0,
    )
    low, mid, high = shifted(chunk, 1), chunk, shifted(chunk, -1)
    at = sub + jitter_rows
    pairs = []
    for m in range(members):
        step = 2 if m >= members // 2 else -2
        for i in range(shards):
            pairs.append((m * shards + i, m * shards + (i + step) % shards))
    far = lax.ppermute(piece[:, :channels], MEMBER + GRID, pairs)
    payload = jnp.concatenate(
        [low[:sub], mid[:sub], high[:sub], far, low[at:], mid[at:], high[at:]], axis=0
    )
    got = swap(jnp.broadcast_to(payload[None], (members,) + payload.shape), MEMBER)
    jitter_all = jnp.concatenate([low[sub:at], mid[sub:at], high[sub:at]], axis=0)
    jitter_all = jnp.pad(jitter_all.reshape(3 * nodes, noise), ((0, 0), (0, channels - noise)))
    w_noise = jnp.pad(w_noise, ((0, channels - noise), (0, 0)))
    residuals = [
        ((nodes, width), F32),
        ((nodes, width), F32),
        ((nodes, width), BF16),
        ((nodes, 2 * attn), F32),
        ((3 * nodes, attn), BF16),
        ((3 * nodes, attn), BF16),
        ((3 * nodes, attn), BF16),
        ((2 * attn // HEAD_DIM, nodes, 2 * nodes), BF16),
        ((ASKED, attn), BF16),
        ((ASKED, width), F32),
        ((ASKED, width), BF16),
        ((3 * nodes, channels), F32),
        ((points + 2 * RIM_G, channels), BF16),
    ]
    forecast, *saved = call(
        functools.partial(forward_kernel, k_enc, k_dec),
        (got, jitter_all, w_noise, w_enc, w_qkv, w_out, unpacker_linear_map),
        (4, 5, 6),
        [((points, channels), F32)] + residuals,
        tuple(range(1, 1 + len(residuals))),
        [
            ((4 * points, channels), BF16),
            ((4 * points, width), BF16),
            ((3 * nodes, width), F32),
            ((ASKED, channels), F32),
        ],
        "forward",
    )

    cells = swap(forecast.reshape(members, sub, channels), MEMBER)
    loss_scale = float(members * points * shards * channels) ** (-0.5)
    fair = jnp.sum(eased_sensitivity(cells[:, None] - cells[None, :]), axis=1)
    sensitivity = (
        eased_sensitivity(cells - truth[None]) / members - fair / (members * (members - 1))
    ) * loss_scale
    grad_forecast = swap(sensitivity.astype(BF16), MEMBER).reshape(points, channels)
    grad_low, grad_high = shifted(grad_forecast, 1), shifted(grad_forecast, -1)

    zl, x = (lax.axis_size(a) for a in MEMBER)
    zh, y, core = (lax.axis_size(a) for a in GRID)
    rows = width // (members * shards)
    order = jnp.arange(width, dtype=jnp.int32).reshape(core, x, y, zl, zh, rows)
    c_i, x_i, y_i, zl_i, zh_i, r_i = (
        lax.broadcasted_iota(jnp.int32, order.shape, d) for d in range(6)
    )
    c_i = c_i ^ lax.axis_index("core")
    target = ((((zl_i * x + x_i) * zh + zh_i) * y + y_i) * core + c_i) * rows + r_i
    target = target.reshape(width, 1)
    reorder = (lax.broadcasted_iota(jnp.int32, (width, width), 1) == target).astype(BF16)
    w_enc_turned = dot(reorder, w_enc, NT).astype(BF16)
    lanes = 4 * attn + 3 * channels
    pooled, state0, normed, raw, query, key, value, prob, attended, state1, dnorm, facts, near = saved
    prepared = call(
        functools.partial(prepare_kernel, k_enc, k_dec),
        (facts, facts.T, near, w_enc_turned, reorder, normed, dnorm),
        (),
        [
            ((width, points + 2 * RIM_G), F32),
            ((width, nodes), BF16),
            ((width, nodes), BF16),
            ((nodes, points + 2 * RIM_G), BF16),
            ((nodes, points + 2 * RIM_G), BF16),
            ((3 * per_node, ASKED, nodes), BF16),
            ((3 * per_node, ASKED, nodes), BF16),
        ],
        tuple(range(7)),
        [],
        "prepare",
    )
    kept, sent = call(
        backward_kernel,
        (
            grad_low,
            grad_forecast,
            grad_high,
            near,
            jitter_all[nodes : 2 * nodes],
            w_qkv,
            w_out,
            unpacker_linear_map,
            reorder,
            pooled,
            state0,
            raw,
            query,
            key,
            value,
            prob,
            attended,
            state1,
            *prepared,
        ),
        (23, 24, 17, 7, 6, 20, 8, 16, 12, 13, 14, 15, 11, 5, 10, 9, 19, 18, 21, 22),
        [((width // core, lanes), BF16)] * 2,
        (),
        [
            ((ASKED, width), F32),
            ((ASKED, width), BF16),
            ((ASKED, attn), BF16),
            ((nodes, attn), F32),
            ((nodes, attn), F32),
            ((nodes, attn), F32),
            ((nodes, 3 * attn), BF16),
        ],
        "backward",
    )

    total = kept.astype(F32) + lax.ppermute(sent, "core", [(0, 1), (1, 0)]).astype(F32)
    total = swap(total.astype(BF16).reshape(x * y, -1, lanes), ("x", "y"))
    total = jnp.sum(total.astype(F32), axis=0)
    total = swap(total.astype(BF16).reshape(zl * zh, rows, lanes), ("zl", "zh"))
    total = jnp.sum(total.astype(F32), axis=0)
    grad_qkv, grad_out, grad_enc, grad_map, grad_noise = (
        total[:, start:stop]
        for start, stop in (
            (0, 3 * attn),
            (3 * attn, 4 * attn),
            (4 * attn, 4 * attn + channels),
            (4 * attn + channels, 4 * attn + 2 * channels),
            (4 * attn + 2 * channels, 4 * attn + 2 * channels + noise),
        )
    )
    return (grad_noise.T, grad_enc.T, grad_qkv, grad_out.T, grad_map)


def solution(mesh):
    member, grid = mesh.shape["member"], mesh.shape["grid"]
    inner = 4 if member == 16 else 2
    fine = Mesh(
        mesh.devices.reshape(member // inner, inner, 2, grid // 4, 2), MEMBER + GRID
    )
    in_specs = (
        P(MEMBER, GRID, None),
        P(),
        P(MEMBER, GRID, None),
        P(),
        P(),
        P(GRID, None),
        P(GRID, None),
        P(),
        P(GRID),
        P(),
        P(),
        P(GRID, None),
        P(GRID, None),
    )
    both = MEMBER + GRID
    out_specs = (P(None, both), P(None, both), P(both, None), P(None, both), P(both, None))
    return jax.shard_map(
        per_device, mesh=fine, in_specs=in_specs, out_specs=out_specs, check_vma=False
    )
```

```python
import functools

import jax
import jax.numpy as jnp
from jax import lax
from jax.experimental import pallas as pl
from jax.experimental.pallas import tpu as pltpu
from jax.sharding import Mesh
from jax.sharding import PartitionSpec as P

HEAD_DIM = 64
RIM_G = 128
RIM_H = 64
WIN = 64

EPS = 1e-06
DELTA_SQ = 0.01

MEMBER = ("zl", "x")
GRID = ("zh", "y", "core")
F32 = jnp.float32
BF16 = jnp.bfloat16
INTERPRET = False
NODES = 128
POINTS = 256
ASKED = NODES + 2 * WIN


def rms_factor(values):
    return lax.rsqrt(jnp.mean(values * values, axis=-1, keepdims=True) + EPS)


def rms_back(values, factor, gradient):
    inner = jnp.mean(gradient * values, axis=-1, keepdims=True)
    return factor * gradient - values * (factor * factor * factor) * inner


def sigmoid(values):
    return 0.5 + 0.5 * jnp.tanh(0.5 * values)


def silu_slope(pre):
    sigma = sigmoid(pre)
    return sigma * (1.0 + pre * (1.0 - sigma))


def eased_sensitivity(diff):
    return diff * lax.rsqrt(diff * diff + DELTA_SQ)


def dot(left, right, dims, **options):
    return lax.dot_general(left, right, (dims, ((), ())), preferred_element_type=F32, **options)


NN = ((1,), (0,))
TN = ((0,), (0,))
NT = ((1,), (1,))


def two_terms(values):
    high = lax.reduce_precision(values, 8, 7)
    return high.astype(BF16), (values - high).astype(BF16)


def three_terms(values):
    high = lax.reduce_precision(values, 8, 7)
    middle = lax.reduce_precision(values - high, 8, 7)
    return [high.astype(BF16), middle.astype(BF16), (values - high - middle).astype(BF16)]


def swap(values, axes):
    return lax.all_to_all(values, axes, split_axis=0, concat_axis=0, tiled=True)


def exchanged(values):
    count = lax.axis_size(GRID)
    near = lax.ppermute(values, GRID, [(i, i ^ 1) for i in range(count)])
    beyond = lax.ppermute(
        values, GRID, [(i, (i + 1 if i % 2 else i - 1) % count) for i in range(count)]
    )
    return near, beyond


def split2(values):
    high = values.astype(BF16)
    return high, (values - high.astype(F32)).astype(BF16)


def same_head(attn):
    row = lax.broadcasted_iota(jnp.int32, (attn, attn), 0) // HEAD_DIM
    column = lax.broadcasted_iota(jnp.int32, (attn, attn), 1) // HEAD_DIM
    return jnp.where(row == column, 1.0, 0.0).astype(BF16)


def head_mean(values, heads):
    return dot(values.astype(BF16), heads, NN) * (1.0 / HEAD_DIM)


def head_masks():
    lane = lax.broadcasted_iota(jnp.int32, (1, 2 * HEAD_DIM), 1)
    return (lane < HEAD_DIM, lane >= HEAD_DIM)


def masked(mask, values):
    return jnp.where(mask, values, jnp.zeros_like(values))


def spread_matrix(facts, k_enc, reach):
    span = lax.broadcasted_iota(jnp.int32, (NODES, reach), 1)
    home = lax.broadcasted_iota(jnp.int32, (NODES, 1), 0) * (POINTS // NODES) + RIM_G
    spread = jnp.zeros((NODES, reach), F32)
    for k in range(k_enc):
        source = facts[:, k : k + 1].astype(jnp.int32) + home
        spread = spread + jnp.where(source == span, facts[:, k_enc + k : k_enc + k + 1], 0.0)
    return split2(spread)


def interleave(parity, shape, point_dim):
    point = lax.broadcasted_iota(jnp.int32, shape, point_dim)
    node = lax.broadcasted_iota(jnp.int32, shape, 1 - point_dim)
    return jnp.where(point == 2 * node + parity, 1.0, 0.0).astype(BF16)


def forward_kernel(k_enc, k_dec, need, push, *refs):
    got_ref, jitter_ref, wn_ref, we_ref, wq_ref, wo_ref, u_ref = refs[:7]
    (forecast_ref, pooled_ref, state0_ref, normed_ref, raw_ref, qn_ref, kn_ref, v_ref) = refs[7:15]
    prob_ref, att_ref, state1_ref, dnorm_ref, facts_ref, near_ref = refs[15:21]
    x_ref, msg_ref, all0_ref, proj_ref = refs[21:]
    attn = wo_ref.shape[0]
    reach = POINTS + 2 * RIM_G
    inv_root = HEAD_DIM ** (-0.5)
    members = got_ref.shape[0]
    sub, share = POINTS // members, NODES // members

    for m in range(members):
        for i in range(3):
            start = RIM_G + i * POINTS + m * sub
            x_ref[start : start + sub, :] = got_ref[m, i * sub : (i + 1) * sub, :]
        start = m * sub - RIM_G if m >= members // 2 else RIM_G + 3 * POINTS + m * sub
        x_ref[start : start + sub, :] = got_ref[m, 3 * sub : 4 * sub, :]
    near_ref[...] = x_ref[POINTS : POINTS + reach, :]
    each = 2 * k_dec
    at = 4 * k_enc + 1
    for m in range(members):
        for i in range(3):
            start = 4 * sub + i * share
            facts_ref[i * NODES + m * share : i * NODES + (m + 1) * share, :] = got_ref[
                m, start : start + share, :
            ].astype(F32)
    facts = facts_ref[...]
    weight = sum(facts[:, k_enc * i : k_enc * (i + 1)] for i in (3, 2, 1))
    scale = sum(facts[:, at + each * i : at + each * (i + 1)] for i in (3, 2, 1))
    facts_ref[:, k_enc : 2 * k_enc] = weight
    facts_ref[:, 2 * k_enc : 2 * k_enc + 1] = facts[:, at - 1 : at]
    facts_ref[:, 2 * k_enc + 1 : 2 * k_enc + 1 + each] = facts[:, at : at + each]
    facts_ref[:, 2 * k_enc + 1 + each : 2 * k_enc + 1 + 2 * each] = scale
    push(12, 13)

    def message_rows(i, carry):
        rows = pl.ds(pl.multiple_of(i * 128, 128), 128)
        pre = dot(x_ref[rows, :], we_ref[...], NN)
        msg_ref[rows, :] = (pre * sigmoid(pre)).astype(BF16)
        return carry

    lax.fori_loop(0, x_ref.shape[0] // 128, message_rows, 0)
    heads = same_head(attn)
    for s in range(3):
        rows = slice(s * NODES, (s + 1) * NODES)
        high, low = spread_matrix(facts_ref[rows, :], k_enc, reach)
        near = msg_ref[s * POINTS : s * POINTS + reach, :]
        pooled = dot(high, near, NN) + dot(low, near, NN)
        state0 = pooled * rms_factor(pooled) + dot(jitter_ref[rows, :], wn_ref[...], NN)
        all0_ref[rows, :] = state0
        normed = (state0 * rms_factor(state0)).astype(BF16)
        if s == 0:
            need(4)
        mixed = dot(normed, wq_ref[...], NN)
        queries, keys = mixed[:, :attn], mixed[:, attn : 2 * attn]
        qn_ref[rows, :] = (
            queries * lax.rsqrt(head_mean(queries * queries, heads) + EPS)
        ).astype(BF16)
        kn_ref[rows, :] = (keys * lax.rsqrt(head_mean(keys * keys, heads) + EPS)).astype(BF16)
        v_ref[rows, :] = mixed[:, 2 * attn :].astype(BF16)
        if s == 1:
            pooled_ref[...] = pooled
            state0_ref[...] = state0
            normed_ref[...] = normed
            raw_ref[...] = mixed[:, : 2 * attn]
            push(1, 2, 3, 4)
    push(5, 6, 7)
    need(5, 6)

    masks = head_masks()
    span = 2 * NODES
    relative = (
        lax.broadcasted_iota(jnp.int32, (NODES, span), 1)
        - lax.broadcasted_iota(jnp.int32, (NODES, span), 0)
        - WIN
    )
    for b in range(2):
        asked = slice(WIN + b * NODES, WIN + (b + 1) * NODES)
        known = slice(b * NODES, b * NODES + span)
        rows = slice(b * NODES, (b + 1) * NODES)
        offsets = facts_ref[asked, 2 * k_enc : 2 * k_enc + 1].astype(jnp.int32)
        allowed = (relative >= offsets) & (relative < offsets + WIN)
        for pair in range(attn // 128):
            lanes = slice(pair * 128, (pair + 1) * 128)
            query, key, value = qn_ref[asked, lanes], kn_ref[known, lanes], v_ref[known, lanes]
            out = jnp.zeros((NODES, 128), F32)
            for h in range(2):
                scores = dot(masked(masks[h], query), key, NT) * inv_root
                weights = jnp.where(allowed, jnp.exp(scores), 0.0)
                prob = (weights * (1.0 / jnp.sum(weights, axis=-1, keepdims=True))).astype(BF16)
                prob_ref[(b * attn // 128 + pair) * 2 + h] = prob
                out = out + dot(prob, masked(masks[h], value), NN)
            att_ref[rows, lanes] = out.astype(BF16)
        state1 = all0_ref[asked, :] + dot(att_ref[rows, :], wo_ref[...], NN)
        state1_ref[rows, :] = state1
        dnorm = (state1 * rms_factor(state1)).astype(BF16)
        dnorm_ref[rows, :] = dnorm
        proj_ref[rows, :] = dot(dnorm, u_ref[...], NN)
    push(8, 9, 10, 11)

    proj_high, proj_low = split2(proj_ref[...])
    facts = facts_ref[NODES : 2 * NODES, :]
    span = lax.broadcasted_iota(jnp.int32, (NODES, ASKED), 1)
    home = lax.broadcasted_iota(jnp.int32, (NODES, 1), 0) + RIM_H
    forecast = x_ref[POINTS + RIM_G : 2 * POINTS + RIM_G, :].astype(F32)
    for parity in range(2):
        arcs = jnp.zeros((NODES, ASKED), F32)
        for k in range(k_dec):
            at = 2 * k_enc + 1 + parity * k_dec + k
            source = facts[:, at : at + 1].astype(jnp.int32) + home
            scale = facts[:, at + 2 * k_dec : at + 2 * k_dec + 1]
            arcs = arcs + jnp.where(source == span, scale, 0.0)
        high, low = split2(arcs)
        rest = dot(high, proj_high, NN) + dot(high, proj_low, NN) + dot(low, proj_high, NN)
        place = interleave(parity, (POINTS, NODES), 0)
        high, low = split2(rest)
        forecast = forecast + dot(place, high, NN) + dot(place, low, NN)
    forecast_ref[...] = forecast


def prepare_kernel(k_enc, k_dec, need, push, *refs):
    facts_ref, turned_ref, x_ref, wet_ref, order_ref, normed_ref, dnorm_ref = refs[:7]
    slope_ref, nt_ref, dt_ref, sh_ref, ah_ref, al_ref = refs[7:]
    quarter = order_ref.shape[0] // 4
    for r in range(4):
        rows = slice(r * quarter, (r + 1) * quarter)
        slope_ref[rows, :] = silu_slope(dot(wet_ref[rows, :], x_ref[...], NT))
    push(0)
    for r in range(4):
        rows = slice(r * quarter, (r + 1) * quarter)
        nt_ref[rows, :] = dot(order_ref[rows, :], normed_ref[...], NT).astype(BF16)
        dt_ref[rows, :] = dot(order_ref[rows, :], dnorm_ref[WIN : WIN + NODES, :], NT).astype(BF16)
    push(1, 2)
    facts = facts_ref[NODES : 2 * NODES, :]
    sh_ref[...] = spread_matrix(facts, k_enc, POINTS + 2 * RIM_G)[0]
    push(3)
    span = lax.broadcasted_iota(jnp.int32, (ASKED, NODES), 0)
    node = lax.broadcasted_iota(jnp.int32, (1, NODES), 1)
    for s in range(3):
        lanes = slice(s * NODES, (s + 1) * NODES)
        for parity in range(2):
            arcs = jnp.zeros((ASKED, NODES), F32)
            for k in range(k_dec):
                at = 2 * k_enc + 1 + parity * k_dec + k
                source = turned_ref[at : at + 1, lanes].astype(jnp.int32) + node
                source = source + (s * NODES - NODES + RIM_H)
                scale = turned_ref[at + 2 * k_dec : at + 2 * k_dec + 1, lanes]
                arcs = arcs + jnp.where(source == span, scale, 0.0)
            ah_ref[2 * s + parity], al_ref[2 * s + parity] = split2(arcs)
    push(4, 5)


def backward_kernel(need, push, *refs):
    (near_ref, mid_ref, beyond_ref, x_ref, jitter_ref, wq_ref, wo_ref, u_ref, order_ref) = refs[:9]
    (pooled_ref, state0_ref, raw_ref, qn_ref, kn_ref, v_ref, prob_ref, att_ref) = refs[9:17]
    (state1_ref, slope_ref, nt_ref, dt_ref, sh_ref, ah_ref, al_ref) = refs[17:24]
    core_ref = refs[24]
    kept_ref, sent_ref, grad1_ref, g1b_ref, ga_ref, gq_ref, gk_ref, gv_ref, mixed_ref = refs[25:]
    attn, width = wo_ref.shape
    inv_root = HEAD_DIM ** (-0.5)
    own_asked = slice(WIN, WIN + NODES)
    quarter = width // 4

    def store(r, start, values):
        ref = kept_ref if r < 2 else sent_ref
        at = (r % 2) * quarter
        ref[at : at + quarter, start : start + values.shape[1]] = values.astype(BF16)

    def turned(r, values):
        return dot(order_ref[r * quarter : (r + 1) * quarter, :], values, NT).astype(BF16)

    need(22, 23)
    odd = core_ref[0] == 1
    near, beyond = near_ref[...].astype(F32), beyond_ref[...].astype(F32)
    low = jnp.where(odd, near, beyond).astype(BF16)
    high = jnp.where(odd, beyond, near).astype(BF16)
    grad_proj = jnp.zeros((ASKED, mid_ref.shape[1]), F32)
    for s, part in enumerate((low, mid_ref[...], high)):
        for parity in range(2):
            grad = dot(interleave(parity, (NODES, POINTS), 1), part, NN).astype(BF16)
            grad_proj = grad_proj + dot(ah_ref[2 * s + parity], grad, NN)
            grad_proj = grad_proj + dot(al_ref[2 * s + parity], grad, NN)
    proj_high, proj_low = split2(grad_proj)
    need(17, 7, 6)
    for b in range(2):
        rows = slice(b * NODES, (b + 1) * NODES)
        state1 = state1_ref[rows, :]
        grad = dot(proj_high[rows], u_ref[...], NT) + dot(proj_low[rows], u_ref[...], NT)
        grad = rms_back(state1, rms_factor(state1), grad)
        grad1_ref[rows, :] = grad
        g1b_ref[rows, :] = grad.astype(BF16)
        ga_ref[rows, :] = dot(g1b_ref[rows, :], wo_ref[...], NT).astype(BF16)
    need(20, 8, 16)
    for r in range(4):
        dnorm = dt_ref[r * quarter : (r + 1) * quarter, :]
        store(
            r,
            4 * attn + 128,
            dot(dnorm, proj_high[own_asked], NN) + dot(dnorm, proj_low[own_asked], NN),
        )
        store(r, 3 * attn, dot(turned(r, g1b_ref[own_asked, :]), att_ref[own_asked, :], NN))

    need(12, 13, 14, 15)
    masks = head_masks()
    for pair in range(attn // 128):
        lanes = slice(pair * 128, (pair + 1) * 128)
        grad_key = jnp.zeros((NODES, 128), F32)
        grad_value = jnp.zeros((NODES, 128), F32)
        for b in range(2):
            asked = slice(WIN + b * NODES, WIN + (b + 1) * NODES)
            known = slice(b * NODES, b * NODES + 2 * NODES)
            mine = slice(NODES, 2 * NODES) if b == 0 else slice(0, NODES)
            half = slice(WIN, NODES) if b == 0 else slice(0, WIN)
            query, key, value = qn_ref[asked, lanes], kn_ref[known, lanes], v_ref[known, lanes]
            grad_out = ga_ref[b * NODES : (b + 1) * NODES, lanes]
            grad_query = jnp.zeros((WIN, 128), F32)
            for h in range(2):
                grad_head = masked(masks[h], grad_out)
                grad_prob = dot(grad_head, value, NT)
                prob = prob_ref[(b * attn // 128 + pair) * 2 + h]
                wide = prob.astype(F32)
                inner = jnp.sum(wide * grad_prob, axis=-1, keepdims=True)
                grad_scores = (wide * (grad_prob - inner)).astype(BF16)
                grad_query = grad_query + dot(grad_scores[half, :], masked(masks[h], key), NN)
                grad_key = grad_key + dot(grad_scores[:, mine], masked(masks[h], query), TN)
                grad_value = grad_value + dot(prob[:, mine], grad_head, TN)
            gq_ref[b * WIN : (b + 1) * WIN, lanes] = grad_query * inv_root
        gk_ref[:, lanes] = grad_key * inv_root
        gv_ref[:, lanes] = grad_value
    heads = same_head(attn)
    need(11)
    for i, ref in enumerate((gq_ref, gk_ref)):
        values = raw_ref[:, i * attn : (i + 1) * attn]
        grad = ref[...]
        factor = lax.rsqrt(head_mean(values * values, heads) + EPS)
        inner = head_mean(grad * values, heads)
        grad = factor * grad - values * (factor * factor * factor) * inner
        mixed_ref[:, i * attn : (i + 1) * attn] = grad.astype(BF16)
    mixed_ref[:, 2 * attn :] = gv_ref[...].astype(BF16)

    need(5, 10, 9, 19, 18, 21)
    grad_normed = dot(mixed_ref[...], wq_ref[...], NT)
    state0 = state0_ref[...]
    grad0 = grad1_ref[own_asked, :] + rms_back(state0, rms_factor(state0), grad_normed)
    grad0_b = grad0.astype(BF16)
    pooled = pooled_ref[...]
    grad_pooled = rms_back(pooled, rms_factor(pooled), grad0).astype(BF16)
    spread = sh_ref[...]
    for r in range(4):
        rows = slice(r * quarter, (r + 1) * quarter)
        store(r, 0, dot(nt_ref[rows, :], mixed_ref[...], NN))
        store(r, 4 * attn + 256, dot(turned(r, grad0_b), jitter_ref[...], NN))
        grad = dot(turned(r, grad_pooled), spread, NN) * slope_ref[rows, :]
        store(r, 4 * attn, dot(grad.astype(BF16), x_ref[...], NN))


def loss_kernel(scale, need, push, cells_ref, truth_ref, out_ref):
    members = cells_ref.shape[0]
    cells = [cells_ref[m] for m in range(members)]
    fair = [jnp.zeros_like(cells[0]) for _ in range(members)]
    for m in range(members):
        for n in range(m + 1, members):
            slope = eased_sensitivity(cells[m] - cells[n])
            fair[m] = fair[m] + slope
            fair[n] = fair[n] - slope
    for m in range(members):
        first = eased_sensitivity(cells[m] - truth_ref[...]) * (scale / members)
        out_ref[m] = (first - fair[m] * (scale / (members * (members - 1)))).astype(BF16)


def call(kernel, args, late, outs, pushed, scratch, name):
    n_in, n_out = len(args), len(outs)
    sems = len(late) + len(pushed)
    smem = pl.BlockSpec(memory_space=pltpu.SMEM)

    def body(*refs):
        ins, out_refs = list(refs[:n_in]), list(refs[n_in : n_in + n_out])
        rest = refs[n_in + n_out :]
        sem, rest = rest[0], rest[1:]
        incoming, outgoing = {}, {}
        for j, i in enumerate(late):
            incoming[i] = pltpu.make_async_copy(ins[i], rest[j], sem.at[j])
            incoming[i].start()
            ins[i] = rest[j]
        for j, o in enumerate(pushed):
            buffer = rest[len(late) + j]
            outgoing[o] = pltpu.make_async_copy(buffer, out_refs[o], sem.at[len(late) + j])
            out_refs[o] = buffer

        def need(*which):
            for i in which:
                incoming[i].wait()

        def push(*which):
            for o in which:
                outgoing[o].start()

        kernel(need, push, *ins, *out_refs, *rest[sems:])
        for o in pushed:
            outgoing[o].wait()

    vmem = pl.BlockSpec(memory_space=pltpu.VMEM)
    hbm = pl.BlockSpec(memory_space=pltpu.HBM)
    buffers = [pltpu.VMEM(args[i].shape, args[i].dtype) for i in late]
    buffers += [pltpu.VMEM(*outs[o]) for o in pushed]
    if not INTERPRET:
        args = [
            pltpu.with_memory_space_constraint(arg, pltpu.HBM) if i in late else arg
            for i, arg in enumerate(args)
        ]
    return pl.pallas_call(
        body,
        out_shape=[
            (pltpu.HBM if o in pushed and not INTERPRET else jax.ShapeDtypeStruct)(*out)
            for o, out in enumerate(outs)
        ],
        in_specs=[
            hbm if i in late else (smem if arg.shape == (1,) else vmem)
            for i, arg in enumerate(args)
        ],
        out_specs=[hbm if o in pushed else vmem for o in range(n_out)],
        scratch_shapes=[pltpu.SemaphoreType.DMA((max(sems, 1),))]
        + buffers
        + [pltpu.VMEM(*one) for one in scratch],
        compiler_params=pltpu.CompilerParams(vmem_limit_bytes=48 << 20),
        interpret=INTERPRET,
        name=name,
    )(*args)


def per_device(
    slabs,
    loader,
    hidden_jitter,
    w_noise,
    w_enc,
    enc_offset,
    enc_weight,
    w_qkv,
    window_offset,
    w_out,
    unpacker_linear_map,
    dec_offset,
    unpacker_arc_scales,
):
    members = lax.axis_size(MEMBER)
    shards = lax.axis_size(GRID)
    channels, width = w_enc.shape
    attn = w_out.shape[0]
    heads = attn // HEAD_DIM
    points = slabs.shape[1]
    nodes = enc_offset.shape[0]
    per_node = points // nodes
    sub = points // members
    noise = w_noise.shape[0]
    k_enc = enc_offset.shape[1]
    k_dec = dec_offset.shape[1]
    inv_root = HEAD_DIM ** (-0.5)

    pieces = swap(slabs[0].reshape(members, sub, 2 * channels), MEMBER)
    piece = lax.dynamic_index_in_dim(pieces, loader[0], 0, keepdims=False)
    truth = piece[:, channels:].astype(F32)

    packed = jnp.concatenate(
        [enc_offset.astype(BF16)]
        + three_terms(enc_weight)
        + [window_offset[:, None].astype(BF16)]
        + [dec_offset.reshape(nodes, per_node * k_dec).astype(BF16)]
        + three_terms(unpacker_arc_scales.reshape(nodes, per_node * k_dec)),
        axis=1,
    )
    packed = jnp.pad(packed, ((0, 0), (0, channels - packed.shape[1])))
    share = nodes // members
    member = lax.axis_index(MEMBER)
    jitter_rows = nodes * noise // channels
    chunk = jnp.concatenate(
        [
            piece[:, :channels],
            hidden_jitter[0].reshape(jitter_rows, channels),
            lax.dynamic_slice_in_dim(packed, member * share, share, 0),
        ],
        axis=0,
    )
    near, beyond = exchanged(chunk)
    odd = lax.axis_index("core") == 1
    low, mid, high = jnp.where(odd, near, beyond), chunk, jnp.where(odd, beyond, near)
    at = sub + jitter_rows
    pairs = []
    for m in range(members):
        step = 2 if m >= members // 2 else -2
        for i in range(shards):
            pairs.append((m * shards + i, m * shards + (i + step) % shards))
    far = lax.ppermute(piece[:, :channels], MEMBER + GRID, pairs)
    payload = jnp.concatenate(
        [low[:sub], mid[:sub], high[:sub], far, low[at:], mid[at:], high[at:]], axis=0
    )
    got = swap(jnp.broadcast_to(payload[None], (members,) + payload.shape), MEMBER)
    jitter_all = jnp.concatenate([low[sub:at], mid[sub:at], high[sub:at]], axis=0)
    jitter_all = jnp.pad(jitter_all.reshape(3 * nodes, noise), ((0, 0), (0, channels - noise)))
    w_noise = jnp.pad(w_noise, ((0, channels - noise), (0, 0)))
    residuals = [
        ((nodes, width), F32),
        ((nodes, width), F32),
        ((nodes, width), BF16),
        ((nodes, 2 * attn), F32),
        ((3 * nodes, attn), BF16),
        ((3 * nodes, attn), BF16),
        ((3 * nodes, attn), BF16),
        ((2 * attn // HEAD_DIM, nodes, 2 * nodes), BF16),
        ((ASKED, attn), BF16),
        ((ASKED, width), F32),
        ((ASKED, width), BF16),
        ((3 * nodes, channels), F32),
        ((points + 2 * RIM_G, channels), BF16),
    ]
    forecast, *saved = call(
        functools.partial(forward_kernel, k_enc, k_dec),
        (got, jitter_all, w_noise, w_enc, w_qkv, w_out, unpacker_linear_map),
        (4, 5, 6),
        [((points, channels), F32)] + residuals,
        tuple(range(1, 1 + len(residuals))),
        [
            ((4 * points, channels), BF16),
            ((4 * points, width), BF16),
            ((3 * nodes, width), F32),
            ((ASKED, channels), F32),
        ],
        "forward",
    )

    cells = swap(forecast.reshape(members, sub, channels), MEMBER)
    loss_scale = float(members * points * shards * channels) ** (-0.5)
    (sensitivity,) = call(
        functools.partial(loss_kernel, loss_scale),
        (cells, truth),
        (),
        [((members, sub, channels), BF16)],
        (),
        [],
        "loss",
    )
    grad_forecast = swap(sensitivity, MEMBER).reshape(points, channels)
    grad_near, grad_beyond = exchanged(grad_forecast)

    zl, x = (lax.axis_size(a) for a in MEMBER)
    zh, y, core = (lax.axis_size(a) for a in GRID)
    rows = width // (members * shards)
    order = jnp.arange(width, dtype=jnp.int32).reshape(core, x, y, zl, zh, rows)
    c_i, x_i, y_i, zl_i, zh_i, r_i = (
        lax.broadcasted_iota(jnp.int32, order.shape, d) for d in range(6)
    )
    c_i = c_i ^ lax.axis_index("core")
    target = ((((zl_i * x + x_i) * zh + zh_i) * y + y_i) * core + c_i) * rows + r_i
    target = target.reshape(width, 1)
    reorder = (lax.broadcasted_iota(jnp.int32, (width, width), 1) == target).astype(BF16)
    w_enc_turned = dot(reorder, w_enc, NT).astype(BF16)
    lanes = 4 * attn + 3 * channels
    pooled, state0, normed, raw, query, key, value, prob, attended, state1, dnorm, facts, near = saved
    prepared = call(
        functools.partial(prepare_kernel, k_enc, k_dec),
        (facts, facts.T, near, w_enc_turned, reorder, normed, dnorm),
        (),
        [
            ((width, points + 2 * RIM_G), F32),
            ((width, nodes), BF16),
            ((width, nodes), BF16),
            ((nodes, points + 2 * RIM_G), BF16),
            ((3 * per_node, ASKED, nodes), BF16),
            ((3 * per_node, ASKED, nodes), BF16),
        ],
        tuple(range(6)),
        [],
        "prepare",
    )
    kept, sent = call(
        backward_kernel,
        (
            grad_near,
            grad_forecast,
            grad_beyond,
            near,
            jitter_all[nodes : 2 * nodes],
            w_qkv,
            w_out,
            unpacker_linear_map,
            reorder,
            pooled,
            state0,
            raw,
            query,
            key,
            value,
            prob,
            attended,
            state1,
            *prepared,
            lax.axis_index("core").astype(jnp.int32).reshape(1),
        ),
        (22, 23, 17, 7, 6, 20, 8, 16, 12, 13, 14, 15, 11, 5, 10, 9, 19, 18, 21),
        [((width // core, lanes), BF16)] * 2,
        (),
        [
            ((ASKED, width), F32),
            ((ASKED, width), BF16),
            ((ASKED, attn), BF16),
            ((nodes, attn), F32),
            ((nodes, attn), F32),
            ((nodes, attn), F32),
            ((nodes, 3 * attn), BF16),
        ],
        "backward",
    )

    total = kept.astype(F32) + lax.ppermute(sent, "core", [(0, 1), (1, 0)]).astype(F32)
    total = swap(total.astype(BF16).reshape(x * y, -1, lanes), ("x", "y"))
    total = jnp.sum(total.astype(F32), axis=0)
    total = swap(total.astype(BF16).reshape(zl * zh, rows, lanes), ("zl", "zh"))
    total = jnp.sum(total.astype(F32), axis=0)
    grad_qkv, grad_out, grad_enc, grad_map, grad_noise = (
        total[:, start:stop]
        for start, stop in (
            (0, 3 * attn),
            (3 * attn, 4 * attn),
            (4 * attn, 4 * attn + channels),
            (4 * attn + channels, 4 * attn + 2 * channels),
            (4 * attn + 2 * channels, 4 * attn + 2 * channels + noise),
        )
    )
    return (grad_noise.T, grad_enc.T, grad_qkv, grad_out.T, grad_map)


def solution(mesh):
    member, grid = mesh.shape["member"], mesh.shape["grid"]
    inner = 4 if member == 16 else 2
    fine = Mesh(
        mesh.devices.reshape(member // inner, inner, 2, grid // 4, 2), MEMBER + GRID
    )
    in_specs = (
        P(MEMBER, GRID, None),
        P(),
        P(MEMBER, GRID, None),
        P(),
        P(),
        P(GRID, None),
        P(GRID, None),
        P(),
        P(GRID),
        P(),
        P(),
        P(GRID, None),
        P(GRID, None),
    )
    both = MEMBER + GRID
    out_specs = (P(None, both), P(None, both), P(both, None), P(None, both), P(both, None))
    return jax.shard_map(
        per_device, mesh=fine, in_specs=in_specs, out_specs=out_specs, check_vma=False
    )
```

```python
import functools

import jax
import jax.numpy as jnp
from jax import lax
from jax.experimental import pallas as pl
from jax.experimental.pallas import tpu as pltpu
from jax.sharding import Mesh
from jax.sharding import PartitionSpec as P

HEAD_DIM = 64
RIM_G = 128
RIM_H = 64
WIN = 64

EPS = 1e-06
DELTA_SQ = 0.01

MEMBER = ("zl", "x")
GRID = ("zh", "y", "core")
F32 = jnp.float32
BF16 = jnp.bfloat16
INTERPRET = False
NODES = 128
POINTS = 256
ASKED = NODES + 2 * WIN


def rms_factor(values):
    return lax.rsqrt(jnp.mean(values * values, axis=-1, keepdims=True) + EPS)


def rms_back(values, factor, gradient):
    inner = jnp.mean(gradient * values, axis=-1, keepdims=True)
    return factor * gradient - values * (factor * factor * factor) * inner


def sigmoid(values):
    return 0.5 + 0.5 * jnp.tanh(0.5 * values)


def silu_slope(pre):
    sigma = sigmoid(pre)
    return sigma * (1.0 + pre * (1.0 - sigma))


def eased_sensitivity(diff):
    return diff * lax.rsqrt(diff * diff + DELTA_SQ)


def dot(left, right, dims, **options):
    return lax.dot_general(left, right, (dims, ((), ())), preferred_element_type=F32, **options)


NN = ((1,), (0,))
TN = ((0,), (0,))
NT = ((1,), (1,))


def swap(values, axes):
    return lax.all_to_all(values, axes, split_axis=0, concat_axis=0, tiled=True)


def exchanged(values):
    count = lax.axis_size(GRID)
    near = lax.ppermute(values, GRID, [(i, i ^ 1) for i in range(count)])
    beyond = lax.ppermute(
        values, GRID, [(i, (i + 1 if i % 2 else i - 1) % count) for i in range(count)]
    )
    return near, beyond


def split2(values):
    high = values.astype(BF16)
    return high, (values - high.astype(F32)).astype(BF16)


def same_head(attn):
    row = lax.broadcasted_iota(jnp.int32, (attn, attn), 0) // HEAD_DIM
    column = lax.broadcasted_iota(jnp.int32, (attn, attn), 1) // HEAD_DIM
    return jnp.where(row == column, 1.0, 0.0).astype(BF16)


def head_mean(values, heads):
    return dot(values.astype(BF16), heads, NN) * (1.0 / HEAD_DIM)


def head_masks():
    lane = lax.broadcasted_iota(jnp.int32, (1, 2 * HEAD_DIM), 1)
    return (lane < HEAD_DIM, lane >= HEAD_DIM)


def masked(mask, values):
    return jnp.where(mask, values, jnp.zeros_like(values))


def spread_matrix(facts, k_enc, reach):
    span = lax.broadcasted_iota(jnp.int32, (NODES, reach), 1)
    home = lax.broadcasted_iota(jnp.int32, (NODES, 1), 0) * (POINTS // NODES) + RIM_G
    spread = jnp.zeros((NODES, reach), F32)
    for k in range(k_enc):
        source = facts[:, k : k + 1].astype(jnp.int32) + home
        spread = spread + jnp.where(source == span, facts[:, k_enc + k : k_enc + k + 1], 0.0)
    return split2(spread)


def interleave(parity, shape, point_dim):
    point = lax.broadcasted_iota(jnp.int32, shape, point_dim)
    node = lax.broadcasted_iota(jnp.int32, shape, 1 - point_dim)
    return jnp.where(point == 2 * node + parity, 1.0, 0.0).astype(BF16)


def split3(values):
    high = values.astype(BF16)
    rest = values - high.astype(F32)
    middle = rest.astype(BF16)
    return high, middle, (rest - middle.astype(F32)).astype(BF16)


def pack_kernel(need, push, member_ref, off_ref, w_ref, win_ref, jit_ref, doff_ref, dw_ref, *refs):
    out_ref, all_ref = refs
    k_enc, k_dec = w_ref.shape[0], dw_ref.shape[0]
    noise = jit_ref.shape[0]
    all_ref[...] = jnp.zeros_like(all_ref)
    all_ref[:k_enc, :] = off_ref[...].astype(F32)
    for i, term in enumerate(split3(w_ref[...])):
        all_ref[k_enc * (i + 1) : k_enc * (i + 2), :] = term.astype(F32)
    at = 4 * k_enc
    all_ref[at : at + 1, :] = win_ref[...].astype(F32)
    at += 1
    tables = (doff_ref[...].astype(F32).astype(BF16),) + split3(dw_ref[...])
    for i, table in enumerate(tables):
        for parity in range(POINTS // NODES):
            start = at + (i * (POINTS // NODES) + parity) * k_dec
            place = interleave(parity, (POINTS, NODES), 0)
            all_ref[start : start + k_dec, :] = dot(table, place, NN)
    width = all_ref.shape[0]
    each = width // noise
    rows = NODES // each
    jitter = jnp.zeros((rows, width), F32)
    target = lax.broadcasted_iota(jnp.int32, (rows, NODES), 0)
    node = lax.broadcasted_iota(jnp.int32, (rows, NODES), 1)
    source = lax.broadcasted_iota(jnp.int32, (noise, width), 0)
    lane = lax.broadcasted_iota(jnp.int32, (noise, width), 1)
    for b in range(each):
        pick = jnp.where(node == target * each + b, 1.0, 0.0).astype(BF16)
        shift = jnp.where(lane == source + b * noise, 1.0, 0.0).astype(BF16)
        jitter = jitter + dot(dot(pick, jit_ref[...], NT).astype(BF16), shift, NN)
    out_ref[:rows, :] = jitter.astype(BF16)
    share = out_ref.shape[0] - rows
    row = lax.broadcasted_iota(jnp.int32, (share, NODES), 0) + member_ref[0] * share
    pick = jnp.where(row == lax.broadcasted_iota(jnp.int32, (share, NODES), 1), 1.0, 0.0)
    out_ref[rows:, :] = dot(pick.astype(BF16), all_ref[...].astype(BF16), NT).astype(BF16)


def forward_kernel(k_enc, k_dec, need, push, *refs):
    got_ref, jitter_ref, wn_ref, we_ref, wq_ref, wo_ref, u_ref = refs[:7]
    (forecast_ref, pooled_ref, state0_ref, normed_ref, raw_ref, qn_ref, kn_ref, v_ref) = refs[7:15]
    prob_ref, att_ref, state1_ref, dnorm_ref, facts_ref, near_ref = refs[15:21]
    x_ref, msg_ref, all0_ref, proj_ref = refs[21:]
    attn = wo_ref.shape[0]
    reach = POINTS + 2 * RIM_G
    inv_root = HEAD_DIM ** (-0.5)
    members = got_ref.shape[0]
    sub, share = POINTS // members, NODES // members

    for m in range(members):
        for i in range(3):
            start = RIM_G + i * POINTS + m * sub
            x_ref[start : start + sub, :] = got_ref[m, i * sub : (i + 1) * sub, :]
        start = m * sub - RIM_G if m >= members // 2 else RIM_G + 3 * POINTS + m * sub
        x_ref[start : start + sub, :] = got_ref[m, 3 * sub : 4 * sub, :]
    near_ref[...] = x_ref[POINTS : POINTS + reach, :]
    each = 2 * k_dec
    at = 4 * k_enc + 1
    for m in range(members):
        for i in range(3):
            start = 4 * sub + i * share
            facts_ref[i * NODES + m * share : i * NODES + (m + 1) * share, :] = got_ref[
                m, start : start + share, :
            ].astype(F32)
    facts = facts_ref[...]
    weight = sum(facts[:, k_enc * i : k_enc * (i + 1)] for i in (3, 2, 1))
    scale = sum(facts[:, at + each * i : at + each * (i + 1)] for i in (3, 2, 1))
    facts_ref[:, k_enc : 2 * k_enc] = weight
    facts_ref[:, 2 * k_enc : 2 * k_enc + 1] = facts[:, at - 1 : at]
    facts_ref[:, 2 * k_enc + 1 : 2 * k_enc + 1 + each] = facts[:, at : at + each]
    facts_ref[:, 2 * k_enc + 1 + each : 2 * k_enc + 1 + 2 * each] = scale
    push(12, 13)

    def message_rows(i, carry):
        rows = pl.ds(pl.multiple_of(i * 128, 128), 128)
        pre = dot(x_ref[rows, :], we_ref[...], NN)
        msg_ref[rows, :] = (pre * sigmoid(pre)).astype(BF16)
        return carry

    lax.fori_loop(0, x_ref.shape[0] // 128, message_rows, 0)
    heads = same_head(attn)
    for s in range(3):
        rows = slice(s * NODES, (s + 1) * NODES)
        high, low = spread_matrix(facts_ref[rows, :], k_enc, reach)
        near = msg_ref[s * POINTS : s * POINTS + reach, :]
        pooled = dot(high, near, NN) + dot(low, near, NN)
        state0 = pooled * rms_factor(pooled) + dot(jitter_ref[rows, :], wn_ref[...], NN)
        all0_ref[rows, :] = state0
        normed = (state0 * rms_factor(state0)).astype(BF16)
        if s == 0:
            need(4)
        mixed = dot(normed, wq_ref[...], NN)
        queries, keys = mixed[:, :attn], mixed[:, attn : 2 * attn]
        qn_ref[rows, :] = (
            queries * lax.rsqrt(head_mean(queries * queries, heads) + EPS)
        ).astype(BF16)
        kn_ref[rows, :] = (keys * lax.rsqrt(head_mean(keys * keys, heads) + EPS)).astype(BF16)
        v_ref[rows, :] = mixed[:, 2 * attn :].astype(BF16)
        if s == 1:
            pooled_ref[...] = pooled
            state0_ref[...] = state0
            normed_ref[...] = normed
            raw_ref[...] = mixed[:, : 2 * attn]
            push(1, 2, 3, 4)
    push(5, 6, 7)
    need(5, 6)

    masks = head_masks()
    span = 2 * NODES
    relative = (
        lax.broadcasted_iota(jnp.int32, (NODES, span), 1)
        - lax.broadcasted_iota(jnp.int32, (NODES, span), 0)
        - WIN
    )
    for b in range(2):
        asked = slice(WIN + b * NODES, WIN + (b + 1) * NODES)
        known = slice(b * NODES, b * NODES + span)
        rows = slice(b * NODES, (b + 1) * NODES)
        offsets = facts_ref[asked, 2 * k_enc : 2 * k_enc + 1].astype(jnp.int32)
        allowed = (relative >= offsets) & (relative < offsets + WIN)
        for pair in range(attn // 128):
            lanes = slice(pair * 128, (pair + 1) * 128)
            query, key, value = qn_ref[asked, lanes], kn_ref[known, lanes], v_ref[known, lanes]
            out = jnp.zeros((NODES, 128), F32)
            for h in range(2):
                scores = dot(masked(masks[h], query), key, NT) * inv_root
                weights = jnp.where(allowed, jnp.exp(scores), 0.0)
                prob = (weights * (1.0 / jnp.sum(weights, axis=-1, keepdims=True))).astype(BF16)
                prob_ref[(b * attn // 128 + pair) * 2 + h] = prob
                out = out + dot(prob, masked(masks[h], value), NN)
            att_ref[rows, lanes] = out.astype(BF16)
        state1 = all0_ref[asked, :] + dot(att_ref[rows, :], wo_ref[...], NN)
        state1_ref[rows, :] = state1
        dnorm = (state1 * rms_factor(state1)).astype(BF16)
        dnorm_ref[rows, :] = dnorm
        proj_ref[rows, :] = dot(dnorm, u_ref[...], NN)
    push(8, 9, 10, 11)

    proj_high, proj_low = split2(proj_ref[...])
    facts = facts_ref[NODES : 2 * NODES, :]
    span = lax.broadcasted_iota(jnp.int32, (NODES, ASKED), 1)
    home = lax.broadcasted_iota(jnp.int32, (NODES, 1), 0) + RIM_H
    forecast = x_ref[POINTS + RIM_G : 2 * POINTS + RIM_G, :].astype(F32)
    for parity in range(2):
        arcs = jnp.zeros((NODES, ASKED), F32)
        for k in range(k_dec):
            at = 2 * k_enc + 1 + parity * k_dec + k
            source = facts[:, at : at + 1].astype(jnp.int32) + home
            scale = facts[:, at + 2 * k_dec : at + 2 * k_dec + 1]
            arcs = arcs + jnp.where(source == span, scale, 0.0)
        high, low = split2(arcs)
        rest = dot(high, proj_high, NN) + dot(high, proj_low, NN) + dot(low, proj_high, NN)
        place = interleave(parity, (POINTS, NODES), 0)
        high, low = split2(rest)
        forecast = forecast + dot(place, high, NN) + dot(place, low, NN)
    forecast_ref[...] = forecast


def prepare_kernel(k_enc, k_dec, need, push, *refs):
    facts_ref, turned_ref, x_ref, wet_ref, order_ref, normed_ref, dnorm_ref = refs[:7]
    slope_ref, nt_ref, dt_ref, sh_ref, ah_ref, al_ref = refs[7:]
    quarter = order_ref.shape[0] // 4
    need(2)
    for r in range(4):
        rows = slice(r * quarter, (r + 1) * quarter)
        slope_ref[rows, :] = silu_slope(dot(wet_ref[rows, :], x_ref[...], NT))
    push(0)
    need(4, 5, 6, 0)
    for r in range(4):
        rows = slice(r * quarter, (r + 1) * quarter)
        nt_ref[rows, :] = dot(order_ref[rows, :], normed_ref[...], NT).astype(BF16)
        dt_ref[rows, :] = dot(order_ref[rows, :], dnorm_ref[WIN : WIN + NODES, :], NT).astype(BF16)
    push(1, 2)
    facts = facts_ref[NODES : 2 * NODES, :]
    sh_ref[...] = spread_matrix(facts, k_enc, POINTS + 2 * RIM_G)[0]
    push(3)
    span = lax.broadcasted_iota(jnp.int32, (ASKED, NODES), 0)
    node = lax.broadcasted_iota(jnp.int32, (1, NODES), 1)
    for s in range(3):
        lanes = slice(s * NODES, (s + 1) * NODES)
        for parity in range(2):
            arcs = jnp.zeros((ASKED, NODES), F32)
            for k in range(k_dec):
                at = 2 * k_enc + 1 + parity * k_dec + k
                source = turned_ref[at : at + 1, lanes].astype(jnp.int32) + node
                source = source + (s * NODES - NODES + RIM_H)
                scale = turned_ref[at + 2 * k_dec : at + 2 * k_dec + 1, lanes]
                arcs = arcs + jnp.where(source == span, scale, 0.0)
            ah_ref[2 * s + parity], al_ref[2 * s + parity] = split2(arcs)
    push(4, 5)


def backward_kernel(need, push, *refs):
    (near_ref, mid_ref, beyond_ref, x_ref, jitter_ref, wq_ref, wo_ref, u_ref, order_ref) = refs[:9]
    (pooled_ref, state0_ref, raw_ref, qn_ref, kn_ref, v_ref, prob_ref, att_ref) = refs[9:17]
    (state1_ref, slope_ref, nt_ref, dt_ref, sh_ref, ah_ref, al_ref) = refs[17:24]
    core_ref = refs[24]
    kept_ref, sent_ref, grad1_ref, g1b_ref, ga_ref, gq_ref, gk_ref, gv_ref, mixed_ref = refs[25:]
    attn, width = wo_ref.shape
    inv_root = HEAD_DIM ** (-0.5)
    own_asked = slice(WIN, WIN + NODES)
    quarter = width // 4

    def store(r, start, values):
        ref = kept_ref if r < 2 else sent_ref
        at = (r % 2) * quarter
        ref[at : at + quarter, start : start + values.shape[1]] = values.astype(BF16)

    def turned(r, values):
        return dot(order_ref[r * quarter : (r + 1) * quarter, :], values, NT).astype(BF16)

    need(22, 23)
    odd = core_ref[0] == 1
    near, beyond = near_ref[...].astype(F32), beyond_ref[...].astype(F32)
    low = jnp.where(odd, near, beyond).astype(BF16)
    high = jnp.where(odd, beyond, near).astype(BF16)
    grad_proj = jnp.zeros((ASKED, mid_ref.shape[1]), F32)
    for s, part in enumerate((low, mid_ref[...], high)):
        for parity in range(2):
            grad = dot(interleave(parity, (NODES, POINTS), 1), part, NN).astype(BF16)
            grad_proj = grad_proj + dot(ah_ref[2 * s + parity], grad, NN)
            grad_proj = grad_proj + dot(al_ref[2 * s + parity], grad, NN)
    proj_high, proj_low = split2(grad_proj)
    need(17, 7, 6)
    for b in range(2):
        rows = slice(b * NODES, (b + 1) * NODES)
        state1 = state1_ref[rows, :]
        grad = dot(proj_high[rows], u_ref[...], NT) + dot(proj_low[rows], u_ref[...], NT)
        grad = rms_back(state1, rms_factor(state1), grad)
        grad1_ref[rows, :] = grad
        g1b_ref[rows, :] = grad.astype(BF16)
        ga_ref[rows, :] = dot(g1b_ref[rows, :], wo_ref[...], NT).astype(BF16)
    need(20, 8, 16)
    for r in range(4):
        dnorm = dt_ref[r * quarter : (r + 1) * quarter, :]
        store(
            r,
            4 * attn + 128,
            dot(dnorm, proj_high[own_asked], NN) + dot(dnorm, proj_low[own_asked], NN),
        )
        store(r, 3 * attn, dot(turned(r, g1b_ref[own_asked, :]), att_ref[own_asked, :], NN))

    need(12, 13, 14, 15)
    masks = head_masks()
    for pair in range(attn // 128):
        lanes = slice(pair * 128, (pair + 1) * 128)
        grad_key = jnp.zeros((NODES, 128), F32)
        grad_value = jnp.zeros((NODES, 128), F32)
        for b in range(2):
            asked = slice(WIN + b * NODES, WIN + (b + 1) * NODES)
            known = slice(b * NODES, b * NODES + 2 * NODES)
            mine = slice(NODES, 2 * NODES) if b == 0 else slice(0, NODES)
            half = slice(WIN, NODES) if b == 0 else slice(0, WIN)
            query, key, value = qn_ref[asked, lanes], kn_ref[known, lanes], v_ref[known, lanes]
            grad_out = ga_ref[b * NODES : (b + 1) * NODES, lanes]
            grad_query = jnp.zeros((WIN, 128), F32)
            for h in range(2):
                grad_head = masked(masks[h], grad_out)
                grad_prob = dot(grad_head, value, NT)
                prob = prob_ref[(b * attn // 128 + pair) * 2 + h]
                wide = prob.astype(F32)
                inner = jnp.sum(wide * grad_prob, axis=-1, keepdims=True)
                grad_scores = (wide * (grad_prob - inner)).astype(BF16)
                grad_query = grad_query + dot(grad_scores[half, :], masked(masks[h], key), NN)
                grad_key = grad_key + dot(grad_scores[:, mine], masked(masks[h], query), TN)
                grad_value = grad_value + dot(prob[:, mine], grad_head, TN)
            gq_ref[b * WIN : (b + 1) * WIN, lanes] = grad_query * inv_root
        gk_ref[:, lanes] = grad_key * inv_root
        gv_ref[:, lanes] = grad_value
    heads = same_head(attn)
    need(11)
    for i, ref in enumerate((gq_ref, gk_ref)):
        values = raw_ref[:, i * attn : (i + 1) * attn]
        grad = ref[...]
        factor = lax.rsqrt(head_mean(values * values, heads) + EPS)
        inner = head_mean(grad * values, heads)
        grad = factor * grad - values * (factor * factor * factor) * inner
        mixed_ref[:, i * attn : (i + 1) * attn] = grad.astype(BF16)
    mixed_ref[:, 2 * attn :] = gv_ref[...].astype(BF16)

    need(5, 10, 9, 19, 18, 21)
    grad_normed = dot(mixed_ref[...], wq_ref[...], NT)
    state0 = state0_ref[...]
    grad0 = grad1_ref[own_asked, :] + rms_back(state0, rms_factor(state0), grad_normed)
    grad0_b = grad0.astype(BF16)
    pooled = pooled_ref[...]
    grad_pooled = rms_back(pooled, rms_factor(pooled), grad0).astype(BF16)
    spread = sh_ref[...]
    for r in range(4):
        rows = slice(r * quarter, (r + 1) * quarter)
        store(r, 0, dot(nt_ref[rows, :], mixed_ref[...], NN))
        store(r, 4 * attn + 256, dot(turned(r, grad0_b), jitter_ref[...], NN))
        grad = dot(turned(r, grad_pooled), spread, NN) * slope_ref[rows, :]
        store(r, 4 * attn, dot(grad.astype(BF16), x_ref[...], NN))


def loss_kernel(scale, need, push, cells_ref, truth_ref, out_ref):
    members = cells_ref.shape[0]
    cells = [cells_ref[m] for m in range(members)]
    fair = [jnp.zeros_like(cells[0]) for _ in range(members)]
    for m in range(members):
        for n in range(m + 1, members):
            slope = eased_sensitivity(cells[m] - cells[n])
            fair[m] = fair[m] + slope
            fair[n] = fair[n] - slope
    for m in range(members):
        first = eased_sensitivity(cells[m] - truth_ref[...]) * (scale / members)
        out_ref[m] = (first - fair[m] * (scale / (members * (members - 1)))).astype(BF16)


def call(kernel, args, late, outs, pushed, scratch, name):
    n_in, n_out = len(args), len(outs)
    sems = len(late) + len(pushed)
    smem = pl.BlockSpec(memory_space=pltpu.SMEM)

    def body(*refs):
        ins, out_refs = list(refs[:n_in]), list(refs[n_in : n_in + n_out])
        rest = refs[n_in + n_out :]
        sem, rest = rest[0], rest[1:]
        incoming, outgoing = {}, {}
        for j, i in enumerate(late):
            incoming[i] = pltpu.make_async_copy(ins[i], rest[j], sem.at[j])
            incoming[i].start()
            ins[i] = rest[j]
        for j, o in enumerate(pushed):
            buffer = rest[len(late) + j]
            outgoing[o] = pltpu.make_async_copy(buffer, out_refs[o], sem.at[len(late) + j])
            out_refs[o] = buffer

        def need(*which):
            for i in which:
                incoming[i].wait()

        def push(*which):
            for o in which:
                outgoing[o].start()

        kernel(need, push, *ins, *out_refs, *rest[sems:])
        for o in pushed:
            outgoing[o].wait()

    vmem = pl.BlockSpec(memory_space=pltpu.VMEM)
    hbm = pl.BlockSpec(memory_space=pltpu.HBM)
    buffers = [pltpu.VMEM(args[i].shape, args[i].dtype) for i in late]
    buffers += [pltpu.VMEM(*outs[o]) for o in pushed]
    if not INTERPRET:
        args = [
            pltpu.with_memory_space_constraint(arg, pltpu.HBM) if i in late else arg
            for i, arg in enumerate(args)
        ]
    return pl.pallas_call(
        body,
        out_shape=[
            (pltpu.HBM if o in pushed and not INTERPRET else jax.ShapeDtypeStruct)(*out)
            for o, out in enumerate(outs)
        ],
        in_specs=[
            hbm if i in late else (smem if arg.shape == (1,) else vmem)
            for i, arg in enumerate(args)
        ],
        out_specs=[hbm if o in pushed else vmem for o in range(n_out)],
        scratch_shapes=[pltpu.SemaphoreType.DMA((max(sems, 1),))]
        + buffers
        + [pltpu.VMEM(*one) for one in scratch],
        compiler_params=pltpu.CompilerParams(vmem_limit_bytes=48 << 20),
        interpret=INTERPRET,
        name=name,
    )(*args)


def per_device(
    slabs,
    loader,
    hidden_jitter,
    w_noise,
    w_enc,
    enc_offset,
    enc_weight,
    w_qkv,
    window_offset,
    w_out,
    unpacker_linear_map,
    dec_offset,
    unpacker_arc_scales,
):
    members = lax.axis_size(MEMBER)
    shards = lax.axis_size(GRID)
    channels, width = w_enc.shape
    attn = w_out.shape[0]
    heads = attn // HEAD_DIM
    points = slabs.shape[1]
    nodes = enc_offset.shape[0]
    per_node = points // nodes
    sub = points // members
    noise = w_noise.shape[0]
    k_enc = enc_offset.shape[1]
    k_dec = dec_offset.shape[1]
    inv_root = HEAD_DIM ** (-0.5)

    zl, x = (lax.axis_size(a) for a in MEMBER)
    zh, y, core = (lax.axis_size(a) for a in GRID)
    rows = width // (members * shards)
    order = jnp.arange(width, dtype=jnp.int32).reshape(core, x, y, zl, zh, rows)
    c_i, x_i, y_i, zl_i, zh_i, r_i = (
        lax.broadcasted_iota(jnp.int32, order.shape, d) for d in range(6)
    )
    c_i = c_i ^ lax.axis_index("core")
    target = ((((zl_i * x + x_i) * zh + zh_i) * y + y_i) * core + c_i) * rows + r_i
    target = target.reshape(width, 1)
    reorder = (lax.broadcasted_iota(jnp.int32, (width, width), 1) == target).astype(BF16)
    w_enc_turned = dot(reorder, w_enc, NT).astype(BF16)

    pieces = swap(slabs[0].reshape(members, sub, 2 * channels), MEMBER)
    piece = lax.dynamic_index_in_dim(pieces, loader[0], 0, keepdims=False)
    truth = piece[:, channels:].astype(F32)

    share = nodes // members
    member = lax.axis_index(MEMBER)
    jitter_rows = nodes * noise // channels
    (packed,) = call(
        pack_kernel,
        (
            member.astype(jnp.int32).reshape(1),
            enc_offset.T,
            enc_weight.T,
            window_offset.reshape(1, nodes),
            hidden_jitter[0].T,
            dec_offset.T,
            unpacker_arc_scales.T,
        ),
        (),
        [((jitter_rows + share, channels), BF16)],
        (),
        [((channels, nodes), F32)],
        "pack",
    )
    chunk = jnp.concatenate([piece[:, :channels], packed], axis=0)
    near, beyond = exchanged(chunk)
    odd = lax.axis_index("core") == 1
    low, mid, high = jnp.where(odd, near, beyond), chunk, jnp.where(odd, beyond, near)
    at = sub + jitter_rows
    pairs = []
    for m in range(members):
        step = 2 if m >= members // 2 else -2
        for i in range(shards):
            pairs.append((m * shards + i, m * shards + (i + step) % shards))
    far = lax.ppermute(piece[:, :channels], MEMBER + GRID, pairs)
    payload = jnp.concatenate(
        [low[:sub], mid[:sub], high[:sub], far, low[at:], mid[at:], high[at:]], axis=0
    )
    got = swap(jnp.broadcast_to(payload[None], (members,) + payload.shape), MEMBER)
    got, reorder, w_enc_turned = lax.optimization_barrier((got, reorder, w_enc_turned))
    jitter_all = jnp.concatenate([low[sub:at], mid[sub:at], high[sub:at]], axis=0)
    jitter_all = jnp.pad(jitter_all.reshape(3 * nodes, noise), ((0, 0), (0, channels - noise)))
    w_noise = jnp.pad(w_noise, ((0, channels - noise), (0, 0)))
    residuals = [
        ((nodes, width), F32),
        ((nodes, width), F32),
        ((nodes, width), BF16),
        ((nodes, 2 * attn), F32),
        ((3 * nodes, attn), BF16),
        ((3 * nodes, attn), BF16),
        ((3 * nodes, attn), BF16),
        ((2 * attn // HEAD_DIM, nodes, 2 * nodes), BF16),
        ((ASKED, attn), BF16),
        ((ASKED, width), F32),
        ((ASKED, width), BF16),
        ((3 * nodes, channels), F32),
        ((points + 2 * RIM_G, channels), BF16),
    ]
    forecast, *saved = call(
        functools.partial(forward_kernel, k_enc, k_dec),
        (got, jitter_all, w_noise, w_enc, w_qkv, w_out, unpacker_linear_map),
        (4, 5, 6),
        [((points, channels), F32)] + residuals,
        tuple(range(1, 1 + len(residuals))),
        [
            ((4 * points, channels), BF16),
            ((4 * points, width), BF16),
            ((3 * nodes, width), F32),
            ((ASKED, channels), F32),
        ],
        "forward",
    )

    cells = swap(forecast.reshape(members, sub, channels), MEMBER)
    pooled, state0, normed, raw, query, key, value, prob, attended, state1, dnorm, facts, near = saved
    prepared = call(
        functools.partial(prepare_kernel, k_enc, k_dec),
        (facts, facts.T, near, w_enc_turned, reorder, normed, dnorm),
        (2, 4, 5, 6, 0),
        [
            ((width, points + 2 * RIM_G), F32),
            ((width, nodes), BF16),
            ((width, nodes), BF16),
            ((nodes, points + 2 * RIM_G), BF16),
            ((3 * per_node, ASKED, nodes), BF16),
            ((3 * per_node, ASKED, nodes), BF16),
        ],
        tuple(range(6)),
        [],
        "prepare",
    )
    cells, *prepared = lax.optimization_barrier((cells, *prepared))
    loss_scale = float(members * points * shards * channels) ** (-0.5)
    (sensitivity,) = call(
        functools.partial(loss_kernel, loss_scale),
        (cells, truth),
        (),
        [((members, sub, channels), BF16)],
        (),
        [],
        "loss",
    )
    grad_forecast = swap(sensitivity, MEMBER).reshape(points, channels)
    grad_near, grad_beyond = exchanged(grad_forecast)

    lanes = 4 * attn + 3 * channels
    kept, sent = call(
        backward_kernel,
        (
            grad_near,
            grad_forecast,
            grad_beyond,
            near,
            jitter_all[nodes : 2 * nodes],
            w_qkv,
            w_out,
            unpacker_linear_map,
            reorder,
            pooled,
            state0,
            raw,
            query,
            key,
            value,
            prob,
            attended,
            state1,
            *prepared,
            lax.axis_index("core").astype(jnp.int32).reshape(1),
        ),
        (22, 23, 17, 7, 6, 20, 8, 16, 12, 13, 14, 15, 11, 5, 10, 9, 19, 18, 21),
        [((width // core, lanes), BF16)] * 2,
        (),
        [
            ((ASKED, width), F32),
            ((ASKED, width), BF16),
            ((ASKED, attn), BF16),
            ((nodes, attn), F32),
            ((nodes, attn), F32),
            ((nodes, attn), F32),
            ((nodes, 3 * attn), BF16),
        ],
        "backward",
    )

    total = kept.astype(F32) + lax.ppermute(sent, "core", [(0, 1), (1, 0)]).astype(F32)
    total = swap(total.astype(BF16).reshape(x * y, -1, lanes), ("x", "y"))
    total = jnp.sum(total.astype(F32), axis=0)
    total = swap(total.astype(BF16).reshape(zl * zh, rows, lanes), ("zl", "zh"))
    total = jnp.sum(total.astype(F32), axis=0)
    grad_qkv, grad_out, grad_enc, grad_map, grad_noise = (
        total[:, start:stop]
        for start, stop in (
            (0, 3 * attn),
            (3 * attn, 4 * attn),
            (4 * attn, 4 * attn + channels),
            (4 * attn + channels, 4 * attn + 2 * channels),
            (4 * attn + 2 * channels, 4 * attn + 2 * channels + noise),
        )
    )
    return (grad_noise.T, grad_enc.T, grad_qkv, grad_out.T, grad_map)


def solution(mesh):
    member, grid = mesh.shape["member"], mesh.shape["grid"]
    inner = 4 if member == 16 else 2
    fine = Mesh(
        mesh.devices.reshape(member // inner, inner, 2, grid // 4, 2), MEMBER + GRID
    )
    in_specs = (
        P(MEMBER, GRID, None),
        P(),
        P(MEMBER, GRID, None),
        P(),
        P(),
        P(GRID, None),
        P(GRID, None),
        P(),
        P(GRID),
        P(),
        P(),
        P(GRID, None),
        P(GRID, None),
    )
    both = MEMBER + GRID
    out_specs = (P(None, both), P(None, both), P(both, None), P(None, both), P(both, None))
    return jax.shard_map(
        per_device, mesh=fine, in_specs=in_specs, out_specs=out_specs, check_vma=False
    )
```

```python
import functools

import jax
import jax.numpy as jnp
from jax import lax
from jax.experimental import pallas as pl
from jax.experimental.pallas import tpu as pltpu
from jax.sharding import Mesh
from jax.sharding import PartitionSpec as P

HEAD_DIM = 64
RIM_G = 128
RIM_H = 64
WIN = 64

EPS = 1e-06
DELTA_SQ = 0.01

MEMBER = ("zl", "x")
GRID = ("zh", "y", "core")
F32 = jnp.float32
BF16 = jnp.bfloat16
INTERPRET = False
NODES = 128
POINTS = 256
ASKED = NODES + 2 * WIN


def rms_factor(values):
    return lax.rsqrt(jnp.mean(values * values, axis=-1, keepdims=True) + EPS)


def rms_back(values, factor, gradient):
    inner = jnp.mean(gradient * values, axis=-1, keepdims=True)
    return factor * gradient - values * (factor * factor * factor) * inner


def sigmoid(values):
    return 0.5 + 0.5 * jnp.tanh(0.5 * values)


def silu_slope(pre):
    sigma = sigmoid(pre)
    return sigma * (1.0 + pre * (1.0 - sigma))


def eased_sensitivity(diff):
    return diff * lax.rsqrt(diff * diff + DELTA_SQ)


def dot(left, right, dims, **options):
    return lax.dot_general(left, right, (dims, ((), ())), preferred_element_type=F32, **options)


NN = ((1,), (0,))
TN = ((0,), (0,))
NT = ((1,), (1,))


def swap(values, axes):
    return lax.all_to_all(values, axes, split_axis=0, concat_axis=0, tiled=True)


def beyond_pair(values):
    count = lax.axis_size(GRID)
    pairs = [(i, (i + 1 if i % 2 else i - 1) % count) for i in range(count)]
    return lax.ppermute(values, GRID, pairs)


def split2(values):
    high = values.astype(BF16)
    return high, (values - high.astype(F32)).astype(BF16)


def same_head(attn):
    row = lax.broadcasted_iota(jnp.int32, (attn, attn), 0) // HEAD_DIM
    column = lax.broadcasted_iota(jnp.int32, (attn, attn), 1) // HEAD_DIM
    return jnp.where(row == column, 1.0, 0.0).astype(BF16)


def head_mean(values, heads):
    return dot(values.astype(BF16), heads, NN) * (1.0 / HEAD_DIM)


def head_masks():
    lane = lax.broadcasted_iota(jnp.int32, (1, 2 * HEAD_DIM), 1)
    return (lane < HEAD_DIM, lane >= HEAD_DIM)


def masked(mask, values):
    return jnp.where(mask, values, jnp.zeros_like(values))


def spread_matrix(facts, k_enc, reach):
    span = lax.broadcasted_iota(jnp.int32, (NODES, reach), 1)
    home = lax.broadcasted_iota(jnp.int32, (NODES, 1), 0) * (POINTS // NODES) + RIM_G
    spread = jnp.zeros((NODES, reach), F32)
    for k in range(k_enc):
        source = facts[:, k : k + 1].astype(jnp.int32) + home
        spread = spread + jnp.where(source == span, facts[:, k_enc + k : k_enc + k + 1], 0.0)
    return split2(spread)


def interleave(parity, shape, point_dim):
    point = lax.broadcasted_iota(jnp.int32, shape, point_dim)
    node = lax.broadcasted_iota(jnp.int32, shape, 1 - point_dim)
    return jnp.where(point == 2 * node + parity, 1.0, 0.0).astype(BF16)


def split3(values):
    high = values.astype(BF16)
    rest = values - high.astype(F32)
    middle = rest.astype(BF16)
    return high, middle, (rest - middle.astype(F32)).astype(BF16)


def pack_kernel(need, push, member_ref, off_ref, w_ref, win_ref, jit_ref, doff_ref, dw_ref, *refs):
    out_ref, all_ref = refs
    k_enc, k_dec = w_ref.shape[0], dw_ref.shape[0]
    noise = jit_ref.shape[0]
    all_ref[...] = jnp.zeros_like(all_ref)
    need(1, 2, 3, 4, 5, 6)
    all_ref[:k_enc, :] = off_ref[...].astype(F32)
    for i, term in enumerate(split3(w_ref[...])):
        all_ref[k_enc * (i + 1) : k_enc * (i + 2), :] = term.astype(F32)
    at = 4 * k_enc
    all_ref[at : at + 1, :] = win_ref[...].astype(F32)
    at += 1
    tables = (doff_ref[...].astype(F32).astype(BF16),) + split3(dw_ref[...])
    for i, table in enumerate(tables):
        for parity in range(POINTS // NODES):
            start = at + (i * (POINTS // NODES) + parity) * k_dec
            place = interleave(parity, (POINTS, NODES), 0)
            all_ref[start : start + k_dec, :] = dot(table, place, NN)
    width = all_ref.shape[0]
    each = width // noise
    rows = NODES // each
    jitter = jnp.zeros((rows, width), F32)
    target = lax.broadcasted_iota(jnp.int32, (rows, NODES), 0)
    node = lax.broadcasted_iota(jnp.int32, (rows, NODES), 1)
    source = lax.broadcasted_iota(jnp.int32, (noise, width), 0)
    lane = lax.broadcasted_iota(jnp.int32, (noise, width), 1)
    for b in range(each):
        pick = jnp.where(node == target * each + b, 1.0, 0.0).astype(BF16)
        shift = jnp.where(lane == source + b * noise, 1.0, 0.0).astype(BF16)
        jitter = jitter + dot(dot(pick, jit_ref[...], NT).astype(BF16), shift, NN)
    out_ref[:rows, :] = jitter.astype(BF16)
    share = out_ref.shape[0] - rows
    row = lax.broadcasted_iota(jnp.int32, (share, NODES), 0) + member_ref[0] * share
    pick = jnp.where(row == lax.broadcasted_iota(jnp.int32, (share, NODES), 1), 1.0, 0.0)
    out_ref[rows:, :] = dot(pick.astype(BF16), all_ref[...].astype(BF16), NT).astype(BF16)


def forward_kernel(k_enc, k_dec, need, push, *refs):
    got_ref, jitter_ref, wn_ref, we_ref, wq_ref, wo_ref, u_ref = refs[:7]
    (forecast_ref, pooled_ref, state0_ref, normed_ref, raw_ref, qn_ref, kn_ref, v_ref) = refs[7:15]
    prob_ref, att_ref, state1_ref, dnorm_ref, facts_ref, near_ref = refs[15:21]
    x_ref, msg_ref, all0_ref, proj_ref = refs[21:]
    attn = wo_ref.shape[0]
    reach = POINTS + 2 * RIM_G
    inv_root = HEAD_DIM ** (-0.5)
    members = got_ref.shape[0]
    sub, share = POINTS // members, NODES // members

    for m in range(members):
        for i in range(3):
            start = RIM_G + i * POINTS + m * sub
            x_ref[start : start + sub, :] = got_ref[m, i * sub : (i + 1) * sub, :]
        start = m * sub - RIM_G if m >= members // 2 else RIM_G + 3 * POINTS + m * sub
        x_ref[start : start + sub, :] = got_ref[m, 3 * sub : 4 * sub, :]
    near_ref[...] = x_ref[POINTS : POINTS + reach, :]
    each = 2 * k_dec
    at = 4 * k_enc + 1
    for m in range(members):
        for i in range(3):
            start = 4 * sub + i * share
            facts_ref[i * NODES + m * share : i * NODES + (m + 1) * share, :] = got_ref[
                m, start : start + share, :
            ].astype(F32)
    facts = facts_ref[...]
    weight = sum(facts[:, k_enc * i : k_enc * (i + 1)] for i in (3, 2, 1))
    scale = sum(facts[:, at + each * i : at + each * (i + 1)] for i in (3, 2, 1))
    facts_ref[:, k_enc : 2 * k_enc] = weight
    facts_ref[:, 2 * k_enc : 2 * k_enc + 1] = facts[:, at - 1 : at]
    facts_ref[:, 2 * k_enc + 1 : 2 * k_enc + 1 + each] = facts[:, at : at + each]
    facts_ref[:, 2 * k_enc + 1 + each : 2 * k_enc + 1 + 2 * each] = scale
    push(12, 13)

    def message_rows(i, carry):
        rows = pl.ds(pl.multiple_of(i * 128, 128), 128)
        pre = dot(x_ref[rows, :], we_ref[...], NN)
        msg_ref[rows, :] = (pre * sigmoid(pre)).astype(BF16)
        return carry

    lax.fori_loop(0, x_ref.shape[0] // 128, message_rows, 0)
    heads = same_head(attn)
    for s in range(3):
        rows = slice(s * NODES, (s + 1) * NODES)
        high, low = spread_matrix(facts_ref[rows, :], k_enc, reach)
        near = msg_ref[s * POINTS : s * POINTS + reach, :]
        pooled = dot(high, near, NN) + dot(low, near, NN)
        state0 = pooled * rms_factor(pooled) + dot(jitter_ref[rows, :], wn_ref[...], NN)
        all0_ref[rows, :] = state0
        normed = (state0 * rms_factor(state0)).astype(BF16)
        if s == 0:
            need(4)
        mixed = dot(normed, wq_ref[...], NN)
        queries, keys = mixed[:, :attn], mixed[:, attn : 2 * attn]
        qn_ref[rows, :] = (
            queries * lax.rsqrt(head_mean(queries * queries, heads) + EPS)
        ).astype(BF16)
        kn_ref[rows, :] = (keys * lax.rsqrt(head_mean(keys * keys, heads) + EPS)).astype(BF16)
        v_ref[rows, :] = mixed[:, 2 * attn :].astype(BF16)
        if s == 1:
            pooled_ref[...] = pooled
            state0_ref[...] = state0
            normed_ref[...] = normed
            raw_ref[...] = mixed[:, : 2 * attn]
            push(1, 2, 3, 4)
    push(5, 6, 7)
    need(5, 6)

    masks = head_masks()
    span = 2 * NODES
    relative = (
        lax.broadcasted_iota(jnp.int32, (NODES, span), 1)
        - lax.broadcasted_iota(jnp.int32, (NODES, span), 0)
        - WIN
    )
    for b in range(2):
        asked = slice(WIN + b * NODES, WIN + (b + 1) * NODES)
        known = slice(b * NODES, b * NODES + span)
        rows = slice(b * NODES, (b + 1) * NODES)
        offsets = facts_ref[asked, 2 * k_enc : 2 * k_enc + 1].astype(jnp.int32)
        allowed = (relative >= offsets) & (relative < offsets + WIN)
        for pair in range(attn // 128):
            lanes = slice(pair * 128, (pair + 1) * 128)
            query, key, value = qn_ref[asked, lanes], kn_ref[known, lanes], v_ref[known, lanes]
            out = jnp.zeros((NODES, 128), F32)
            for h in range(2):
                scores = dot(masked(masks[h], query), key, NT) * inv_root
                weights = jnp.where(allowed, jnp.exp(scores), 0.0)
                prob = (weights * (1.0 / jnp.sum(weights, axis=-1, keepdims=True))).astype(BF16)
                prob_ref[(b * attn // 128 + pair) * 2 + h] = prob
                out = out + dot(prob, masked(masks[h], value), NN)
            att_ref[rows, lanes] = out.astype(BF16)
        state1 = all0_ref[asked, :] + dot(att_ref[rows, :], wo_ref[...], NN)
        state1_ref[rows, :] = state1
        dnorm = (state1 * rms_factor(state1)).astype(BF16)
        dnorm_ref[rows, :] = dnorm
        proj_ref[rows, :] = dot(dnorm, u_ref[...], NN)
    push(8, 9, 10, 11)

    proj_high, proj_low = split2(proj_ref[...])
    facts = facts_ref[NODES : 2 * NODES, :]
    span = lax.broadcasted_iota(jnp.int32, (NODES, ASKED), 1)
    home = lax.broadcasted_iota(jnp.int32, (NODES, 1), 0) + RIM_H
    forecast = x_ref[POINTS + RIM_G : 2 * POINTS + RIM_G, :].astype(F32)
    for parity in range(2):
        arcs = jnp.zeros((NODES, ASKED), F32)
        for k in range(k_dec):
            at = 2 * k_enc + 1 + parity * k_dec + k
            source = facts[:, at : at + 1].astype(jnp.int32) + home
            scale = facts[:, at + 2 * k_dec : at + 2 * k_dec + 1]
            arcs = arcs + jnp.where(source == span, scale, 0.0)
        high, low = split2(arcs)
        rest = dot(high, proj_high, NN) + dot(high, proj_low, NN) + dot(low, proj_high, NN)
        place = interleave(parity, (POINTS, NODES), 0)
        high, low = split2(rest)
        forecast = forecast + dot(place, high, NN) + dot(place, low, NN)
    forecast_ref[...] = forecast


def prepare_kernel(k_enc, k_dec, need, push, *refs):
    facts_ref, turned_ref, x_ref, wet_ref, order_ref, normed_ref, dnorm_ref = refs[:7]
    slope_ref, nt_ref, dt_ref, sh_ref, ah_ref, al_ref = refs[7:]
    quarter = order_ref.shape[0] // 4
    need(2)
    for r in range(4):
        rows = slice(r * quarter, (r + 1) * quarter)
        slope_ref[rows, :] = silu_slope(dot(wet_ref[rows, :], x_ref[...], NT))
    push(0)
    need(4, 5, 6, 0)
    for r in range(4):
        rows = slice(r * quarter, (r + 1) * quarter)
        nt_ref[rows, :] = dot(order_ref[rows, :], normed_ref[...], NT).astype(BF16)
        dt_ref[rows, :] = dot(order_ref[rows, :], dnorm_ref[WIN : WIN + NODES, :], NT).astype(BF16)
    push(1, 2)
    facts = facts_ref[NODES : 2 * NODES, :]
    sh_ref[...] = spread_matrix(facts, k_enc, POINTS + 2 * RIM_G)[0]
    push(3)
    span = lax.broadcasted_iota(jnp.int32, (ASKED, NODES), 0)
    node = lax.broadcasted_iota(jnp.int32, (1, NODES), 1)
    for s in range(3):
        lanes = slice(s * NODES, (s + 1) * NODES)
        for parity in range(2):
            arcs = jnp.zeros((ASKED, NODES), F32)
            for k in range(k_dec):
                at = 2 * k_enc + 1 + parity * k_dec + k
                source = turned_ref[at : at + 1, lanes].astype(jnp.int32) + node
                source = source + (s * NODES - NODES + RIM_H)
                scale = turned_ref[at + 2 * k_dec : at + 2 * k_dec + 1, lanes]
                arcs = arcs + jnp.where(source == span, scale, 0.0)
            ah_ref[2 * s + parity], al_ref[2 * s + parity] = split2(arcs)
    push(4, 5)


def backward_kernel(need, push, *refs):
    (pair_ref, beyond_ref, x_ref, jitter_ref, wq_ref, wo_ref, u_ref, order_ref) = refs[:8]
    (pooled_ref, state0_ref, raw_ref, qn_ref, kn_ref, v_ref, prob_ref, att_ref) = refs[8:16]
    (state1_ref, slope_ref, nt_ref, dt_ref, sh_ref, ah_ref, al_ref) = refs[16:23]
    core_ref = refs[23]
    kept_ref, sent_ref, grad1_ref, g1b_ref, ga_ref, gq_ref, gk_ref, gv_ref, mixed_ref, both_ref = refs[24:]
    attn, width = wo_ref.shape
    inv_root = HEAD_DIM ** (-0.5)
    own_asked = slice(WIN, WIN + NODES)
    quarter = width // 4

    def store(r, start, values):
        ref = kept_ref if r < 2 else sent_ref
        at = (r % 2) * quarter
        ref[at : at + quarter, start : start + values.shape[1]] = values.astype(BF16)

    def turned(r, values):
        return dot(order_ref[r * quarter : (r + 1) * quarter, :], values, NT).astype(BF16)

    need(21, 22)
    odd = core_ref[0] == 1
    members, sub = pair_ref.shape[0], pair_ref.shape[2]
    for m in range(members):
        for c in range(2):
            both_ref[c, m * sub : (m + 1) * sub, :] = pair_ref[m, c]
    even, second = both_ref[0].astype(F32), both_ref[1].astype(F32)
    beyond = beyond_ref[...].astype(F32)
    low = jnp.where(odd, even, beyond).astype(BF16)
    middle = jnp.where(odd, second, even).astype(BF16)
    high = jnp.where(odd, beyond, second).astype(BF16)
    grad_proj = jnp.zeros((ASKED, beyond_ref.shape[1]), F32)
    for s, part in enumerate((low, middle, high)):
        for parity in range(2):
            grad = dot(interleave(parity, (NODES, POINTS), 1), part, NN).astype(BF16)
            grad_proj = grad_proj + dot(ah_ref[2 * s + parity], grad, NN)
            grad_proj = grad_proj + dot(al_ref[2 * s + parity], grad, NN)
    proj_high, proj_low = split2(grad_proj)
    need(16, 6, 5)
    for b in range(2):
        rows = slice(b * NODES, (b + 1) * NODES)
        state1 = state1_ref[rows, :]
        grad = dot(proj_high[rows], u_ref[...], NT) + dot(proj_low[rows], u_ref[...], NT)
        grad = rms_back(state1, rms_factor(state1), grad)
        grad1_ref[rows, :] = grad
        g1b_ref[rows, :] = grad.astype(BF16)
        ga_ref[rows, :] = dot(g1b_ref[rows, :], wo_ref[...], NT).astype(BF16)
    need(19, 7, 15)
    for r in range(4):
        dnorm = dt_ref[r * quarter : (r + 1) * quarter, :]
        store(
            r,
            4 * attn + 128,
            dot(dnorm, proj_high[own_asked], NN) + dot(dnorm, proj_low[own_asked], NN),
        )
        store(r, 3 * attn, dot(turned(r, g1b_ref[own_asked, :]), att_ref[own_asked, :], NN))

    need(11, 12, 13, 14)
    masks = head_masks()
    for pair in range(attn // 128):
        lanes = slice(pair * 128, (pair + 1) * 128)
        grad_key = jnp.zeros((NODES, 128), F32)
        grad_value = jnp.zeros((NODES, 128), F32)
        for b in range(2):
            asked = slice(WIN + b * NODES, WIN + (b + 1) * NODES)
            known = slice(b * NODES, b * NODES + 2 * NODES)
            mine = slice(NODES, 2 * NODES) if b == 0 else slice(0, NODES)
            half = slice(WIN, NODES) if b == 0 else slice(0, WIN)
            query, key, value = qn_ref[asked, lanes], kn_ref[known, lanes], v_ref[known, lanes]
            grad_out = ga_ref[b * NODES : (b + 1) * NODES, lanes]
            grad_query = jnp.zeros((WIN, 128), F32)
            for h in range(2):
                grad_head = masked(masks[h], grad_out)
                grad_prob = dot(grad_head, value, NT)
                prob = prob_ref[(b * attn // 128 + pair) * 2 + h]
                wide = prob.astype(F32)
                inner = jnp.sum(wide * grad_prob, axis=-1, keepdims=True)
                grad_scores = (wide * (grad_prob - inner)).astype(BF16)
                grad_query = grad_query + dot(grad_scores[half, :], masked(masks[h], key), NN)
                grad_key = grad_key + dot(grad_scores[:, mine], masked(masks[h], query), TN)
                grad_value = grad_value + dot(prob[:, mine], grad_head, TN)
            gq_ref[b * WIN : (b + 1) * WIN, lanes] = grad_query * inv_root
        gk_ref[:, lanes] = grad_key * inv_root
        gv_ref[:, lanes] = grad_value
    heads = same_head(attn)
    need(10)
    for i, ref in enumerate((gq_ref, gk_ref)):
        values = raw_ref[:, i * attn : (i + 1) * attn]
        grad = ref[...]
        factor = lax.rsqrt(head_mean(values * values, heads) + EPS)
        inner = head_mean(grad * values, heads)
        grad = factor * grad - values * (factor * factor * factor) * inner
        mixed_ref[:, i * attn : (i + 1) * attn] = grad.astype(BF16)
    mixed_ref[:, 2 * attn :] = gv_ref[...].astype(BF16)

    need(4, 9, 8, 18, 17, 20)
    grad_normed = dot(mixed_ref[...], wq_ref[...], NT)
    state0 = state0_ref[...]
    grad0 = grad1_ref[own_asked, :] + rms_back(state0, rms_factor(state0), grad_normed)
    grad0_b = grad0.astype(BF16)
    pooled = pooled_ref[...]
    grad_pooled = rms_back(pooled, rms_factor(pooled), grad0).astype(BF16)
    spread = sh_ref[...]
    for r in range(4):
        rows = slice(r * quarter, (r + 1) * quarter)
        store(r, 0, dot(nt_ref[rows, :], mixed_ref[...], NN))
        store(r, 4 * attn + 256, dot(turned(r, grad0_b), jitter_ref[...], NN))
        grad = dot(turned(r, grad_pooled), spread, NN) * slope_ref[rows, :]
        store(r, 4 * attn, dot(grad.astype(BF16), x_ref[...], NN))


def loss_kernel(scale, need, push, cells_ref, truth_ref, out_ref):
    members = cells_ref.shape[0]
    cells = [cells_ref[m] for m in range(members)]
    fair = [jnp.zeros_like(cells[0]) for _ in range(members)]
    for m in range(members):
        for n in range(m + 1, members):
            slope = eased_sensitivity(cells[m] - cells[n])
            fair[m] = fair[m] + slope
            fair[n] = fair[n] - slope
    for m in range(members):
        first = eased_sensitivity(cells[m] - truth_ref[...]) * (scale / members)
        out = (first - fair[m] * (scale / (members * (members - 1)))).astype(BF16)
        for c in range(out_ref.shape[1]):
            out_ref[m, c] = out


def call(kernel, args, late, outs, pushed, scratch, name):
    n_in, n_out = len(args), len(outs)
    sems = len(late) + len(pushed)
    smem = pl.BlockSpec(memory_space=pltpu.SMEM)

    def body(*refs):
        ins, out_refs = list(refs[:n_in]), list(refs[n_in : n_in + n_out])
        rest = refs[n_in + n_out :]
        sem, rest = rest[0], rest[1:]
        incoming, outgoing = {}, {}
        for j, i in enumerate(late):
            incoming[i] = pltpu.make_async_copy(ins[i], rest[j], sem.at[j])
            incoming[i].start()
            ins[i] = rest[j]
        for j, o in enumerate(pushed):
            buffer = rest[len(late) + j]
            outgoing[o] = pltpu.make_async_copy(buffer, out_refs[o], sem.at[len(late) + j])
            out_refs[o] = buffer

        def need(*which):
            for i in which:
                incoming[i].wait()

        def push(*which):
            for o in which:
                outgoing[o].start()

        kernel(need, push, *ins, *out_refs, *rest[sems:])
        for o in pushed:
            outgoing[o].wait()

    vmem = pl.BlockSpec(memory_space=pltpu.VMEM)
    hbm = pl.BlockSpec(memory_space=pltpu.HBM)
    buffers = [pltpu.VMEM(args[i].shape, args[i].dtype) for i in late]
    buffers += [pltpu.VMEM(*outs[o]) for o in pushed]
    if not INTERPRET:
        args = [
            pltpu.with_memory_space_constraint(arg, pltpu.HBM) if i in late else arg
            for i, arg in enumerate(args)
        ]
    return pl.pallas_call(
        body,
        out_shape=[
            (pltpu.HBM if o in pushed and not INTERPRET else jax.ShapeDtypeStruct)(*out)
            for o, out in enumerate(outs)
        ],
        in_specs=[
            hbm if i in late else (smem if arg.shape == (1,) else vmem)
            for i, arg in enumerate(args)
        ],
        out_specs=[hbm if o in pushed else vmem for o in range(n_out)],
        scratch_shapes=[pltpu.SemaphoreType.DMA((max(sems, 1),))]
        + buffers
        + [pltpu.VMEM(*one) for one in scratch],
        compiler_params=pltpu.CompilerParams(vmem_limit_bytes=48 << 20),
        interpret=INTERPRET,
        name=name,
    )(*args)


def per_device(
    slabs,
    loader,
    hidden_jitter,
    w_noise,
    w_enc,
    enc_offset,
    enc_weight,
    w_qkv,
    window_offset,
    w_out,
    unpacker_linear_map,
    dec_offset,
    unpacker_arc_scales,
):
    members = lax.axis_size(MEMBER)
    shards = lax.axis_size(GRID)
    channels, width = w_enc.shape
    attn = w_out.shape[0]
    heads = attn // HEAD_DIM
    points = slabs.shape[1]
    nodes = enc_offset.shape[0]
    per_node = points // nodes
    sub = points // members
    noise = w_noise.shape[0]
    k_enc = enc_offset.shape[1]
    k_dec = dec_offset.shape[1]
    inv_root = HEAD_DIM ** (-0.5)

    zl, x = (lax.axis_size(a) for a in MEMBER)
    zh, y, core = (lax.axis_size(a) for a in GRID)
    rows = width // (members * shards)
    order = jnp.arange(width, dtype=jnp.int32).reshape(core, x, y, zl, zh, rows)
    c_i, x_i, y_i, zl_i, zh_i, r_i = (
        lax.broadcasted_iota(jnp.int32, order.shape, d) for d in range(6)
    )
    c_i = c_i ^ lax.axis_index("core")
    target = ((((zl_i * x + x_i) * zh + zh_i) * y + y_i) * core + c_i) * rows + r_i
    target = target.reshape(width, 1)
    reorder = (lax.broadcasted_iota(jnp.int32, (width, width), 1) == target).astype(BF16)
    w_enc_turned = dot(reorder, w_enc, NT).astype(BF16)

    pieces = swap(slabs[0].reshape(members, sub, 2 * channels), MEMBER)
    piece = lax.dynamic_index_in_dim(pieces, loader[0], 0, keepdims=False)
    truth = piece[:, channels:].astype(F32)

    share = nodes // members
    member = lax.axis_index(MEMBER)
    jitter_rows = nodes * noise // channels
    (packed,) = call(
        pack_kernel,
        (
            member.astype(jnp.int32).reshape(1),
            enc_offset.T,
            enc_weight.T,
            window_offset.reshape(1, nodes),
            hidden_jitter[0].T,
            dec_offset.T,
            unpacker_arc_scales.T,
        ),
        (1, 2, 3, 4, 5, 6),
        [((jitter_rows + share, channels), BF16)],
        (),
        [((channels, nodes), F32)],
        "pack",
    )
    chunk = jnp.concatenate([piece[:, :channels], packed], axis=0)
    near = lax.ppermute(chunk, "core", [(0, 1), (1, 0)])
    beyond = beyond_pair(chunk)
    odd = lax.axis_index("core") == 1
    low, mid, high = jnp.where(odd, near, beyond), chunk, jnp.where(odd, beyond, near)
    at = sub + jitter_rows
    pairs = []
    for m in range(members):
        step = 2 if m >= members // 2 else -2
        for i in range(shards):
            pairs.append((m * shards + i, m * shards + (i + step) % shards))
    far = lax.ppermute(piece[:, :channels], MEMBER + GRID, pairs)
    payload = jnp.concatenate(
        [low[:sub], mid[:sub], high[:sub], far, low[at:], mid[at:], high[at:]], axis=0
    )
    got = swap(jnp.broadcast_to(payload[None], (members,) + payload.shape), MEMBER)
    got, reorder, w_enc_turned = lax.optimization_barrier((got, reorder, w_enc_turned))
    jitter_all = jnp.concatenate([low[sub:at], mid[sub:at], high[sub:at]], axis=0)
    jitter_all = jnp.pad(jitter_all.reshape(3 * nodes, noise), ((0, 0), (0, channels - noise)))
    w_noise = jnp.pad(w_noise, ((0, channels - noise), (0, 0)))
    residuals = [
        ((nodes, width), F32),
        ((nodes, width), F32),
        ((nodes, width), BF16),
        ((nodes, 2 * attn), F32),
        ((3 * nodes, attn), BF16),
        ((3 * nodes, attn), BF16),
        ((3 * nodes, attn), BF16),
        ((2 * attn // HEAD_DIM, nodes, 2 * nodes), BF16),
        ((ASKED, attn), BF16),
        ((ASKED, width), F32),
        ((ASKED, width), BF16),
        ((3 * nodes, channels), F32),
        ((points + 2 * RIM_G, channels), BF16),
    ]
    forecast, *saved = call(
        functools.partial(forward_kernel, k_enc, k_dec),
        (got, jitter_all, w_noise, w_enc, w_qkv, w_out, unpacker_linear_map),
        (4, 5, 6),
        [((points, channels), F32)] + residuals,
        tuple(range(1, 1 + len(residuals))),
        [
            ((4 * points, channels), BF16),
            ((4 * points, width), BF16),
            ((3 * nodes, width), F32),
            ((ASKED, channels), F32),
        ],
        "forward",
    )

    cells = swap(forecast.reshape(members, sub, channels), MEMBER)
    pooled, state0, normed, raw, query, key, value, prob, attended, state1, dnorm, facts, near = saved
    prepared = call(
        functools.partial(prepare_kernel, k_enc, k_dec),
        (facts, facts.T, near, w_enc_turned, reorder, normed, dnorm),
        (2, 4, 5, 6, 0),
        [
            ((width, points + 2 * RIM_G), F32),
            ((width, nodes), BF16),
            ((width, nodes), BF16),
            ((nodes, points + 2 * RIM_G), BF16),
            ((3 * per_node, ASKED, nodes), BF16),
            ((3 * per_node, ASKED, nodes), BF16),
        ],
        tuple(range(6)),
        [],
        "prepare",
    )
    cells, *prepared = lax.optimization_barrier((cells, *prepared))
    loss_scale = float(members * points * shards * channels) ** (-0.5)
    (sensitivity,) = call(
        functools.partial(loss_kernel, loss_scale),
        (cells, truth),
        (),
        [((members, core, sub, channels), BF16)],
        (),
        [],
        "loss",
    )
    pair = swap(sensitivity.reshape(members * core, sub, channels), MEMBER + ("core",))
    pair = pair.reshape(members, core, sub, channels)
    grad_own = lax.dynamic_index_in_dim(pair, lax.axis_index("core"), 1, keepdims=False)
    grad_beyond = beyond_pair(grad_own.reshape(points, channels))

    lanes = 4 * attn + 3 * channels
    kept, sent = call(
        backward_kernel,
        (
            pair,
            grad_beyond,
            near,
            jitter_all[nodes : 2 * nodes],
            w_qkv,
            w_out,
            unpacker_linear_map,
            reorder,
            pooled,
            state0,
            raw,
            query,
            key,
            value,
            prob,
            attended,
            state1,
            *prepared,
            lax.axis_index("core").astype(jnp.int32).reshape(1),
        ),
        (21, 22, 16, 6, 5, 19, 7, 15, 11, 12, 13, 14, 10, 4, 9, 8, 18, 17, 20),
        [((width // core, lanes), BF16)] * 2,
        (),
        [
            ((ASKED, width), F32),
            ((ASKED, width), BF16),
            ((ASKED, attn), BF16),
            ((nodes, attn), F32),
            ((nodes, attn), F32),
            ((nodes, attn), F32),
            ((nodes, 3 * attn), BF16),
            ((core, points, channels), BF16),
        ],
        "backward",
    )

    total = kept.astype(F32) + lax.ppermute(sent, "core", [(0, 1), (1, 0)]).astype(F32)
    total = swap(total.astype(BF16).reshape(x * y, -1, lanes), ("x", "y"))
    total = jnp.sum(total.astype(F32), axis=0)
    total = swap(total.astype(BF16).reshape(zl * zh, rows, lanes), ("zl", "zh"))
    total = jnp.sum(total.astype(F32), axis=0)
    grad_qkv, grad_out, grad_enc, grad_map, grad_noise = (
        total[:, start:stop]
        for start, stop in (
            (0, 3 * attn),
            (3 * attn, 4 * attn),
            (4 * attn, 4 * attn + channels),
            (4 * attn + channels, 4 * attn + 2 * channels),
            (4 * attn + 2 * channels, 4 * attn + 2 * channels + noise),
        )
    )
    return (grad_noise.T, grad_enc.T, grad_qkv, grad_out.T, grad_map)


def solution(mesh):
    member, grid = mesh.shape["member"], mesh.shape["grid"]
    inner = 4 if member == 16 else 2
    fine = Mesh(
        mesh.devices.reshape(member // inner, inner, 2, grid // 4, 2), MEMBER + GRID
    )
    in_specs = (
        P(MEMBER, GRID, None),
        P(),
        P(MEMBER, GRID, None),
        P(),
        P(),
        P(GRID, None),
        P(GRID, None),
        P(),
        P(GRID),
        P(),
        P(),
        P(GRID, None),
        P(GRID, None),
    )
    both = MEMBER + GRID
    out_specs = (P(None, both), P(None, both), P(both, None), P(None, both), P(both, None))
    return jax.shard_map(
        per_device, mesh=fine, in_specs=in_specs, out_specs=out_specs, check_vma=False
    )
```

```python
import functools

import jax
import jax.numpy as jnp
from jax import lax
from jax.experimental import pallas as pl
from jax.experimental.pallas import tpu as pltpu
from jax.sharding import Mesh
from jax.sharding import PartitionSpec as P

HEAD_DIM = 64
RIM_G = 128
RIM_H = 64
WIN = 64

EPS = 1e-06
DELTA_SQ = 0.01

MEMBER = ("zl", "x")
GRID = ("zh", "y", "core")
F32 = jnp.float32
BF16 = jnp.bfloat16
INTERPRET = False
NODES = 128
POINTS = 256
ASKED = NODES + 2 * WIN


def rms_factor(values):
    return lax.rsqrt(jnp.mean(values * values, axis=-1, keepdims=True) + EPS)


def rms_back(values, factor, gradient):
    inner = jnp.mean(gradient * values, axis=-1, keepdims=True)
    return factor * gradient - values * (factor * factor * factor) * inner


def sigmoid(values):
    return 0.5 + 0.5 * jnp.tanh(0.5 * values)


def silu_slope(pre):
    sigma = sigmoid(pre)
    return sigma * (1.0 + pre * (1.0 - sigma))


def eased_sensitivity(diff):
    return diff * lax.rsqrt(diff * diff + DELTA_SQ)


def dot(left, right, dims, **options):
    return lax.dot_general(left, right, (dims, ((), ())), preferred_element_type=F32, **options)


NN = ((1,), (0,))
TN = ((0,), (0,))
NT = ((1,), (1,))


def swap(values, axes):
    return lax.all_to_all(values, axes, split_axis=0, concat_axis=0, tiled=True)


def exchanged(values):
    count = lax.axis_size(GRID)
    near = lax.ppermute(values, GRID, [(i, i ^ 1) for i in range(count)])
    beyond = lax.ppermute(
        values, GRID, [(i, (i + 1 if i % 2 else i - 1) % count) for i in range(count)]
    )
    return near, beyond


def split2(values):
    high = values.astype(BF16)
    return high, (values - high.astype(F32)).astype(BF16)


def same_head(attn):
    row = lax.broadcasted_iota(jnp.int32, (attn, attn), 0) // HEAD_DIM
    column = lax.broadcasted_iota(jnp.int32, (attn, attn), 1) // HEAD_DIM
    return jnp.where(row == column, 1.0, 0.0).astype(BF16)


def head_mean(values, heads):
    return dot(values.astype(BF16), heads, NN) * (1.0 / HEAD_DIM)


def head_masks():
    lane = lax.broadcasted_iota(jnp.int32, (1, 2 * HEAD_DIM), 1)
    return (lane < HEAD_DIM, lane >= HEAD_DIM)


def masked(mask, values):
    return jnp.where(mask, values, jnp.zeros_like(values))


def spread_matrix(facts, k_enc, reach):
    span = lax.broadcasted_iota(jnp.int32, (NODES, reach), 1)
    home = lax.broadcasted_iota(jnp.int32, (NODES, 1), 0) * (POINTS // NODES) + RIM_G
    spread = jnp.zeros((NODES, reach), F32)
    for k in range(k_enc):
        source = facts[:, k : k + 1].astype(jnp.int32) + home
        spread = spread + jnp.where(source == span, facts[:, k_enc + k : k_enc + k + 1], 0.0)
    return split2(spread)


def interleave(parity, shape, point_dim):
    point = lax.broadcasted_iota(jnp.int32, shape, point_dim)
    node = lax.broadcasted_iota(jnp.int32, shape, 1 - point_dim)
    return jnp.where(point == 2 * node + parity, 1.0, 0.0).astype(BF16)


def split3(values):
    high = values.astype(BF16)
    rest = values - high.astype(F32)
    middle = rest.astype(BF16)
    return high, middle, (rest - middle.astype(F32)).astype(BF16)


def pack_kernel(need, push, member_ref, off_ref, w_ref, win_ref, jit_ref, doff_ref, dw_ref, *refs):
    out_ref, all_ref = refs
    k_enc, k_dec = w_ref.shape[0], dw_ref.shape[0]
    noise = jit_ref.shape[0]
    all_ref[...] = jnp.zeros_like(all_ref)
    need(1, 2, 3, 4, 5, 6)
    all_ref[:k_enc, :] = off_ref[...].astype(F32)
    for i, term in enumerate(split3(w_ref[...])):
        all_ref[k_enc * (i + 1) : k_enc * (i + 2), :] = term.astype(F32)
    at = 4 * k_enc
    all_ref[at : at + 1, :] = win_ref[...].astype(F32)
    at += 1
    tables = (doff_ref[...].astype(F32).astype(BF16),) + split3(dw_ref[...])
    for i, table in enumerate(tables):
        for parity in range(POINTS // NODES):
            start = at + (i * (POINTS // NODES) + parity) * k_dec
            place = interleave(parity, (POINTS, NODES), 0)
            all_ref[start : start + k_dec, :] = dot(table, place, NN)
    width = all_ref.shape[0]
    each = width // noise
    rows = NODES // each
    jitter = jnp.zeros((rows, width), F32)
    target = lax.broadcasted_iota(jnp.int32, (rows, NODES), 0)
    node = lax.broadcasted_iota(jnp.int32, (rows, NODES), 1)
    source = lax.broadcasted_iota(jnp.int32, (noise, width), 0)
    lane = lax.broadcasted_iota(jnp.int32, (noise, width), 1)
    for b in range(each):
        pick = jnp.where(node == target * each + b, 1.0, 0.0).astype(BF16)
        shift = jnp.where(lane == source + b * noise, 1.0, 0.0).astype(BF16)
        jitter = jitter + dot(dot(pick, jit_ref[...], NT).astype(BF16), shift, NN)
    out_ref[:rows, :] = jitter.astype(BF16)
    share = out_ref.shape[0] - rows
    row = lax.broadcasted_iota(jnp.int32, (share, NODES), 0) + member_ref[0] * share
    pick = jnp.where(row == lax.broadcasted_iota(jnp.int32, (share, NODES), 1), 1.0, 0.0)
    out_ref[rows:, :] = dot(pick.astype(BF16), all_ref[...].astype(BF16), NT).astype(BF16)


def forward_kernel(k_enc, k_dec, need, push, *refs):
    got_ref, jitter_ref, wn_ref, we_ref, wq_ref, wo_ref, u_ref = refs[:7]
    (forecast_ref, pooled_ref, state0_ref, normed_ref, raw_ref, qn_ref, kn_ref, v_ref) = refs[7:15]
    prob_ref, att_ref, state1_ref, dnorm_ref, facts_ref, near_ref = refs[15:21]
    x_ref, msg_ref, all0_ref, proj_ref = refs[21:]
    attn = wo_ref.shape[0]
    reach = POINTS + 2 * RIM_G
    inv_root = HEAD_DIM ** (-0.5)
    members = got_ref.shape[0]
    sub, share = POINTS // members, NODES // members

    for m in range(members):
        for i in range(3):
            start = RIM_G + i * POINTS + m * sub
            x_ref[start : start + sub, :] = got_ref[m, i * sub : (i + 1) * sub, :]
        start = m * sub - RIM_G if m >= members // 2 else RIM_G + 3 * POINTS + m * sub
        x_ref[start : start + sub, :] = got_ref[m, 3 * sub : 4 * sub, :]
    near_ref[...] = x_ref[POINTS : POINTS + reach, :]
    each = 2 * k_dec
    at = 4 * k_enc + 1
    for m in range(members):
        for i in range(3):
            start = 4 * sub + i * share
            facts_ref[i * NODES + m * share : i * NODES + (m + 1) * share, :] = got_ref[
                m, start : start + share, :
            ].astype(F32)
    facts = facts_ref[...]
    weight = sum(facts[:, k_enc * i : k_enc * (i + 1)] for i in (3, 2, 1))
    scale = sum(facts[:, at + each * i : at + each * (i + 1)] for i in (3, 2, 1))
    facts_ref[:, k_enc : 2 * k_enc] = weight
    facts_ref[:, 2 * k_enc : 2 * k_enc + 1] = facts[:, at - 1 : at]
    facts_ref[:, 2 * k_enc + 1 : 2 * k_enc + 1 + each] = facts[:, at : at + each]
    facts_ref[:, 2 * k_enc + 1 + each : 2 * k_enc + 1 + 2 * each] = scale
    push(12, 13)

    def message_rows(i, carry):
        rows = pl.ds(pl.multiple_of(i * 128, 128), 128)
        pre = dot(x_ref[rows, :], we_ref[...], NN)
        msg_ref[rows, :] = (pre * sigmoid(pre)).astype(BF16)
        return carry

    lax.fori_loop(0, x_ref.shape[0] // 128, message_rows, 0)
    heads = same_head(attn)
    for s in range(3):
        rows = slice(s * NODES, (s + 1) * NODES)
        high, low = spread_matrix(facts_ref[rows, :], k_enc, reach)
        near = msg_ref[s * POINTS : s * POINTS + reach, :]
        pooled = dot(high, near, NN) + dot(low, near, NN)
        state0 = pooled * rms_factor(pooled) + dot(jitter_ref[rows, :], wn_ref[...], NN)
        all0_ref[rows, :] = state0
        normed = (state0 * rms_factor(state0)).astype(BF16)
        if s == 0:
            need(4)
        mixed = dot(normed, wq_ref[...], NN)
        queries, keys = mixed[:, :attn], mixed[:, attn : 2 * attn]
        qn_ref[rows, :] = (
            queries * lax.rsqrt(head_mean(queries * queries, heads) + EPS)
        ).astype(BF16)
        kn_ref[rows, :] = (keys * lax.rsqrt(head_mean(keys * keys, heads) + EPS)).astype(BF16)
        v_ref[rows, :] = mixed[:, 2 * attn :].astype(BF16)
        if s == 1:
            pooled_ref[...] = pooled
            state0_ref[...] = state0
            normed_ref[...] = normed
            raw_ref[...] = mixed[:, : 2 * attn]
            push(1, 2, 3, 4)
    push(5, 6, 7)
    need(5, 6)

    masks = head_masks()
    span = 2 * NODES
    relative = (
        lax.broadcasted_iota(jnp.int32, (NODES, span), 1)
        - lax.broadcasted_iota(jnp.int32, (NODES, span), 0)
        - WIN
    )
    for b in range(2):
        asked = slice(WIN + b * NODES, WIN + (b + 1) * NODES)
        known = slice(b * NODES, b * NODES + span)
        rows = slice(b * NODES, (b + 1) * NODES)
        offsets = facts_ref[asked, 2 * k_enc : 2 * k_enc + 1].astype(jnp.int32)
        allowed = (relative >= offsets) & (relative < offsets + WIN)
        for pair in range(attn // 128):
            lanes = slice(pair * 128, (pair + 1) * 128)
            query, key, value = qn_ref[asked, lanes], kn_ref[known, lanes], v_ref[known, lanes]
            out = jnp.zeros((NODES, 128), F32)
            for h in range(2):
                scores = dot(masked(masks[h], query), key, NT) * inv_root
                weights = jnp.where(allowed, jnp.exp(scores), 0.0)
                prob = (weights * (1.0 / jnp.sum(weights, axis=-1, keepdims=True))).astype(BF16)
                prob_ref[(b * attn // 128 + pair) * 2 + h] = prob
                out = out + dot(prob, masked(masks[h], value), NN)
            att_ref[rows, lanes] = out.astype(BF16)
        state1 = all0_ref[asked, :] + dot(att_ref[rows, :], wo_ref[...], NN)
        state1_ref[rows, :] = state1
        dnorm = (state1 * rms_factor(state1)).astype(BF16)
        dnorm_ref[rows, :] = dnorm
        proj_ref[rows, :] = dot(dnorm, u_ref[...], NN)
    push(8, 9, 10, 11)

    proj_high, proj_low = split2(proj_ref[...])
    facts = facts_ref[NODES : 2 * NODES, :]
    span = lax.broadcasted_iota(jnp.int32, (NODES, ASKED), 1)
    home = lax.broadcasted_iota(jnp.int32, (NODES, 1), 0) + RIM_H
    forecast = x_ref[POINTS + RIM_G : 2 * POINTS + RIM_G, :].astype(F32)
    for parity in range(2):
        arcs = jnp.zeros((NODES, ASKED), F32)
        for k in range(k_dec):
            at = 2 * k_enc + 1 + parity * k_dec + k
            source = facts[:, at : at + 1].astype(jnp.int32) + home
            scale = facts[:, at + 2 * k_dec : at + 2 * k_dec + 1]
            arcs = arcs + jnp.where(source == span, scale, 0.0)
        high, low = split2(arcs)
        rest = dot(high, proj_high, NN) + dot(high, proj_low, NN) + dot(low, proj_high, NN)
        place = interleave(parity, (POINTS, NODES), 0)
        high, low = split2(rest)
        forecast = forecast + dot(place, high, NN) + dot(place, low, NN)
    forecast_ref[...] = forecast


def prepare_kernel(k_enc, k_dec, need, push, *refs):
    facts_ref, turned_ref, x_ref, wet_ref, order_ref, normed_ref, dnorm_ref = refs[:7]
    slope_ref, nt_ref, dt_ref, sh_ref, ah_ref, al_ref = refs[7:]
    quarter = order_ref.shape[0] // 4
    need(2)
    for r in range(4):
        rows = slice(r * quarter, (r + 1) * quarter)
        slope_ref[rows, :] = silu_slope(dot(wet_ref[rows, :], x_ref[...], NT))
    push(0)
    need(4, 5, 6, 0)
    for r in range(4):
        rows = slice(r * quarter, (r + 1) * quarter)
        nt_ref[rows, :] = dot(order_ref[rows, :], normed_ref[...], NT).astype(BF16)
        dt_ref[rows, :] = dot(order_ref[rows, :], dnorm_ref[WIN : WIN + NODES, :], NT).astype(BF16)
    push(1, 2)
    facts = facts_ref[NODES : 2 * NODES, :]
    sh_ref[...] = spread_matrix(facts, k_enc, POINTS + 2 * RIM_G)[0]
    push(3)
    span = lax.broadcasted_iota(jnp.int32, (ASKED, NODES), 0)
    node = lax.broadcasted_iota(jnp.int32, (1, NODES), 1)
    for s in range(3):
        lanes = slice(s * NODES, (s + 1) * NODES)
        for parity in range(2):
            arcs = jnp.zeros((ASKED, NODES), F32)
            for k in range(k_dec):
                at = 2 * k_enc + 1 + parity * k_dec + k
                source = turned_ref[at : at + 1, lanes].astype(jnp.int32) + node
                source = source + (s * NODES - NODES + RIM_H)
                scale = turned_ref[at + 2 * k_dec : at + 2 * k_dec + 1, lanes]
                arcs = arcs + jnp.where(source == span, scale, 0.0)
            ah_ref[2 * s + parity], al_ref[2 * s + parity] = split2(arcs)
    push(4, 5)


def backward_kernel(need, push, *refs):
    (near_ref, mid_ref, beyond_ref, x_ref, jitter_ref, wq_ref, wo_ref, u_ref, order_ref) = refs[:9]
    (pooled_ref, state0_ref, raw_ref, qn_ref, kn_ref, v_ref, prob_ref, att_ref) = refs[9:17]
    (state1_ref, slope_ref, nt_ref, dt_ref, sh_ref, ah_ref, al_ref) = refs[17:24]
    core_ref = refs[24]
    kept_ref, sent_ref, grad1_ref, g1b_ref, ga_ref, gq_ref, gk_ref, gv_ref, mixed_ref = refs[25:]
    attn, width = wo_ref.shape
    inv_root = HEAD_DIM ** (-0.5)
    own_asked = slice(WIN, WIN + NODES)
    quarter = width // 4

    def store(r, start, values):
        ref = kept_ref if r < 2 else sent_ref
        at = (r % 2) * quarter
        ref[at : at + quarter, start : start + values.shape[1]] = values.astype(BF16)

    def turned(r, values):
        return dot(order_ref[r * quarter : (r + 1) * quarter, :], values, NT).astype(BF16)

    need(22, 23)
    odd = core_ref[0] == 1
    near, beyond = near_ref[...].astype(F32), beyond_ref[...].astype(F32)
    low = jnp.where(odd, near, beyond).astype(BF16)
    high = jnp.where(odd, beyond, near).astype(BF16)
    grad_proj = jnp.zeros((ASKED, mid_ref.shape[1]), F32)
    for s, part in enumerate((low, mid_ref[...], high)):
        for parity in range(2):
            grad = dot(interleave(parity, (NODES, POINTS), 1), part, NN).astype(BF16)
            grad_proj = grad_proj + dot(ah_ref[2 * s + parity], grad, NN)
            grad_proj = grad_proj + dot(al_ref[2 * s + parity], grad, NN)
    proj_high, proj_low = split2(grad_proj)
    need(17, 7, 6)
    for b in range(2):
        rows = slice(b * NODES, (b + 1) * NODES)
        state1 = state1_ref[rows, :]
        grad = dot(proj_high[rows], u_ref[...], NT) + dot(proj_low[rows], u_ref[...], NT)
        grad = rms_back(state1, rms_factor(state1), grad)
        grad1_ref[rows, :] = grad
        g1b_ref[rows, :] = grad.astype(BF16)
        ga_ref[rows, :] = dot(g1b_ref[rows, :], wo_ref[...], NT).astype(BF16)
    need(20, 8, 16)
    for r in range(4):
        dnorm = dt_ref[r * quarter : (r + 1) * quarter, :]
        store(
            r,
            4 * attn + 128,
            dot(dnorm, proj_high[own_asked], NN) + dot(dnorm, proj_low[own_asked], NN),
        )
        store(r, 3 * attn, dot(turned(r, g1b_ref[own_asked, :]), att_ref[own_asked, :], NN))

    need(12, 13, 14, 15)
    masks = head_masks()
    for pair in range(attn // 128):
        lanes = slice(pair * 128, (pair + 1) * 128)
        grad_key = jnp.zeros((NODES, 128), F32)
        grad_value = jnp.zeros((NODES, 128), F32)
        for b in range(2):
            asked = slice(WIN + b * NODES, WIN + (b + 1) * NODES)
            known = slice(b * NODES, b * NODES + 2 * NODES)
            mine = slice(NODES, 2 * NODES) if b == 0 else slice(0, NODES)
            half = slice(WIN, NODES) if b == 0 else slice(0, WIN)
            query, key, value = qn_ref[asked, lanes], kn_ref[known, lanes], v_ref[known, lanes]
            grad_out = ga_ref[b * NODES : (b + 1) * NODES, lanes]
            grad_query = jnp.zeros((WIN, 128), F32)
            for h in range(2):
                grad_head = masked(masks[h], grad_out)
                grad_prob = dot(grad_head, value, NT)
                prob = prob_ref[(b * attn // 128 + pair) * 2 + h]
                wide = prob.astype(F32)
                inner = jnp.sum(wide * grad_prob, axis=-1, keepdims=True)
                grad_scores = (wide * (grad_prob - inner)).astype(BF16)
                grad_query = grad_query + dot(grad_scores[half, :], masked(masks[h], key), NN)
                grad_key = grad_key + dot(grad_scores[:, mine], masked(masks[h], query), TN)
                grad_value = grad_value + dot(prob[:, mine], grad_head, TN)
            gq_ref[b * WIN : (b + 1) * WIN, lanes] = grad_query * inv_root
        gk_ref[:, lanes] = grad_key * inv_root
        gv_ref[:, lanes] = grad_value
    heads = same_head(attn)
    need(11)
    for i, ref in enumerate((gq_ref, gk_ref)):
        values = raw_ref[:, i * attn : (i + 1) * attn]
        grad = ref[...]
        factor = lax.rsqrt(head_mean(values * values, heads) + EPS)
        inner = head_mean(grad * values, heads)
        grad = factor * grad - values * (factor * factor * factor) * inner
        mixed_ref[:, i * attn : (i + 1) * attn] = grad.astype(BF16)
    mixed_ref[:, 2 * attn :] = gv_ref[...].astype(BF16)

    need(5, 10, 9, 19, 18, 21)
    grad_normed = dot(mixed_ref[...], wq_ref[...], NT)
    state0 = state0_ref[...]
    grad0 = grad1_ref[own_asked, :] + rms_back(state0, rms_factor(state0), grad_normed)
    grad0_b = grad0.astype(BF16)
    pooled = pooled_ref[...]
    grad_pooled = rms_back(pooled, rms_factor(pooled), grad0).astype(BF16)
    spread = sh_ref[...]
    for r in range(4):
        rows = slice(r * quarter, (r + 1) * quarter)
        store(r, 0, dot(nt_ref[rows, :], mixed_ref[...], NN))
        store(r, 4 * attn + 256, dot(turned(r, grad0_b), jitter_ref[...], NN))
        grad = dot(turned(r, grad_pooled), spread, NN) * slope_ref[rows, :]
        store(r, 4 * attn, dot(grad.astype(BF16), x_ref[...], NN))


def last_kernel(need, push, total_ref, *out_refs):
    start = 0
    for ref in out_refs:
        stop = start + ref.shape[1]
        ref[...] = sum(
            total_ref[i, :, start:stop].astype(F32) for i in range(total_ref.shape[0])
        )
        start = stop


def loss_kernel(scale, need, push, cells_ref, truth_ref, out_ref):
    members = cells_ref.shape[0]
    cells = [cells_ref[m] for m in range(members)]
    fair = [jnp.zeros_like(cells[0]) for _ in range(members)]
    for m in range(members):
        for n in range(m + 1, members):
            slope = eased_sensitivity(cells[m] - cells[n])
            fair[m] = fair[m] + slope
            fair[n] = fair[n] - slope
    for m in range(members):
        first = eased_sensitivity(cells[m] - truth_ref[...]) * (scale / members)
        out_ref[m] = (first - fair[m] * (scale / (members * (members - 1)))).astype(BF16)


def call(kernel, args, late, outs, pushed, scratch, name):
    n_in, n_out = len(args), len(outs)
    sems = len(late) + len(pushed)
    smem = pl.BlockSpec(memory_space=pltpu.SMEM)

    def body(*refs):
        ins, out_refs = list(refs[:n_in]), list(refs[n_in : n_in + n_out])
        rest = refs[n_in + n_out :]
        sem, rest = rest[0], rest[1:]
        incoming, outgoing = {}, {}
        for j, i in enumerate(late):
            incoming[i] = pltpu.make_async_copy(ins[i], rest[j], sem.at[j])
            incoming[i].start()
            ins[i] = rest[j]
        for j, o in enumerate(pushed):
            buffer = rest[len(late) + j]
            outgoing[o] = pltpu.make_async_copy(buffer, out_refs[o], sem.at[len(late) + j])
            out_refs[o] = buffer

        def need(*which):
            for i in which:
                incoming[i].wait()

        def push(*which):
            for o in which:
                outgoing[o].start()

        kernel(need, push, *ins, *out_refs, *rest[sems:])
        for o in pushed:
            outgoing[o].wait()

    vmem = pl.BlockSpec(memory_space=pltpu.VMEM)
    hbm = pl.BlockSpec(memory_space=pltpu.HBM)
    buffers = [pltpu.VMEM(args[i].shape, args[i].dtype) for i in late]
    buffers += [pltpu.VMEM(*outs[o]) for o in pushed]
    if not INTERPRET:
        args = [
            pltpu.with_memory_space_constraint(arg, pltpu.HBM) if i in late else arg
            for i, arg in enumerate(args)
        ]
    return pl.pallas_call(
        body,
        out_shape=[
            (pltpu.HBM if o in pushed and not INTERPRET else jax.ShapeDtypeStruct)(*out)
            for o, out in enumerate(outs)
        ],
        in_specs=[
            hbm if i in late else (smem if arg.shape == (1,) else vmem)
            for i, arg in enumerate(args)
        ],
        out_specs=[hbm if o in pushed else vmem for o in range(n_out)],
        scratch_shapes=[pltpu.SemaphoreType.DMA((max(sems, 1),))]
        + buffers
        + [pltpu.VMEM(*one) for one in scratch],
        compiler_params=pltpu.CompilerParams(vmem_limit_bytes=48 << 20),
        interpret=INTERPRET,
        name=name,
    )(*args)


def per_device(
    slabs,
    loader,
    hidden_jitter,
    w_noise,
    w_enc,
    enc_offset,
    enc_weight,
    w_qkv,
    window_offset,
    w_out,
    unpacker_linear_map,
    dec_offset,
    unpacker_arc_scales,
):
    members = lax.axis_size(MEMBER)
    shards = lax.axis_size(GRID)
    channels, width = w_enc.shape
    attn = w_out.shape[0]
    heads = attn // HEAD_DIM
    points = slabs.shape[1]
    nodes = enc_offset.shape[0]
    per_node = points // nodes
    sub = points // members
    noise = w_noise.shape[0]
    k_enc = enc_offset.shape[1]
    k_dec = dec_offset.shape[1]
    inv_root = HEAD_DIM ** (-0.5)

    zl, x = (lax.axis_size(a) for a in MEMBER)
    zh, y, core = (lax.axis_size(a) for a in GRID)
    rows = width // (members * shards)
    order = jnp.arange(width, dtype=jnp.int32).reshape(core, x, y, zl, zh, rows)
    c_i, x_i, y_i, zl_i, zh_i, r_i = (
        lax.broadcasted_iota(jnp.int32, order.shape, d) for d in range(6)
    )
    c_i = c_i ^ lax.axis_index("core")
    target = ((((zl_i * x + x_i) * zh + zh_i) * y + y_i) * core + c_i) * rows + r_i
    target = target.reshape(width, 1)
    reorder = (lax.broadcasted_iota(jnp.int32, (width, width), 1) == target).astype(BF16)
    w_enc_turned = dot(reorder, w_enc, NT).astype(BF16)

    pieces = swap(slabs[0].reshape(members, sub, 2 * channels), MEMBER)
    piece = lax.dynamic_index_in_dim(pieces, loader[0], 0, keepdims=False)
    truth = piece[:, channels:].astype(F32)

    share = nodes // members
    member = lax.axis_index(MEMBER)
    jitter_rows = nodes * noise // channels
    (packed,) = call(
        pack_kernel,
        (
            member.astype(jnp.int32).reshape(1),
            enc_offset.T,
            enc_weight.T,
            window_offset.reshape(1, nodes),
            hidden_jitter[0].T,
            dec_offset.T,
            unpacker_arc_scales.T,
        ),
        (1, 2, 3, 4, 5, 6),
        [((jitter_rows + share, channels), BF16)],
        (),
        [((channels, nodes), F32)],
        "pack",
    )
    chunk = jnp.concatenate([piece[:, :channels], packed], axis=0)
    near, beyond = exchanged(chunk)
    odd = lax.axis_index("core") == 1
    low, mid, high = jnp.where(odd, near, beyond), chunk, jnp.where(odd, beyond, near)
    at = sub + jitter_rows
    pairs = []
    for m in range(members):
        step = 2 if m >= members // 2 else -2
        for i in range(shards):
            pairs.append((m * shards + i, m * shards + (i + step) % shards))
    far = lax.ppermute(piece[:, :channels], MEMBER + GRID, pairs)
    payload = jnp.concatenate(
        [low[:sub], mid[:sub], high[:sub], far, low[at:], mid[at:], high[at:]], axis=0
    )
    got = swap(jnp.broadcast_to(payload[None], (members,) + payload.shape), MEMBER)
    got, reorder, w_enc_turned = lax.optimization_barrier((got, reorder, w_enc_turned))
    jitter_all = jnp.concatenate([low[sub:at], mid[sub:at], high[sub:at]], axis=0)
    jitter_all = jnp.pad(jitter_all.reshape(3 * nodes, noise), ((0, 0), (0, channels - noise)))
    w_noise = jnp.pad(w_noise, ((0, channels - noise), (0, 0)))
    residuals = [
        ((nodes, width), F32),
        ((nodes, width), F32),
        ((nodes, width), BF16),
        ((nodes, 2 * attn), F32),
        ((3 * nodes, attn), BF16),
        ((3 * nodes, attn), BF16),
        ((3 * nodes, attn), BF16),
        ((2 * attn // HEAD_DIM, nodes, 2 * nodes), BF16),
        ((ASKED, attn), BF16),
        ((ASKED, width), F32),
        ((ASKED, width), BF16),
        ((3 * nodes, channels), F32),
        ((points + 2 * RIM_G, channels), BF16),
    ]
    forecast, *saved = call(
        functools.partial(forward_kernel, k_enc, k_dec),
        (got, jitter_all, w_noise, w_enc, w_qkv, w_out, unpacker_linear_map),
        (4, 5, 6),
        [((points, channels), F32)] + residuals,
        tuple(range(1, 1 + len(residuals))),
        [
            ((4 * points, channels), BF16),
            ((4 * points, width), BF16),
            ((3 * nodes, width), F32),
            ((ASKED, channels), F32),
        ],
        "forward",
    )

    cells = swap(forecast.reshape(members, sub, channels), MEMBER)
    pooled, state0, normed, raw, query, key, value, prob, attended, state1, dnorm, facts, near = saved
    prepared = call(
        functools.partial(prepare_kernel, k_enc, k_dec),
        (facts, facts.T, near, w_enc_turned, reorder, normed, dnorm),
        (2, 4, 5, 6, 0),
        [
            ((width, points + 2 * RIM_G), F32),
            ((width, nodes), BF16),
            ((width, nodes), BF16),
            ((nodes, points + 2 * RIM_G), BF16),
            ((3 * per_node, ASKED, nodes), BF16),
            ((3 * per_node, ASKED, nodes), BF16),
        ],
        tuple(range(6)),
        [],
        "prepare",
    )
    cells, *prepared = lax.optimization_barrier((cells, *prepared))
    loss_scale = float(members * points * shards * channels) ** (-0.5)
    (sensitivity,) = call(
        functools.partial(loss_kernel, loss_scale),
        (cells, truth),
        (),
        [((members, sub, channels), BF16)],
        (),
        [],
        "loss",
    )
    grad_forecast = swap(sensitivity, MEMBER).reshape(points, channels)
    grad_near, grad_beyond = exchanged(grad_forecast)

    lanes = 4 * attn + 3 * channels
    kept, sent = call(
        backward_kernel,
        (
            grad_near,
            grad_forecast,
            grad_beyond,
            near,
            jitter_all[nodes : 2 * nodes],
            w_qkv,
            w_out,
            unpacker_linear_map,
            reorder,
            pooled,
            state0,
            raw,
            query,
            key,
            value,
            prob,
            attended,
            state1,
            *prepared,
            lax.axis_index("core").astype(jnp.int32).reshape(1),
        ),
        (22, 23, 17, 7, 6, 20, 8, 16, 12, 13, 14, 15, 11, 5, 10, 9, 19, 18, 21),
        [((width // core, lanes), BF16)] * 2,
        (),
        [
            ((ASKED, width), F32),
            ((ASKED, width), BF16),
            ((ASKED, attn), BF16),
            ((nodes, attn), F32),
            ((nodes, attn), F32),
            ((nodes, attn), F32),
            ((nodes, 3 * attn), BF16),
        ],
        "backward",
    )

    total = kept.astype(F32) + lax.ppermute(sent, "core", [(0, 1), (1, 0)]).astype(F32)
    total = swap(total.astype(BF16).reshape(x * y, -1, lanes), ("x", "y"))
    total = jnp.sum(total.astype(F32), axis=0)
    total = swap(total.astype(BF16).reshape(zl * zh, rows, lanes), ("zl", "zh"))
    cuts = (3 * attn, attn, channels, channels, noise)
    grad_qkv, grad_out, grad_enc, grad_map, grad_noise = call(
        last_kernel,
        (total,),
        (),
        [((rows, cut), F32) for cut in cuts],
        (),
        [],
        "last",
    )
    return (grad_noise.T, grad_enc.T, grad_qkv, grad_out.T, grad_map)


def solution(mesh):
    member, grid = mesh.shape["member"], mesh.shape["grid"]
    inner = 4 if member == 16 else 2
    fine = Mesh(
        mesh.devices.reshape(member // inner, inner, 2, grid // 4, 2), MEMBER + GRID
    )
    in_specs = (
        P(MEMBER, GRID, None),
        P(),
        P(MEMBER, GRID, None),
        P(),
        P(),
        P(GRID, None),
        P(GRID, None),
        P(),
        P(GRID),
        P(),
        P(),
        P(GRID, None),
        P(GRID, None),
    )
    both = MEMBER + GRID
    out_specs = (P(None, both), P(None, both), P(both, None), P(None, both), P(both, None))
    return jax.shard_map(
        per_device, mesh=fine, in_specs=in_specs, out_specs=out_specs, check_vma=False
    )
```

```python
import functools

import jax
import jax.numpy as jnp
from jax import lax
from jax.experimental import pallas as pl
from jax.experimental.pallas import tpu as pltpu
from jax.sharding import Mesh
from jax.sharding import PartitionSpec as P

HEAD_DIM = 64
RIM_G = 128
RIM_H = 64
WIN = 64

EPS = 1e-06
DELTA_SQ = 0.01

MEMBER = ("zl", "x")
GRID = ("zh", "y", "core")
F32 = jnp.float32
BF16 = jnp.bfloat16
INTERPRET = False
NODES = 128
POINTS = 256
ASKED = NODES + 2 * WIN


def rms_factor(values):
    return lax.rsqrt(jnp.mean(values * values, axis=-1, keepdims=True) + EPS)


def rms_back(values, factor, gradient):
    inner = jnp.mean(gradient * values, axis=-1, keepdims=True)
    return factor * gradient - values * (factor * factor * factor) * inner


def sigmoid(values):
    return 0.5 + 0.5 * jnp.tanh(0.5 * values)


def silu_slope(pre):
    sigma = sigmoid(pre)
    return sigma * (1.0 + pre * (1.0 - sigma))


def eased_sensitivity(diff):
    return diff * lax.rsqrt(diff * diff + DELTA_SQ)


def dot(left, right, dims, **options):
    return lax.dot_general(left, right, (dims, ((), ())), preferred_element_type=F32, **options)


NN = ((1,), (0,))
TN = ((0,), (0,))
NT = ((1,), (1,))


def swap(values, axes):
    return lax.all_to_all(values, axes, split_axis=0, concat_axis=0, tiled=True)


def exchanged(values):
    count = lax.axis_size(GRID)
    near = lax.ppermute(values, GRID, [(i, i ^ 1) for i in range(count)])
    beyond = lax.ppermute(
        values, GRID, [(i, (i + 1 if i % 2 else i - 1) % count) for i in range(count)]
    )
    return near, beyond


def split2(values):
    high = values.astype(BF16)
    return high, (values - high.astype(F32)).astype(BF16)


def same_head(attn):
    row = lax.broadcasted_iota(jnp.int32, (attn, attn), 0) // HEAD_DIM
    column = lax.broadcasted_iota(jnp.int32, (attn, attn), 1) // HEAD_DIM
    return jnp.where(row == column, 1.0, 0.0).astype(BF16)


def head_mean(values, heads):
    return dot(values.astype(BF16), heads, NN) * (1.0 / HEAD_DIM)


def head_masks():
    lane = lax.broadcasted_iota(jnp.int32, (1, 2 * HEAD_DIM), 1)
    return (lane < HEAD_DIM, lane >= HEAD_DIM)


def masked(mask, values):
    return jnp.where(mask, values, jnp.zeros_like(values))


def spread_matrix(facts, k_enc, reach):
    span = lax.broadcasted_iota(jnp.int32, (NODES, reach), 1)
    home = lax.broadcasted_iota(jnp.int32, (NODES, 1), 0) * (POINTS // NODES) + RIM_G
    spread = jnp.zeros((NODES, reach), F32)
    for k in range(k_enc):
        source = facts[:, k : k + 1].astype(jnp.int32) + home
        spread = spread + jnp.where(source == span, facts[:, k_enc + k : k_enc + k + 1], 0.0)
    return split2(spread)


def interleave(parity, shape, point_dim):
    point = lax.broadcasted_iota(jnp.int32, shape, point_dim)
    node = lax.broadcasted_iota(jnp.int32, shape, 1 - point_dim)
    return jnp.where(point == 2 * node + parity, 1.0, 0.0).astype(BF16)


def split3(values):
    high = values.astype(BF16)
    rest = values - high.astype(F32)
    middle = rest.astype(BF16)
    return high, middle, (rest - middle.astype(F32)).astype(BF16)


def pack_kernel(need, push, member_ref, off_ref, w_ref, win_ref, jit_ref, doff_ref, dw_ref, *refs):
    out_ref, all_ref = refs
    k_enc, k_dec = w_ref.shape[0], dw_ref.shape[0]
    noise = jit_ref.shape[0]
    all_ref[...] = jnp.zeros_like(all_ref)
    need(1, 2, 3, 4, 5, 6)
    all_ref[:k_enc, :] = off_ref[...].astype(F32)
    for i, term in enumerate(split3(w_ref[...])):
        all_ref[k_enc * (i + 1) : k_enc * (i + 2), :] = term.astype(F32)
    at = 4 * k_enc
    all_ref[at : at + 1, :] = win_ref[...].astype(F32)
    at += 1
    tables = (doff_ref[...].astype(F32).astype(BF16),) + split3(dw_ref[...])
    for i, table in enumerate(tables):
        for parity in range(POINTS // NODES):
            start = at + (i * (POINTS // NODES) + parity) * k_dec
            place = interleave(parity, (POINTS, NODES), 0)
            all_ref[start : start + k_dec, :] = dot(table, place, NN)
    width = all_ref.shape[0]
    each = width // noise
    rows = NODES // each
    jitter = jnp.zeros((rows, width), F32)
    target = lax.broadcasted_iota(jnp.int32, (rows, NODES), 0)
    node = lax.broadcasted_iota(jnp.int32, (rows, NODES), 1)
    source = lax.broadcasted_iota(jnp.int32, (noise, width), 0)
    lane = lax.broadcasted_iota(jnp.int32, (noise, width), 1)
    for b in range(each):
        pick = jnp.where(node == target * each + b, 1.0, 0.0).astype(BF16)
        shift = jnp.where(lane == source + b * noise, 1.0, 0.0).astype(BF16)
        jitter = jitter + dot(dot(pick, jit_ref[...], NT).astype(BF16), shift, NN)
    out_ref[:rows, :] = jitter.astype(BF16)
    share = out_ref.shape[0] - rows
    row = lax.broadcasted_iota(jnp.int32, (share, NODES), 0) + member_ref[0] * share
    pick = jnp.where(row == lax.broadcasted_iota(jnp.int32, (share, NODES), 1), 1.0, 0.0)
    out_ref[rows:, :] = dot(pick.astype(BF16), all_ref[...].astype(BF16), NT).astype(BF16)


def forward_kernel(k_enc, k_dec, need, push, *refs):
    got_ref, jitter_ref, wn_ref, we_ref, wq_ref, wo_ref, u_ref = refs[:7]
    (forecast_ref, pooled_ref, state0_ref, normed_ref, raw_ref, qn_ref, kn_ref, v_ref) = refs[7:15]
    prob_ref, att_ref, state1_ref, dnorm_ref, facts_ref, near_ref, turned_ref = refs[15:22]
    x_ref, msg_ref, all0_ref, proj_ref = refs[22:]
    attn = wo_ref.shape[0]
    reach = POINTS + 2 * RIM_G
    inv_root = HEAD_DIM ** (-0.5)
    members = got_ref.shape[0]
    sub, share = POINTS // members, NODES // members

    for m in range(members):
        for i in range(3):
            start = RIM_G + i * POINTS + m * sub
            x_ref[start : start + sub, :] = got_ref[m, i * sub : (i + 1) * sub, :]
        start = m * sub - RIM_G if m >= members // 2 else RIM_G + 3 * POINTS + m * sub
        x_ref[start : start + sub, :] = got_ref[m, 3 * sub : 4 * sub, :]
    near_ref[...] = x_ref[POINTS : POINTS + reach, :]
    each = 2 * k_dec
    at = 4 * k_enc + 1
    for m in range(members):
        for i in range(3):
            start = 4 * sub + i * share
            facts_ref[i * NODES + m * share : i * NODES + (m + 1) * share, :] = got_ref[
                m, start : start + share, :
            ].astype(F32)
    facts = facts_ref[...]
    weight = sum(facts[:, k_enc * i : k_enc * (i + 1)] for i in (3, 2, 1))
    scale = sum(facts[:, at + each * i : at + each * (i + 1)] for i in (3, 2, 1))
    facts_ref[:, k_enc : 2 * k_enc] = weight
    facts_ref[:, 2 * k_enc : 2 * k_enc + 1] = facts[:, at - 1 : at]
    facts_ref[:, 2 * k_enc + 1 : 2 * k_enc + 1 + each] = facts[:, at : at + each]
    facts_ref[:, 2 * k_enc + 1 + each : 2 * k_enc + 1 + 2 * each] = scale
    turned_ref[...] = facts_ref[...].T
    push(12, 13, 14)

    def message_rows(i, carry):
        rows = pl.ds(pl.multiple_of(i * 128, 128), 128)
        pre = dot(x_ref[rows, :], we_ref[...], NN)
        msg_ref[rows, :] = (pre * sigmoid(pre)).astype(BF16)
        return carry

    lax.fori_loop(0, x_ref.shape[0] // 128, message_rows, 0)
    heads = same_head(attn)
    for s in range(3):
        rows = slice(s * NODES, (s + 1) * NODES)
        high, low = spread_matrix(facts_ref[rows, :], k_enc, reach)
        near = msg_ref[s * POINTS : s * POINTS + reach, :]
        pooled = dot(high, near, NN) + dot(low, near, NN)
        state0 = pooled * rms_factor(pooled) + dot(jitter_ref[rows, :], wn_ref[...], NN)
        all0_ref[rows, :] = state0
        normed = (state0 * rms_factor(state0)).astype(BF16)
        if s == 0:
            need(4)
        mixed = dot(normed, wq_ref[...], NN)
        queries, keys = mixed[:, :attn], mixed[:, attn : 2 * attn]
        qn_ref[rows, :] = (
            queries * lax.rsqrt(head_mean(queries * queries, heads) + EPS)
        ).astype(BF16)
        kn_ref[rows, :] = (keys * lax.rsqrt(head_mean(keys * keys, heads) + EPS)).astype(BF16)
        v_ref[rows, :] = mixed[:, 2 * attn :].astype(BF16)
        if s == 1:
            pooled_ref[...] = pooled
            state0_ref[...] = state0
            normed_ref[...] = normed
            raw_ref[...] = mixed[:, : 2 * attn]
            push(1, 2, 3, 4)
    push(5, 6, 7)
    need(5, 6)

    masks = head_masks()
    span = 2 * NODES
    relative = (
        lax.broadcasted_iota(jnp.int32, (NODES, span), 1)
        - lax.broadcasted_iota(jnp.int32, (NODES, span), 0)
        - WIN
    )
    for b in range(2):
        asked = slice(WIN + b * NODES, WIN + (b + 1) * NODES)
        known = slice(b * NODES, b * NODES + span)
        rows = slice(b * NODES, (b + 1) * NODES)
        offsets = facts_ref[asked, 2 * k_enc : 2 * k_enc + 1].astype(jnp.int32)
        allowed = (relative >= offsets) & (relative < offsets + WIN)
        for pair in range(attn // 128):
            lanes = slice(pair * 128, (pair + 1) * 128)
            query, key, value = qn_ref[asked, lanes], kn_ref[known, lanes], v_ref[known, lanes]
            out = jnp.zeros((NODES, 128), F32)
            for h in range(2):
                scores = dot(masked(masks[h], query), key, NT) * inv_root
                weights = jnp.where(allowed, jnp.exp(scores), 0.0)
                prob = (weights * (1.0 / jnp.sum(weights, axis=-1, keepdims=True))).astype(BF16)
                prob_ref[(b * attn // 128 + pair) * 2 + h] = prob
                out = out + dot(prob, masked(masks[h], value), NN)
            att_ref[rows, lanes] = out.astype(BF16)
        state1 = all0_ref[asked, :] + dot(att_ref[rows, :], wo_ref[...], NN)
        state1_ref[rows, :] = state1
        dnorm = (state1 * rms_factor(state1)).astype(BF16)
        dnorm_ref[rows, :] = dnorm
        proj_ref[rows, :] = dot(dnorm, u_ref[...], NN)
    push(8, 9, 10, 11)

    proj_high, proj_low = split2(proj_ref[...])
    facts = facts_ref[NODES : 2 * NODES, :]
    span = lax.broadcasted_iota(jnp.int32, (NODES, ASKED), 1)
    home = lax.broadcasted_iota(jnp.int32, (NODES, 1), 0) + RIM_H
    forecast = x_ref[POINTS + RIM_G : 2 * POINTS + RIM_G, :].astype(F32)
    for parity in range(2):
        arcs = jnp.zeros((NODES, ASKED), F32)
        for k in range(k_dec):
            at = 2 * k_enc + 1 + parity * k_dec + k
            source = facts[:, at : at + 1].astype(jnp.int32) + home
            scale = facts[:, at + 2 * k_dec : at + 2 * k_dec + 1]
            arcs = arcs + jnp.where(source == span, scale, 0.0)
        high, low = split2(arcs)
        rest = dot(high, proj_high, NN) + dot(high, proj_low, NN) + dot(low, proj_high, NN)
        place = interleave(parity, (POINTS, NODES), 0)
        high, low = split2(rest)
        forecast = forecast + dot(place, high, NN) + dot(place, low, NN)
    forecast_ref[...] = forecast.astype(BF16)


def prepare_kernel(k_enc, k_dec, need, push, *refs):
    facts_ref, turned_ref, x_ref, wet_ref, order_ref, normed_ref, dnorm_ref = refs[:7]
    slope_ref, nt_ref, dt_ref, sh_ref, ah_ref, al_ref = refs[7:]
    quarter = order_ref.shape[0] // 4
    need(2)
    for r in range(4):
        rows = slice(r * quarter, (r + 1) * quarter)
        slope_ref[rows, :] = silu_slope(dot(wet_ref[rows, :], x_ref[...], NT))
    push(0)
    need(4, 5, 6, 0, 1)
    for r in range(4):
        rows = slice(r * quarter, (r + 1) * quarter)
        nt_ref[rows, :] = dot(order_ref[rows, :], normed_ref[...], NT).astype(BF16)
        dt_ref[rows, :] = dot(order_ref[rows, :], dnorm_ref[WIN : WIN + NODES, :], NT).astype(BF16)
    push(1, 2)
    facts = facts_ref[NODES : 2 * NODES, :]
    sh_ref[...] = spread_matrix(facts, k_enc, POINTS + 2 * RIM_G)[0]
    push(3)
    span = lax.broadcasted_iota(jnp.int32, (ASKED, NODES), 0)
    node = lax.broadcasted_iota(jnp.int32, (1, NODES), 1)
    for s in range(3):
        lanes = slice(s * NODES, (s + 1) * NODES)
        for parity in range(2):
            arcs = jnp.zeros((ASKED, NODES), F32)
            for k in range(k_dec):
                at = 2 * k_enc + 1 + parity * k_dec + k
                source = turned_ref[at : at + 1, lanes].astype(jnp.int32) + node
                source = source + (s * NODES - NODES + RIM_H)
                scale = turned_ref[at + 2 * k_dec : at + 2 * k_dec + 1, lanes]
                arcs = arcs + jnp.where(source == span, scale, 0.0)
            ah_ref[2 * s + parity], al_ref[2 * s + parity] = split2(arcs)
    push(4, 5)


def backward_kernel(need, push, *refs):
    (near_ref, mid_ref, beyond_ref, x_ref, jitter_ref, wq_ref, wo_ref, u_ref, order_ref) = refs[:9]
    (pooled_ref, state0_ref, raw_ref, qn_ref, kn_ref, v_ref, prob_ref, att_ref) = refs[9:17]
    (state1_ref, slope_ref, nt_ref, dt_ref, sh_ref, ah_ref, al_ref) = refs[17:24]
    core_ref = refs[24]
    kept_ref, sent_ref, grad1_ref, g1b_ref, ga_ref, gq_ref, gk_ref, gv_ref, mixed_ref = refs[25:]
    attn, width = wo_ref.shape
    inv_root = HEAD_DIM ** (-0.5)
    own_asked = slice(WIN, WIN + NODES)
    quarter = width // 4

    def store(r, start, values):
        ref = kept_ref if r < 2 else sent_ref
        at = (r % 2) * quarter
        ref[at : at + quarter, start : start + values.shape[1]] = values.astype(BF16)

    def turned(r, values):
        return dot(order_ref[r * quarter : (r + 1) * quarter, :], values, NT).astype(BF16)

    need(22, 23)
    odd = core_ref[0] == 1
    near, beyond = near_ref[...].astype(F32), beyond_ref[...].astype(F32)
    low = jnp.where(odd, near, beyond).astype(BF16)
    high = jnp.where(odd, beyond, near).astype(BF16)
    grad_proj = jnp.zeros((ASKED, mid_ref.shape[1]), F32)
    for s, part in enumerate((low, mid_ref[...], high)):
        for parity in range(2):
            grad = dot(interleave(parity, (NODES, POINTS), 1), part, NN).astype(BF16)
            grad_proj = grad_proj + dot(ah_ref[2 * s + parity], grad, NN)
            grad_proj = grad_proj + dot(al_ref[2 * s + parity], grad, NN)
    proj_high, proj_low = split2(grad_proj)
    need(17, 7, 6)
    for b in range(2):
        rows = slice(b * NODES, (b + 1) * NODES)
        state1 = state1_ref[rows, :]
        grad = dot(proj_high[rows], u_ref[...], NT) + dot(proj_low[rows], u_ref[...], NT)
        grad = rms_back(state1, rms_factor(state1), grad)
        grad1_ref[rows, :] = grad
        g1b_ref[rows, :] = grad.astype(BF16)
        ga_ref[rows, :] = dot(g1b_ref[rows, :], wo_ref[...], NT).astype(BF16)
    need(20, 8, 16)
    for r in range(4):
        dnorm = dt_ref[r * quarter : (r + 1) * quarter, :]
        store(
            r,
            4 * attn + 128,
            dot(dnorm, proj_high[own_asked], NN) + dot(dnorm, proj_low[own_asked], NN),
        )
        store(r, 3 * attn, dot(turned(r, g1b_ref[own_asked, :]), att_ref[own_asked, :], NN))

    need(12, 13, 14, 15)
    masks = head_masks()
    for pair in range(attn // 128):
        lanes = slice(pair * 128, (pair + 1) * 128)
        grad_key = jnp.zeros((NODES, 128), F32)
        grad_value = jnp.zeros((NODES, 128), F32)
        for b in range(2):
            asked = slice(WIN + b * NODES, WIN + (b + 1) * NODES)
            known = slice(b * NODES, b * NODES + 2 * NODES)
            mine = slice(NODES, 2 * NODES) if b == 0 else slice(0, NODES)
            half = slice(WIN, NODES) if b == 0 else slice(0, WIN)
            query, key, value = qn_ref[asked, lanes], kn_ref[known, lanes], v_ref[known, lanes]
            grad_out = ga_ref[b * NODES : (b + 1) * NODES, lanes]
            grad_query = jnp.zeros((WIN, 128), F32)
            for h in range(2):
                grad_head = masked(masks[h], grad_out)
                grad_prob = dot(grad_head, value, NT)
                prob = prob_ref[(b * attn // 128 + pair) * 2 + h]
                wide = prob.astype(F32)
                inner = jnp.sum(wide * grad_prob, axis=-1, keepdims=True)
                grad_scores = (wide * (grad_prob - inner)).astype(BF16)
                grad_query = grad_query + dot(grad_scores[half, :], masked(masks[h], key), NN)
                grad_key = grad_key + dot(grad_scores[:, mine], masked(masks[h], query), TN)
                grad_value = grad_value + dot(prob[:, mine], grad_head, TN)
            gq_ref[b * WIN : (b + 1) * WIN, lanes] = grad_query * inv_root
        gk_ref[:, lanes] = grad_key * inv_root
        gv_ref[:, lanes] = grad_value
    heads = same_head(attn)
    need(11)
    for i, ref in enumerate((gq_ref, gk_ref)):
        values = raw_ref[:, i * attn : (i + 1) * attn]
        grad = ref[...]
        factor = lax.rsqrt(head_mean(values * values, heads) + EPS)
        inner = head_mean(grad * values, heads)
        grad = factor * grad - values * (factor * factor * factor) * inner
        mixed_ref[:, i * attn : (i + 1) * attn] = grad.astype(BF16)
    mixed_ref[:, 2 * attn :] = gv_ref[...].astype(BF16)

    need(5, 10, 9, 19, 18, 21)
    grad_normed = dot(mixed_ref[...], wq_ref[...], NT)
    state0 = state0_ref[...]
    grad0 = grad1_ref[own_asked, :] + rms_back(state0, rms_factor(state0), grad_normed)
    grad0_b = grad0.astype(BF16)
    pooled = pooled_ref[...]
    grad_pooled = rms_back(pooled, rms_factor(pooled), grad0).astype(BF16)
    spread = sh_ref[...]
    for r in range(4):
        rows = slice(r * quarter, (r + 1) * quarter)
        store(r, 0, dot(nt_ref[rows, :], mixed_ref[...], NN))
        store(r, 4 * attn + 256, dot(turned(r, grad0_b), jitter_ref[...], NN))
        grad = dot(turned(r, grad_pooled), spread, NN) * slope_ref[rows, :]
        store(r, 4 * attn, dot(grad.astype(BF16), x_ref[...], NN))


def last_kernel(need, push, total_ref, *out_refs):
    start = 0
    for ref in out_refs:
        stop = start + ref.shape[1]
        ref[...] = sum(
            total_ref[i, :, start:stop].astype(F32) for i in range(total_ref.shape[0])
        )
        start = stop


def loss_kernel(scale, need, push, cells_ref, truth_ref, out_ref):
    members = cells_ref.shape[0]
    cells = [cells_ref[m].astype(F32) for m in range(members)]
    fair = [jnp.zeros_like(cells[0]) for _ in range(members)]
    for m in range(members):
        for n in range(m + 1, members):
            slope = eased_sensitivity(cells[m] - cells[n])
            fair[m] = fair[m] + slope
            fair[n] = fair[n] - slope
    for m in range(members):
        first = eased_sensitivity(cells[m] - truth_ref[...]) * (scale / members)
        out_ref[m] = (first - fair[m] * (scale / (members * (members - 1)))).astype(BF16)


def call(kernel, args, late, outs, pushed, scratch, name):
    n_in, n_out = len(args), len(outs)
    sems = len(late) + len(pushed)
    smem = pl.BlockSpec(memory_space=pltpu.SMEM)

    def body(*refs):
        ins, out_refs = list(refs[:n_in]), list(refs[n_in : n_in + n_out])
        rest = refs[n_in + n_out :]
        sem, rest = rest[0], rest[1:]
        incoming, outgoing = {}, {}
        for j, i in enumerate(late):
            incoming[i] = pltpu.make_async_copy(ins[i], rest[j], sem.at[j])
            incoming[i].start()
            ins[i] = rest[j]
        for j, o in enumerate(pushed):
            buffer = rest[len(late) + j]
            outgoing[o] = pltpu.make_async_copy(buffer, out_refs[o], sem.at[len(late) + j])
            out_refs[o] = buffer

        def need(*which):
            for i in which:
                incoming[i].wait()

        def push(*which):
            for o in which:
                outgoing[o].start()

        kernel(need, push, *ins, *out_refs, *rest[sems:])
        for o in pushed:
            outgoing[o].wait()

    vmem = pl.BlockSpec(memory_space=pltpu.VMEM)
    hbm = pl.BlockSpec(memory_space=pltpu.HBM)
    buffers = [pltpu.VMEM(args[i].shape, args[i].dtype) for i in late]
    buffers += [pltpu.VMEM(*outs[o]) for o in pushed]
    if not INTERPRET:
        args = [
            pltpu.with_memory_space_constraint(arg, pltpu.HBM) if i in late else arg
            for i, arg in enumerate(args)
        ]
    return pl.pallas_call(
        body,
        out_shape=[
            (pltpu.HBM if o in pushed and not INTERPRET else jax.ShapeDtypeStruct)(*out)
            for o, out in enumerate(outs)
        ],
        in_specs=[
            hbm if i in late else (smem if arg.shape == (1,) else vmem)
            for i, arg in enumerate(args)
        ],
        out_specs=[hbm if o in pushed else vmem for o in range(n_out)],
        scratch_shapes=[pltpu.SemaphoreType.DMA((max(sems, 1),))]
        + buffers
        + [pltpu.VMEM(*one) for one in scratch],
        compiler_params=pltpu.CompilerParams(vmem_limit_bytes=48 << 20),
        interpret=INTERPRET,
        name=name,
    )(*args)


def per_device(
    slabs,
    loader,
    hidden_jitter,
    w_noise,
    w_enc,
    enc_offset,
    enc_weight,
    w_qkv,
    window_offset,
    w_out,
    unpacker_linear_map,
    dec_offset,
    unpacker_arc_scales,
):
    members = lax.axis_size(MEMBER)
    shards = lax.axis_size(GRID)
    channels, width = w_enc.shape
    attn = w_out.shape[0]
    heads = attn // HEAD_DIM
    points = slabs.shape[1]
    nodes = enc_offset.shape[0]
    per_node = points // nodes
    sub = points // members
    noise = w_noise.shape[0]
    k_enc = enc_offset.shape[1]
    k_dec = dec_offset.shape[1]
    inv_root = HEAD_DIM ** (-0.5)

    zl, x = (lax.axis_size(a) for a in MEMBER)
    zh, y, core = (lax.axis_size(a) for a in GRID)
    rows = width // (members * shards)
    order = jnp.arange(width, dtype=jnp.int32).reshape(core, x, y, zl, zh, rows)
    c_i, x_i, y_i, zl_i, zh_i, r_i = (
        lax.broadcasted_iota(jnp.int32, order.shape, d) for d in range(6)
    )
    c_i = c_i ^ lax.axis_index("core")
    target = ((((zl_i * x + x_i) * zh + zh_i) * y + y_i) * core + c_i) * rows + r_i
    target = target.reshape(width, 1)
    reorder = (lax.broadcasted_iota(jnp.int32, (width, width), 1) == target).astype(BF16)
    w_enc_turned = dot(reorder, w_enc, NT).astype(BF16)

    pieces = swap(slabs[0].reshape(members, sub, 2 * channels), MEMBER)
    piece = lax.dynamic_index_in_dim(pieces, loader[0], 0, keepdims=False)
    truth = piece[:, channels:].astype(F32)

    share = nodes // members
    member = lax.axis_index(MEMBER)
    jitter_rows = nodes * noise // channels
    (packed,) = call(
        pack_kernel,
        (
            member.astype(jnp.int32).reshape(1),
            enc_offset.T,
            enc_weight.T,
            window_offset.reshape(1, nodes),
            hidden_jitter[0].T,
            dec_offset.T,
            unpacker_arc_scales.T,
        ),
        (1, 2, 3, 4, 5, 6),
        [((jitter_rows + share, channels), BF16)],
        (),
        [((channels, nodes), F32)],
        "pack",
    )
    chunk = jnp.concatenate([piece[:, :channels], packed], axis=0)
    near, beyond = exchanged(chunk)
    odd = lax.axis_index("core") == 1
    low, mid, high = jnp.where(odd, near, beyond), chunk, jnp.where(odd, beyond, near)
    at = sub + jitter_rows
    pairs = []
    for m in range(members):
        step = 2 if m >= members // 2 else -2
        for i in range(shards):
            pairs.append((m * shards + i, m * shards + (i + step) % shards))
    far = lax.ppermute(piece[:, :channels], MEMBER + GRID, pairs)
    payload = jnp.concatenate(
        [low[:sub], mid[:sub], high[:sub], far, low[at:], mid[at:], high[at:]], axis=0
    )
    got = swap(jnp.broadcast_to(payload[None], (members,) + payload.shape), MEMBER)
    got, reorder, w_enc_turned = lax.optimization_barrier((got, reorder, w_enc_turned))
    jitter_all = jnp.concatenate([low[sub:at], mid[sub:at], high[sub:at]], axis=0)
    jitter_all = jnp.pad(jitter_all.reshape(3 * nodes, noise), ((0, 0), (0, channels - noise)))
    w_noise = jnp.pad(w_noise, ((0, channels - noise), (0, 0)))
    residuals = [
        ((nodes, width), F32),
        ((nodes, width), F32),
        ((nodes, width), BF16),
        ((nodes, 2 * attn), F32),
        ((3 * nodes, attn), BF16),
        ((3 * nodes, attn), BF16),
        ((3 * nodes, attn), BF16),
        ((2 * attn // HEAD_DIM, nodes, 2 * nodes), BF16),
        ((ASKED, attn), BF16),
        ((ASKED, width), F32),
        ((ASKED, width), BF16),
        ((3 * nodes, channels), F32),
        ((points + 2 * RIM_G, channels), BF16),
        ((channels, 3 * nodes), F32),
    ]
    forecast, *saved = call(
        functools.partial(forward_kernel, k_enc, k_dec),
        (got, jitter_all, w_noise, w_enc, w_qkv, w_out, unpacker_linear_map),
        (4, 5, 6),
        [((points, channels), BF16)] + residuals,
        tuple(range(1, 1 + len(residuals))),
        [
            ((4 * points, channels), BF16),
            ((4 * points, width), BF16),
            ((3 * nodes, width), F32),
            ((ASKED, channels), F32),
        ],
        "forward",
    )

    cells = swap(forecast.reshape(members, sub, channels), MEMBER)
    pooled, state0, normed, raw, query, key, value, prob, attended, state1, dnorm, facts, near, turn = saved
    prepared = call(
        functools.partial(prepare_kernel, k_enc, k_dec),
        (facts, turn, near, w_enc_turned, reorder, normed, dnorm),
        (2, 4, 5, 6, 0, 1),
        [
            ((width, points + 2 * RIM_G), F32),
            ((width, nodes), BF16),
            ((width, nodes), BF16),
            ((nodes, points + 2 * RIM_G), BF16),
            ((3 * per_node, ASKED, nodes), BF16),
            ((3 * per_node, ASKED, nodes), BF16),
        ],
        tuple(range(6)),
        [],
        "prepare",
    )
    cells, *prepared = lax.optimization_barrier((cells, *prepared))
    loss_scale = float(members * points * shards * channels) ** (-0.5)
    (sensitivity,) = call(
        functools.partial(loss_kernel, loss_scale),
        (cells, truth),
        (),
        [((members, sub, channels), BF16)],
        (),
        [],
        "loss",
    )
    grad_forecast = swap(sensitivity, MEMBER).reshape(points, channels)
    grad_near, grad_beyond = exchanged(grad_forecast)

    lanes = 4 * attn + 3 * channels
    kept, sent = call(
        backward_kernel,
        (
            grad_near,
            grad_forecast,
            grad_beyond,
            near,
            jitter_all[nodes : 2 * nodes],
            w_qkv,
            w_out,
            unpacker_linear_map,
            reorder,
            pooled,
            state0,
            raw,
            query,
            key,
            value,
            prob,
            attended,
            state1,
            *prepared,
            lax.axis_index("core").astype(jnp.int32).reshape(1),
        ),
        (22, 23, 17, 7, 6, 20, 8, 16, 12, 13, 14, 15, 11, 5, 10, 9, 19, 18, 21),
        [((width // core, lanes), BF16)] * 2,
        (),
        [
            ((ASKED, width), F32),
            ((ASKED, width), BF16),
            ((ASKED, attn), BF16),
            ((nodes, attn), F32),
            ((nodes, attn), F32),
            ((nodes, attn), F32),
            ((nodes, 3 * attn), BF16),
        ],
        "backward",
    )

    total = kept.astype(F32) + lax.ppermute(sent, "core", [(0, 1), (1, 0)]).astype(F32)
    total = swap(total.astype(BF16).reshape(x * y, -1, lanes), ("x", "y"))
    total = jnp.sum(total.astype(F32), axis=0)
    total = swap(total.astype(BF16).reshape(zl * zh, rows, lanes), ("zl", "zh"))
    cuts = (3 * attn, attn, channels, channels, noise)
    grad_qkv, grad_out, grad_enc, grad_map, grad_noise = call(
        last_kernel,
        (total,),
        (),
        [((rows, cut), F32) for cut in cuts],
        (),
        [],
        "last",
    )
    return (grad_noise.T, grad_enc.T, grad_qkv, grad_out.T, grad_map)


def solution(mesh):
    member, grid = mesh.shape["member"], mesh.shape["grid"]
    inner = 4 if member == 16 else 2
    fine = Mesh(
        mesh.devices.reshape(member // inner, inner, 2, grid // 4, 2), MEMBER + GRID
    )
    in_specs = (
        P(MEMBER, GRID, None),
        P(),
        P(MEMBER, GRID, None),
        P(),
        P(),
        P(GRID, None),
        P(GRID, None),
        P(),
        P(GRID),
        P(),
        P(),
        P(GRID, None),
        P(GRID, None),
    )
    both = MEMBER + GRID
    out_specs = (P(None, both), P(None, both), P(both, None), P(None, both), P(both, None))
    return jax.shard_map(
        per_device, mesh=fine, in_specs=in_specs, out_specs=out_specs, check_vma=False
    )
```
